128 devices in a mesh: seq: 16 (over x_hi, z, core), head: 8 (over y, x_lo).
Axes of the slice: x: 4 (x_hi: 2, x_lo: 2; x = x_hi * 2 + x_lo), y: 4, z: 4, core: 2. Of those that a mesh axis runs over, the one named last changes fastest.
Arguments:
- grid_state: bfloat16 [131072, 1024], P('seq', 'head'), may hold values from -6 to 6
- encode_index: int32 [256, 8], P('seq'), may hold values from 0 to 1023, as said below
- encode_weights: bfloat16 [256, 8, 128, 128], P('seq'), may hold values from -0.1875 to 0.1875
- first_gain: float32 [1024], replicated, may hold values from 0.1 to 1.9
- project_in: bfloat16 [1024, 3, 1024], P(None, None, 'head'), may hold values from -8 to 8
- project_out: bfloat16 [1024, 1024], P('head'), may hold values from -0.25 to 0.25
- second_gain: float32 [1024], replicated, may hold values from 0.1 to 1.9
- expand_weights: bfloat16 [1024, 4096], P(None, 'head'), may hold values from -0.1875 to 0.1875
- shrink_weights: bfloat16 [4096, 1024], P('head'), may hold values from -0.125 to 0.125
- decode_index: int32 [1024, 2], P('seq'), may hold values from 0 to 255, as said below
- decode_weights: bfloat16 [1024, 2, 128, 128], P('seq'), may hold values from -0.375 to 0.375
- output_gain: float32 [1024], P('head'), may hold values from 0.1 to 1.9
Outputs:
- grid_output: bfloat16 [131072, 1024], P('seq', 'head')
The draws below stay inside these ranges and needn't reach their ends.
Inputs may be any that keep to these rules, and one draw needn't show every extreme that they name: `encode_index`: for a mesh block of band b (blocks b * 16 onward), every entry lies in b * 64 - 2048 / 128 to (b + 1) * 64 + 2048 / 128 - 1. `decode_index`: for a grid block of band b (blocks b * 64 onward), every entry lies in b * 16 - 2048 / 256 to (b + 1) * 16 + 2048 / 256 - 1, with the division rounded down.
All inputs are finite; a program needn't handle non-finite values.
Results may differ from the reference program's by a relative error of at most 0.012.
Values may be sent and summed in bfloat16 or wider, within the bound.
No kernel may reach another device: no remote copies, remote signals or barrier semaphores. Data moves between devices by JAX's collectives and lax.ppermute only.
A program may use at most 128 MiB of HBM per device.

```python
import jax
import jax.numpy as jnp
from jax import lax

D = 1024
HEADS = 16
MLP = 4096
HEAD_DIM = 64
WINDOW = 1120
M_DEV = 2048
G_DEV = 8192
BLOCK = 128
SLOTS_IN = 8
SLOTS_OUT = 2
GRID = 131072
MESH_BLOCKS = 256
GRID_BLOCKS = 1024


def band_table(key, row_count, rows_band, rim_blocks, own_blocks, total_blocks, slot_count):
    row_iota = jnp.arange(row_count, dtype=jnp.int32)
    band_number = row_iota // rows_band
    lowest = jnp.maximum(band_number * own_blocks - rim_blocks, 0)
    highest = jnp.minimum((band_number + 1) * own_blocks + rim_blocks, total_blocks)
    drawn = jax.random.randint(key, (row_count, slot_count), lowest[:, None], highest[:, None])
    within = row_iota % rows_band
    drawn = drawn.at[:, 0].set(jnp.where(within == 0, lowest, drawn[:, 0]))
    drawn = drawn.at[:, slot_count - 1].set(jnp.where(within == rows_band - 1, highest - 1, drawn[:, slot_count - 1]))
    return drawn.astype(jnp.int32)


def draw_encode_index(key, part):
    mesh_band = M_DEV // BLOCK
    return band_table(jax.random.fold_in(key, 11), MESH_BLOCKS, mesh_band, mesh_band, G_DEV // BLOCK, GRID_BLOCKS, SLOTS_IN)


def draw_decode_index(key, part):
    mesh_band = M_DEV // BLOCK
    return band_table(jax.random.fold_in(key, 13), GRID_BLOCKS, G_DEV // BLOCK, mesh_band // 2, mesh_band, MESH_BLOCKS, SLOTS_OUT)


def draw_project_in(key, part):
    matrix = jax.random.normal(jax.random.fold_in(key, 17), (D, 3, D), jnp.float32) * D ** (-0.5)
    return jnp.clip(matrix, -8.0, 8.0).astype(jnp.bfloat16)


def strengthened(array, key, source, target, parts, factor):
    owner, partner = [(jnp.arange(array.shape[dim]) // (array.shape[dim] // parts)).reshape([-1 if axis == dim else 1 for axis in range(array.ndim)]) for dim in (source, target)]
    chosen = jax.random.permutation(key, parts)[partner]
    strong = (owner == chosen) | (owner == (partner + parts // 2) % parts)
    return jnp.where(strong, factor * array, array)


def level_of(stream_key, shape, pieces, least, high):
    def one(dim, blocks):
        steps = jax.random.uniform(jax.random.fold_in(jax.random.fold_in(stream_key, 6), dim), (blocks,), jnp.float32, least / len(pieces), high / len(pieces))
        return jnp.repeat(jnp.exp(steps), shape[dim] // blocks).reshape((-1,) + (1,) * (len(shape) - dim - 1))

    factor_of = one(*pieces[0])
    for cut in pieces[1:]:
        factor_of = factor_of * one(*cut)
    return factor_of


def bell_draw(key, extent, scale, limit, split=(), held_as=jnp.bfloat16):
    level = level_of(key, extent, split, -0.22, 0.18) if split else 1.0
    result = jax.random.normal(key, extent, jnp.float32) * scale * level
    return jnp.minimum(jnp.maximum(result, -limit), limit).astype(held_as)


def heavy_noise(own_key, shape, scale, bound, cuts, heavy, kind=jnp.bfloat16):
    result = scale * jax.random.normal(own_key, shape, jnp.float32)
    if cuts:
        result = result * level_of(own_key, shape, cuts, -0.22, 0.18)
    return jnp.clip(strengthened(result, jax.random.fold_in(own_key, 3), *heavy), -bound, bound).astype(kind)


def setup_inputs(seed: int = 0) -> dict:
    key_of = jax.random.split(jax.random.key(seed), 13)
    return {
        "grid_state": bell_draw(key_of[0], (GRID, D), 1.0, 6.0, ((0, 16), (1, 8))),
        "encode_index": draw_encode_index(jax.random.fold_in(key_of[12], 71), 0),
        "encode_weights": bell_draw(key_of[2], (MESH_BLOCKS, SLOTS_IN, BLOCK, BLOCK), (SLOTS_IN * BLOCK) ** -0.5, 0.1875, ((0, 16),)),
        "first_gain": jnp.clip(1.0 + 0.18 * jax.random.normal(key_of[3], (D,), jnp.float32), 0.1, 1.9),
        "project_in": draw_project_in(jax.random.fold_in(key_of[12], 71), 0),
        "project_out": heavy_noise(key_of[5], (D, D), D ** -0.5, 0.25, ((0, 8),), (0, 1, 8, 2.0)),
        "second_gain": jnp.clip(1.0 + 0.18 * jax.random.normal(key_of[6], (D,), jnp.float32), 0.1, 1.9),
        "expand_weights": bell_draw(key_of[7], (D, MLP), D ** -0.5, 0.1875, ((1, 8),)),
        "shrink_weights": heavy_noise(key_of[8], (MLP, D), MLP ** -0.5, 0.125, ((0, 8),), (0, 1, 8, 2.0)),
        "decode_index": draw_decode_index(jax.random.fold_in(key_of[12], 71), 0),
        "decode_weights": bell_draw(key_of[10], (GRID_BLOCKS, SLOTS_OUT, BLOCK, BLOCK), (SLOTS_OUT * BLOCK) ** -0.5, 0.375, ((0, 16),)),
        "output_gain": jnp.clip(1.0 + 0.18 * jax.random.normal(key_of[11], (D,), jnp.float32), 0.1, 1.9),
    }


EPSILON = 1e-05

def settle(values):
    return lax.optimization_barrier(values)

def layer_norm(values, scales):
    average = lax.optimization_barrier(jnp.mean(values, axis=1, keepdims=True))
    centred = values - average
    spread = lax.optimization_barrier(jnp.mean(centred * centred, axis=1, keepdims=True))
    return centred * lax.rsqrt(spread + EPSILON) * scales

def interpolate(source, index_table, weight_table):
    columns = source.shape[1]
    blocks = source.reshape(-1, BLOCK, columns)

    def one_block(pair):
        position, weight_block = pair
        picked = jnp.take(blocks, position, axis=0).astype(jnp.float32)
        return jnp.einsum('kij,kjc->ic', weight_block.astype(jnp.float32), picked, precision=lax.Precision.HIGHEST)
    return lax.map(one_block, (index_table, weight_table)).reshape(-1, columns)

def window_mask(query_rows, key_count, key_anchor, total_rows):
    query_iota = lax.broadcasted_iota(jnp.int32, (query_rows, key_count), 0)
    key_iota = lax.broadcasted_iota(jnp.int32, (query_rows, key_count), 1)
    distance = key_iota - query_iota
    global_key = key_anchor + key_iota
    return (distance >= 0) & (distance <= 2 * WINDOW) & (global_key >= 0) & (global_key < total_rows)

def softmax_values(scores, allowed, value_block):
    masked = jnp.where(allowed[None], scores, -1e+30)
    highest = lax.optimization_barrier(jnp.max(masked, axis=2, keepdims=True))
    powers = jnp.where(allowed[None], jnp.exp(masked - highest), 0.0)
    probs = settle((powers / lax.optimization_barrier(jnp.sum(powers, axis=2, keepdims=True))).astype(jnp.bfloat16))
    context = jnp.einsum('hqk,khd->qhd', probs.astype(jnp.float32), value_block, precision=lax.Precision.HIGHEST)
    return context.astype(jnp.bfloat16)

def attention(queries, keys, values):
    total_rows = queries.shape[0]
    query_rows = min(512, M_DEV)
    key_count = query_rows + 2 * WINDOW
    padding = ((WINDOW, WINDOW), (0, 0), (0, 0))
    keys_wide = jnp.pad(keys, padding)
    values_wide = jnp.pad(values, padding)

    def attend(first_row):
        query_block = lax.dynamic_slice_in_dim(queries, first_row, query_rows, 0).astype(jnp.float32)
        key_block = lax.dynamic_slice_in_dim(keys_wide, first_row, key_count, 0).astype(jnp.float32)
        value_block = lax.dynamic_slice_in_dim(values_wide, first_row, key_count, 0).astype(jnp.float32)
        scores = jnp.einsum('qhd,khd->hqk', query_block, key_block, precision=lax.Precision.HIGHEST) * HEAD_DIM ** (-0.5)
        allowed = window_mask(query_rows, key_count, first_row - WINDOW, total_rows)
        return softmax_values(scores, allowed, value_block)
    starts = jnp.arange(total_rows // query_rows, dtype=jnp.int32) * query_rows
    return lax.map(attend, starts).reshape(total_rows, HEADS * HEAD_DIM)

def reference(grid_state, encode_index, encode_weights, first_gain, project_in, project_out, second_gain, expand_weights, shrink_weights, decode_index, decode_weights, output_gain):
    mesh_start = settle(interpolate(grid_state, encode_index, encode_weights).astype(jnp.bfloat16))
    first_norm = layer_norm(mesh_start.astype(jnp.float32), first_gain).astype(jnp.bfloat16)
    heads_shape = (mesh_start.shape[0], HEADS, HEAD_DIM)
    queries = settle(jnp.dot(first_norm, project_in[:, 0, :], preferred_element_type=jnp.float32).astype(jnp.bfloat16)).reshape(heads_shape)
    keys = settle(jnp.dot(first_norm, project_in[:, 1, :], preferred_element_type=jnp.float32).astype(jnp.bfloat16)).reshape(heads_shape)
    values = settle(jnp.dot(first_norm, project_in[:, 2, :], preferred_element_type=jnp.float32).astype(jnp.bfloat16)).reshape(heads_shape)
    context = attention(queries, keys, values)
    attended = jnp.dot(context, project_out, preferred_element_type=jnp.float32)
    mesh_middle = settle((mesh_start.astype(jnp.float32) + attended).astype(jnp.bfloat16))
    second_norm = layer_norm(mesh_middle.astype(jnp.float32), second_gain).astype(jnp.bfloat16)
    hidden = jax.nn.gelu(jnp.dot(second_norm, expand_weights, preferred_element_type=jnp.float32)).astype(jnp.bfloat16)
    shrunk = jnp.dot(hidden, shrink_weights, preferred_element_type=jnp.float32)
    mesh_end = settle((mesh_middle.astype(jnp.float32) + shrunk).astype(jnp.bfloat16))
    back = interpolate(mesh_end, decode_index, decode_weights)
    average = lax.optimization_barrier(jnp.sum(back, axis=1, keepdims=True)) / D
    squares = lax.optimization_barrier(jnp.sum(back * back, axis=1, keepdims=True)) / D
    normed = (back - average) * lax.rsqrt(squares - average * average + EPSILON) * output_gain
    return (grid_state.astype(jnp.float32) + normed).astype(jnp.bfloat16)
```

```python
import jax
import jax.numpy as jnp
from jax import lax
from jax.experimental import pallas as pl
from jax.experimental.pallas import tpu as pltpu
from jax.sharding import PartitionSpec as P

D = 1024
HEAD_DIM = 64
WINDOW = 1120
REACH = 1152
BLOCK = 128
EPSILON = 1e-05
LOG2E = 1.4426950408889634
BF = jnp.bfloat16
F32 = jnp.float32
NT = (((1,), (1,)), ((), ()))
TN = (((0,), (0,)), ((), ()))
MIB = 1 << 20


def params(mib):
    return pltpu.CompilerParams(
        dimension_semantics=("arbitrary",), vmem_limit_bytes=mib * MIB
    )


def dot(a, b):
    return jnp.dot(a, b, preferred_element_type=F32)


ANY = pl.BlockSpec(memory_space=pl.ANY)


def whole(shape):
    return pl.BlockSpec(shape, lambda i, *_: (0,) * len(shape))


def encode_kernel(index, low, own, high, weights, out, source, sems):
    step = pl.program_id(0)
    rim = low.shape[0]

    @pl.when(step == 0)
    def _():
        copies = [
            pltpu.make_async_copy(low, source.at[pl.ds(0, rim)], sems.at[0]),
            pltpu.make_async_copy(own, source.at[pl.ds(rim, own.shape[0])], sems.at[1]),
            pltpu.make_async_copy(
                high, source.at[pl.ds(rim + own.shape[0], rim)], sems.at[2]
            ),
        ]
        for c in copies:
            c.start()
        for c in copies:
            c.wait()

    per, slots = weights.shape[0], weights.shape[1]
    for b in range(per):
        left = jnp.concatenate([weights[b, k] for k in range(slots)], axis=1)
        right = jnp.concatenate(
            [source[index[step * per + b, k]] for k in range(slots)], axis=0
        )
        out[b * BLOCK : (b + 1) * BLOCK] = dot(left, right).astype(BF)


def encode(index, low, own, high, weights):
    count, slots = weights.shape[:2]
    per = 2
    blocks = own.shape[0] // BLOCK
    rim = low.shape[0] // BLOCK
    shaped = [v.reshape(-1, BLOCK, BLOCK) for v in (low, own, high)]
    return pl.pallas_call(
        encode_kernel,
        out_shape=jax.ShapeDtypeStruct((count * BLOCK, BLOCK), BF),
        grid_spec=pltpu.PrefetchScalarGridSpec(
            num_scalar_prefetch=1,
            grid=(count // per,),
            in_specs=[
                ANY,
                ANY,
                ANY,
                pl.BlockSpec((per, slots, BLOCK, BLOCK), lambda i, _: (i, 0, 0, 0)),
            ],
            out_specs=pl.BlockSpec((per * BLOCK, BLOCK), lambda i, _: (i, 0)),
            scratch_shapes=[
                pltpu.VMEM((blocks + 2 * rim, BLOCK, BLOCK), BF),
                pltpu.SemaphoreType.DMA((3,)),
            ],
        ),
        compiler_params=params(24),
        name="encode",
    )(index, *shaped, weights)


def project_kernel(
    order, s0, s1, s2, s3, s4, s5, lo6, hi6, lo7, hi7, gain, weights,
    queries, keys_values, share, ordered,
):
    step = pl.program_id(0)
    half = pl.num_programs(0) // 2

    @pl.when(step == 0)
    def _():
        for p in range(8):
            ordered[p * BLOCK : (p + 1) * BLOCK] = weights[order[p]]

    early = step < half
    raw = [s[...] for s in (s0, s1, s2, s3, s4, s5)]
    raw.append(jnp.where(early, lo6[...], hi6[...]))
    raw.append(jnp.where(early, lo7[...], hi7[...]))

    @pl.when(step == order[0])
    def _():
        for p in range(8):
            share[order[p]] = raw[p]

    pieces = [r.astype(F32) for r in raw]
    total = pieces[0]
    for x in pieces[1:]:
        total = total + x
    average = jnp.sum(total, axis=1, keepdims=True) * (1.0 / D)
    pieces = [x - average for x in pieces]
    total = pieces[0] * pieces[0]
    for x in pieces[1:]:
        total = total + x * x
    spread = lax.rsqrt(jnp.sum(total, axis=1, keepdims=True) * (1.0 / D) + EPSILON)
    normed = jnp.concatenate(
        [(x * spread * gain[order[p]]).astype(BF) for p, x in enumerate(pieces)], axis=1
    )
    made = dot(normed, ordered[...]).astype(BF)
    queries[...] = (made[:, :BLOCK].astype(F32) * (HEAD_DIM**-0.5)).astype(BF)
    keys_values[...] = made[:, BLOCK:]


def project(order, slots, gain, weights):
    rows = slots[0].shape[0]
    tile = rows // 8
    full = pl.BlockSpec((tile, BLOCK), lambda i, _: (i, 0))
    early = pl.BlockSpec((tile, BLOCK), lambda i, _: (jnp.minimum(i, 3), 0))
    late = pl.BlockSpec((tile, BLOCK), lambda i, _: (jnp.maximum(i - 4, 0), 0))
    return pl.pallas_call(
        project_kernel,
        out_shape=(
            jax.ShapeDtypeStruct((rows, BLOCK), BF),
            jax.ShapeDtypeStruct((rows, 2 * BLOCK), BF),
            jax.ShapeDtypeStruct((8, tile, BLOCK), BF),
        ),
        grid_spec=pltpu.PrefetchScalarGridSpec(
            num_scalar_prefetch=1,
            grid=(8,),
            in_specs=[full] * 6
            + [early, late, early, late]
            + [whole((8, 1, BLOCK)), whole((8, BLOCK, 3 * BLOCK))],
            out_specs=(
                full,
                pl.BlockSpec((tile, 2 * BLOCK), lambda i, _: (i, 0)),
                whole((8, tile, BLOCK)),
            ),
            scratch_shapes=[pltpu.VMEM((D, 3 * BLOCK), BF)],
        ),
        compiler_params=params(24),
        name="project",
    )(order, *slots, gain.reshape(8, 1, BLOCK), weights.reshape(8, BLOCK, 3 * BLOCK))


TILE = 256
SPAN = TILE + 2 * REACH
CHUNKS = SPAN // TILE


def attend_kernel(edges, queries, low, own, high, out, keys, values, scores, sems):
    step = pl.program_id(0)
    rows = own.shape[0]

    @pl.when(step == 0)
    def _():
        copies = []
        for n, (part, start) in enumerate(
            ((low, 0), (own, REACH), (high, REACH + rows))
        ):
            for m, target in enumerate((keys, values)):
                copies.append(
                    pltpu.make_async_copy(
                        part.at[:, pl.ds(m * BLOCK, BLOCK)],
                        target.at[pl.ds(start, part.shape[0]), pl.ds(0, BLOCK)],
                        sems.at[2 * n + m],
                    )
                )
        for c in copies:
            c.start()
        values[:, BLOCK:] = jnp.ones((values.shape[0], BLOCK), BF)
        first = lax.broadcasted_iota(jnp.int32, (keys.shape[0], BLOCK), 1) == 0
        row = lax.broadcasted_iota(jnp.int32, (keys.shape[0], BLOCK), 0)
        absent = ((row < REACH) & (edges[0] == 1)) | (
            (row >= REACH + rows) & (edges[1] == 1)
        )
        keys[:, BLOCK:] = jnp.where(first & absent, -1e30, 0.0).astype(BF)
        for c in copies:
            c.wait()

    lane = lax.broadcasted_iota(jnp.int32, (TILE, BLOCK), 1)
    q = queries[...]
    zero = jnp.zeros_like(q)
    both = jnp.concatenate(
        [jnp.where(lane < HEAD_DIM, q, zero), jnp.where(lane < HEAD_DIM, zero, q)], axis=0
    )
    mark = jnp.where(
        lax.broadcasted_iota(jnp.int32, (2 * TILE, BLOCK), 1) == 0, 1.0, 0.0
    ).astype(BF)
    stacked = jnp.concatenate([both, mark], axis=1)
    row = lax.broadcasted_iota(jnp.int32, (2 * TILE, TILE), 0) & (TILE - 1)
    column = lax.broadcasted_iota(jnp.int32, (2 * TILE, TILE), 1)
    highest = jnp.full((2 * TILE, BLOCK), -1e30, F32)
    for c in range(CHUNKS):
        part = keys[pl.ds(pl.multiple_of((step + c) * TILE, TILE), TILE)]
        s = lax.dot_general(stacked, part, NT, preferred_element_type=F32)
        least = c * TILE - REACH
        gap = column - row + least
        if least - TILE < -WINDOW:
            s = jnp.where(gap >= -WINDOW, s, -1e30)
        if least + TILE > WINDOW:
            s = jnp.where(gap <= WINDOW, s, -1e30)
        scores[:, c * TILE : (c + 1) * TILE] = s
        highest = jnp.maximum(highest, jnp.maximum(s[:, :BLOCK], s[:, BLOCK:]))
    peak = jnp.max(highest, axis=1, keepdims=True) * LOG2E
    total = jnp.zeros((2 * TILE, 2 * BLOCK), F32)
    for c in range(CHUNKS):
        part = values[pl.ds(pl.multiple_of((step + c) * TILE, TILE), TILE)]
        powers = jnp.exp2(scores[:, c * TILE : (c + 1) * TILE] * LOG2E - peak)
        total = total + dot(powers.astype(BF), part)
    made = total[:, :BLOCK] / total[:, BLOCK:]
    out[...] = jnp.where(lane < HEAD_DIM, made[:TILE], made[TILE:]).astype(BF)


def attend(edges, queries, low, own, high):
    rows = own.shape[0]
    return pl.pallas_call(
        attend_kernel,
        out_shape=jax.ShapeDtypeStruct((rows, BLOCK), BF),
        grid_spec=pltpu.PrefetchScalarGridSpec(
            num_scalar_prefetch=1,
            grid=(rows // TILE,),
            in_specs=[pl.BlockSpec((TILE, BLOCK), lambda i, _: (i, 0)), ANY, ANY, ANY],
            out_specs=pl.BlockSpec((TILE, BLOCK), lambda i, _: (i, 0)),
            scratch_shapes=[
                pltpu.VMEM((rows + 2 * REACH, 2 * BLOCK), BF),
                pltpu.VMEM((rows + 2 * REACH, 2 * BLOCK), BF),
                pltpu.VMEM((2 * TILE, SPAN), F32),
                pltpu.SemaphoreType.DMA((6,)),
            ],
        ),
        compiler_params=params(32),
        name="attend",
    )(edges, queries, low, own, high)


ROWS_E = 64
ROWS_S = 64
ROWS_P = 16
PACK = ROWS_E + ROWS_S + ROWS_P


def pack_weights(position, expand, shrink, project_out):
    part = lax.dynamic_slice_in_dim(expand, position * 2 * ROWS_E, 2 * ROWS_E, 0)
    return jnp.concatenate(
        [
            jnp.concatenate([part[:ROWS_E], part[ROWS_E:]], axis=1),
            lax.dynamic_slice_in_dim(shrink, position * ROWS_S, ROWS_S, 0),
            lax.dynamic_slice_in_dim(project_out, position * ROWS_P, ROWS_P, 0),
        ],
        axis=0,
    )


def gelu(v):
    return 0.5 * v * (1.0 + jnp.tanh(0.7978845608028654 * (v + 0.044715 * v * v * v)))


def forward_kernel(table, *refs):
    parts = refs[:10]
    context, share, gain, out, expand, shrink, outward, sems = refs[10:]
    groups = ([], [], [])
    width = expand.shape[2]
    for n, part in enumerate(parts):
        first = 4 if n % 5 == 4 else 0
        count = part.shape[0]
        where = table[8 + n]
        slots = pl.ds(first, count)

        def copy(group, source, target):
            groups[group].append(
                pltpu.make_async_copy(source, target, sems.at[group, len(groups[group])])
            )

        copy(
            0,
            part.at[:, pl.ds(ROWS_E + ROWS_S, ROWS_P), :],
            outward.at[slots, pl.ds(pl.multiple_of(where * ROWS_P, ROWS_P), ROWS_P), :],
        )
        for side in range(2):
            copy(
                1,
                part.at[:, pl.ds(0, ROWS_E), pl.ds(side * width, width)],
                expand.at[
                    slots,
                    pl.ds(pl.multiple_of(where * 2 * ROWS_E + side * ROWS_E, ROWS_E), ROWS_E),
                    :,
                ],
            )
        copy(
            2,
            part.at[:, pl.ds(ROWS_E, ROWS_S), :],
            shrink.at[slots, pl.ds(pl.multiple_of(where * ROWS_S, ROWS_S), ROWS_S), :],
        )
    for group in groups:
        for c in group:
            c.start()
    for c in groups[0]:
        c.wait()
    total = dot(context[table[0]], outward[0])
    for p in range(1, 8):
        total = total + dot(context[table[p]], outward[p])
    start = jnp.concatenate([share[h] for h in range(8)], axis=1).astype(F32)
    middle = (start + total).astype(BF).astype(F32)
    average = jnp.mean(middle, axis=1, keepdims=True)
    centred = middle - average
    spread = jnp.mean(centred * centred, axis=1, keepdims=True)
    normed = (centred * lax.rsqrt(spread + EPSILON) * gain[...]).astype(BF)
    for c in groups[1]:
        c.wait()
    hidden = [gelu(dot(normed, expand[p])).astype(BF) for p in range(8)]
    for c in groups[2]:
        c.wait()
    total = middle
    for p in range(8):
        total = total + dot(hidden[p], shrink[p])
    done = total.astype(BF)
    for h in range(8):
        out[h] = done[:, h * BLOCK : (h + 1) * BLOCK]


def forward(table, parts, context, share, gain):
    rows = share.shape[1]
    width = D // 2
    return pl.pallas_call(
        forward_kernel,
        out_shape=jax.ShapeDtypeStruct((8, rows, BLOCK), BF),
        grid_spec=pltpu.PrefetchScalarGridSpec(
            num_scalar_prefetch=1,
            grid=(1,),
            in_specs=[ANY] * 10
            + [whole((8, rows, BLOCK)), whole((8, rows, BLOCK)), whole((1, D))],
            out_specs=whole((8, rows, BLOCK)),
            scratch_shapes=[
                pltpu.VMEM((8, D, width), BF),
                pltpu.VMEM((8, width, D), BF),
                pltpu.VMEM((8, BLOCK, D), BF),
                pltpu.SemaphoreType.DMA((3, 20)),
            ],
        ),
        compiler_params=params(48),
        name="forward",
    )(table, *parts, context, share, gain.reshape(1, D))


EACH = 8


def decode_kernel(index, low, own, high, weights, back, sums, source, sems):
    step = pl.program_id(0)
    rim = low.shape[0]

    @pl.when(step == 0)
    def _():
        copies = [
            pltpu.make_async_copy(low, source.at[pl.ds(0, rim)], sems.at[0]),
            pltpu.make_async_copy(own, source.at[pl.ds(rim, own.shape[0])], sems.at[1]),
            pltpu.make_async_copy(
                high, source.at[pl.ds(rim + own.shape[0], rim)], sems.at[2]
            ),
        ]
        for c in copies:
            c.start()
        for c in copies:
            c.wait()

    slots = weights.shape[1]
    ones = jnp.ones((2 * EACH, BLOCK), BF)
    row = lax.broadcasted_iota(jnp.int32, (2 * EACH, BLOCK), 0)
    held = jnp.zeros((2 * EACH, BLOCK), F32)
    for b in range(EACH):
        left = jnp.concatenate([weights[b, k] for k in range(slots)], axis=1)
        right = jnp.concatenate(
            [source[index[step * EACH + b, k]] for k in range(slots)], axis=0
        )
        made = dot(left, right)
        back[b * BLOCK : (b + 1) * BLOCK] = made
        plain = lax.dot_general(ones, made.astype(BF), NT, preferred_element_type=F32)
        square = lax.dot_general(
            ones, (made * made).astype(BF), NT, preferred_element_type=F32
        )
        held = jnp.where(row == b, plain, jnp.where(row == EACH + b, square, held))
    sums[0] = held.astype(BF)


def decode(index, low, own, high, weights):
    count, slots = weights.shape[:2]
    blocks = own.shape[0]
    rim = low.shape[0]
    steps = count // EACH
    return pl.pallas_call(
        decode_kernel,
        out_shape=(
            jax.ShapeDtypeStruct((count * BLOCK, BLOCK), F32),
            jax.ShapeDtypeStruct((steps, 2 * EACH, BLOCK), BF),
        ),
        grid_spec=pltpu.PrefetchScalarGridSpec(
            num_scalar_prefetch=1,
            grid=(steps,),
            in_specs=[
                ANY,
                ANY,
                ANY,
                pl.BlockSpec((EACH, slots, BLOCK, BLOCK), lambda i, _: (i, 0, 0, 0)),
            ],
            out_specs=(
                pl.BlockSpec((EACH * BLOCK, BLOCK), lambda i, _: (i, 0)),
                pl.BlockSpec((1, 2 * EACH, BLOCK), lambda i, _: (i, 0, 0)),
            ),
            scratch_shapes=[
                pltpu.VMEM((blocks + 2 * rim, BLOCK, BLOCK), BF),
                pltpu.SemaphoreType.DMA((3,)),
            ],
        ),
        compiler_params=params(24),
        name="decode",
    )(index, low, own, high, weights)


def finish_kernel(sums, back, state, gain, out):
    count = sums.shape[0]
    stats = jnp.concatenate([sums[h, 0] for h in range(count)], axis=0)
    depth = count * 2 * EACH
    row = lax.broadcasted_iota(jnp.int32, (depth, 2 * EACH * BLOCK), 0)
    column = lax.broadcasted_iota(jnp.int32, (depth, 2 * EACH * BLOCK), 1)
    pick = jnp.where((row % (2 * EACH)) == (column // BLOCK), 1.0, 0.0).astype(BF)
    spread = lax.dot_general(stats, pick, TN, preferred_element_type=F32) * (1.0 / D)
    for b in range(EACH):
        rows = slice(b * BLOCK, (b + 1) * BLOCK)
        average = spread[:, b * BLOCK : (b + 1) * BLOCK]
        squares = spread[:, (EACH + b) * BLOCK : (EACH + b + 1) * BLOCK]
        scale = lax.rsqrt(squares - average * average + EPSILON) * gain[...]
        out[rows] = (
            state[rows].astype(F32) + (back[rows] - average) * scale
        ).astype(BF)


def finish(sums, back, state, gain):
    rows = state.shape[0]
    tile = pl.BlockSpec((EACH * BLOCK, BLOCK), lambda i: (i, 0))
    return pl.pallas_call(
        finish_kernel,
        out_shape=jax.ShapeDtypeStruct((rows, BLOCK), BF),
        grid_spec=pl.GridSpec(
            grid=(rows // (EACH * BLOCK),),
            in_specs=[
                pl.BlockSpec((sums.shape[0], 1, 2 * EACH, BLOCK), lambda i: (0, i, 0, 0)),
                tile,
                tile,
                pl.BlockSpec((1, BLOCK), lambda i: (0, 0)),
            ],
            out_specs=tile,
        ),
        compiler_params=params(24),
        name="finish",
    )(sums, back, state, gain.reshape(1, BLOCK))


def shifted(value, by):
    return lax.ppermute(value, "seq", [(i, i + by) for i in range(16) if 0 <= i + by < 16])


def among(value, axis, count, to):
    return lax.ppermute(value, axis, [(i, to(i)) for i in range(count)])


def head_ring(x):
    half = x.shape[0] // 2
    north = lambda v: among(v, "head", 8, lambda i: (i + 2) % 8)
    south = lambda v: among(v, "head", 8, lambda i: (i - 2) % 8)
    y = among(x, "head", 8, lambda i: i ^ 1)
    xa, xb = north(x), south(x)
    ya, yb = north(y), south(y)
    return (
        x, y, xa, ya, xb, yb,
        north(xa[:half]), south(xb[half:]), north(ya[:half]), south(yb[half:]),
    )


def along_z(i, by):
    return (i // 8) * 8 + ((i // 2 + by) % 4) * 2 + i % 2


def gathered_weights(packed):
    s = head_ring(packed)
    mine = jnp.stack(
        s[:6] + (jnp.concatenate(s[6:8], axis=0), jnp.concatenate(s[8:10], axis=0))
    )
    up = lambda v: among(v, "seq", 16, lambda i: along_z(i, 1))
    down = lambda v: among(v, "seq", 16, lambda i: along_z(i, -1))
    a, b = up(mine), down(mine)
    here = [mine, a, b, up(a[:4]), down(b[4:])]
    return here + [among(v, "seq", 16, lambda i: i ^ 1) for v in here]


def on_device(
    grid_state,
    encode_index,
    encode_weights,
    first_gain,
    project_in,
    project_out,
    second_gain,
    expand_weights,
    shrink_weights,
    decode_index,
    decode_weights,
    output_gain,
):
    band = lax.axis_index("seq")
    bands = lax.axis_size("seq")
    me = lax.axis_index("head")
    mesh_blocks = encode_weights.shape[0]
    mesh_rows = mesh_blocks * BLOCK
    grid_blocks = grid_state.shape[0] // BLOCK
    rim = mesh_blocks * BLOCK
    low = shifted(grid_state[-rim:], 1)
    high = shifted(grid_state[:rim], -1)

    position = band % 8
    parts = gathered_weights(
        pack_weights(position, expand_weights, shrink_weights, project_out)
    )

    mesh_start = encode(
        encode_index - (band * grid_blocks - mesh_blocks), low, grid_state, high, encode_weights
    )
    slots = head_ring(mesh_start)
    partner = me ^ 1
    order = jnp.stack(
        [me, partner] + [(v + by) % 8 for by in (6, 2, 4) for v in (me, partner)]
    ).astype(jnp.int32)
    queries, keys_values, share = project(order, slots, first_gain, project_in)
    below = shifted(keys_values[mesh_rows - REACH :], 1)
    above = shifted(keys_values[:REACH], -1)
    edges = jnp.stack([band == 0, band == bands - 1]).astype(jnp.int32)
    context = attend(edges, queries, below, keys_values, above)
    context = lax.all_to_all(
        context.reshape(8, mesh_rows // 8, BLOCK), "head", 0, 0, tiled=True
    )
    z, core = position // 2, position % 2
    places = [
        ((z + by) % 4) * 2 + side
        for side in (core, 1 - core)
        for by in (0, 3, 1, 2, 2)
    ]
    table = jnp.concatenate([order, jnp.stack(places).astype(jnp.int32)])
    mesh_end = forward(table, parts, context, share, second_gain)
    mesh_end = lax.all_to_all(mesh_end, "head", 0, 0, tiled=True)
    mesh_end = mesh_end.reshape(mesh_blocks, BLOCK, BLOCK)
    edge = mesh_blocks // 2
    back, sums = decode(
        decode_index - (band * mesh_blocks - edge),
        shifted(mesh_end[-edge:], 1),
        mesh_end,
        shifted(mesh_end[:edge], -1),
        decode_weights,
    )
    sums = lax.all_to_all(
        jnp.broadcast_to(sums, (8, *sums.shape)), "head", 0, 0, tiled=True
    )
    return finish(sums, back, grid_state, output_gain)


def solution(mesh):
    in_specs = (
        P("seq", "head"),
        P("seq", None),
        P("seq", None, None, None),
        P(),
        P(None, None, "head"),
        P("head", None),
        P(),
        P(None, "head"),
        P("head", None),
        P("seq", None),
        P("seq", None, None, None),
        P("head"),
    )
    return jax.shard_map(
        on_device, mesh=mesh, in_specs=in_specs, out_specs=P("seq", "head"), check_vma=False
    )
```

```python
import jax
import jax.numpy as jnp
from jax import lax
from jax.experimental import pallas as pl
from jax.experimental.pallas import tpu as pltpu
from jax.sharding import PartitionSpec as P

D = 1024
HEAD_DIM = 64
WINDOW = 1120
REACH = 1152
BLOCK = 128
EPSILON = 1e-05
LOG2E = 1.4426950408889634
BF = jnp.bfloat16
F32 = jnp.float32
NT = (((1,), (1,)), ((), ()))
TN = (((0,), (0,)), ((), ()))
MIB = 1 << 20


def params(mib):
    return pltpu.CompilerParams(
        dimension_semantics=("arbitrary",), vmem_limit_bytes=mib * MIB
    )


def dot(a, b):
    return jnp.dot(a, b, preferred_element_type=F32)


def cost(flops, moved, powers=0):
    return pl.CostEstimate(flops=flops, bytes_accessed=moved, transcendentals=powers)


ANY = pl.BlockSpec(memory_space=pl.ANY)


def whole(shape):
    return pl.BlockSpec(shape, lambda i, *_: (0,) * len(shape))


def encode_kernel(index, low, own, high, weights, out, source, sems):
    step = pl.program_id(0)
    rim = low.shape[0]

    @pl.when(step == 0)
    def _():
        copies = [
            pltpu.make_async_copy(low, source.at[pl.ds(0, rim)], sems.at[0]),
            pltpu.make_async_copy(own, source.at[pl.ds(rim, own.shape[0])], sems.at[1]),
            pltpu.make_async_copy(
                high, source.at[pl.ds(rim + own.shape[0], rim)], sems.at[2]
            ),
        ]
        for c in copies:
            c.start()
        for c in copies:
            c.wait()

    per, slots = weights.shape[0], weights.shape[1]
    for b in range(per):
        left = jnp.concatenate([weights[b, k] for k in range(slots)], axis=1)
        right = jnp.concatenate(
            [source[index[step * per + b, k]] for k in range(slots)], axis=0
        )
        out[b * BLOCK : (b + 1) * BLOCK] = dot(left, right).astype(BF)


def encode(index, low, own, high, weights):
    count, slots = weights.shape[:2]
    per = 2
    blocks = own.shape[0] // BLOCK
    rim = low.shape[0] // BLOCK
    shaped = [v.reshape(-1, BLOCK, BLOCK) for v in (low, own, high)]
    return pl.pallas_call(
        encode_kernel,
        out_shape=jax.ShapeDtypeStruct((count * BLOCK, BLOCK), BF),
        grid_spec=pltpu.PrefetchScalarGridSpec(
            num_scalar_prefetch=1,
            grid=(count // per,),
            in_specs=[
                ANY,
                ANY,
                ANY,
                pl.BlockSpec((per, slots, BLOCK, BLOCK), lambda i, _: (i, 0, 0, 0)),
            ],
            out_specs=pl.BlockSpec((per * BLOCK, BLOCK), lambda i, _: (i, 0)),
            scratch_shapes=[
                pltpu.VMEM((blocks + 2 * rim, BLOCK, BLOCK), BF),
                pltpu.SemaphoreType.DMA((3,)),
            ],
        ),
        compiler_params=params(56),
        cost_estimate=cost(540_000_000, 8_000_000),
        name="encode",
    )(index, *shaped, weights)


def project_kernel(
    order, s0, s1, s2, s3, s4, s5, lo6, hi6, lo7, hi7, gain, weights,
    queries, keys_values, share, ordered,
):
    step = pl.program_id(0)
    half = pl.num_programs(0) // 2

    @pl.when(step == 0)
    def _():
        for p in range(8):
            ordered[p * BLOCK : (p + 1) * BLOCK] = weights[order[p]]

    early = step < half
    raw = [s[...] for s in (s0, s1, s2, s3, s4, s5)]
    raw.append(jnp.where(early, lo6[...], hi6[...]))
    raw.append(jnp.where(early, lo7[...], hi7[...]))

    @pl.when(step == order[0])
    def _():
        for p in range(8):
            share[order[p]] = raw[p]

    pieces = [r.astype(F32) for r in raw]
    total = pieces[0]
    for x in pieces[1:]:
        total = total + x
    average = jnp.sum(total, axis=1, keepdims=True) * (1.0 / D)
    pieces = [x - average for x in pieces]
    total = pieces[0] * pieces[0]
    for x in pieces[1:]:
        total = total + x * x
    spread = lax.rsqrt(jnp.sum(total, axis=1, keepdims=True) * (1.0 / D) + EPSILON)
    normed = jnp.concatenate(
        [(x * spread * gain[order[p]]).astype(BF) for p, x in enumerate(pieces)], axis=1
    )
    made = dot(normed, ordered[...]).astype(BF)
    queries[...] = (made[:, :BLOCK].astype(F32) * (HEAD_DIM**-0.5)).astype(BF)
    keys_values[...] = made[:, BLOCK:]


def project(order, slots, gain, weights):
    rows = slots[0].shape[0]
    tile = rows // 8
    full = pl.BlockSpec((tile, BLOCK), lambda i, _: (i, 0))
    early = pl.BlockSpec((tile, BLOCK), lambda i, _: (jnp.minimum(i, 3), 0))
    late = pl.BlockSpec((tile, BLOCK), lambda i, _: (jnp.maximum(i - 4, 0), 0))
    return pl.pallas_call(
        project_kernel,
        out_shape=(
            jax.ShapeDtypeStruct((rows, BLOCK), BF),
            jax.ShapeDtypeStruct((rows, 2 * BLOCK), BF),
            jax.ShapeDtypeStruct((8, tile, BLOCK), BF),
        ),
        grid_spec=pltpu.PrefetchScalarGridSpec(
            num_scalar_prefetch=1,
            grid=(8,),
            in_specs=[full] * 6
            + [early, late, early, late]
            + [whole((8, 1, BLOCK)), whole((8, BLOCK, 3 * BLOCK))],
            out_specs=(
                full,
                pl.BlockSpec((tile, 2 * BLOCK), lambda i, _: (i, 0)),
                whole((8, tile, BLOCK)),
            ),
            scratch_shapes=[pltpu.VMEM((D, 3 * BLOCK), BF)],
        ),
        compiler_params=params(56),
        cost_estimate=cost(1_600_000_000, 7_000_000),
        name="project",
    )(order, *slots, gain.reshape(8, 1, BLOCK), weights)


TILE = 256
SPAN = TILE + 2 * REACH
CHUNKS = SPAN // TILE


def attend_kernel(edges, queries, low, own, high, out, keys, values, scores, sems):
    step = pl.program_id(0)
    rows = own.shape[0]

    @pl.when(step == 0)
    def _():
        copies = []
        for n, (part, start) in enumerate(
            ((low, 0), (own, REACH), (high, REACH + rows))
        ):
            for m, target in enumerate((keys, values)):
                copies.append(
                    pltpu.make_async_copy(
                        part.at[:, pl.ds(m * BLOCK, BLOCK)],
                        target.at[pl.ds(start, part.shape[0]), pl.ds(0, BLOCK)],
                        sems.at[2 * n + m],
                    )
                )
        for c in copies:
            c.start()
        values[:, BLOCK:] = jnp.ones((values.shape[0], BLOCK), BF)
        first = lax.broadcasted_iota(jnp.int32, (keys.shape[0], BLOCK), 1) == 0
        row = lax.broadcasted_iota(jnp.int32, (keys.shape[0], BLOCK), 0)
        absent = ((row < REACH) & (edges[0] == 1)) | (
            (row >= REACH + rows) & (edges[1] == 1)
        )
        keys[:, BLOCK:] = jnp.where(first & absent, -1e30, 0.0).astype(BF)
        for c in copies:
            c.wait()

    lane = lax.broadcasted_iota(jnp.int32, (TILE, BLOCK), 1)
    q = queries[...]
    zero = jnp.zeros_like(q)
    both = jnp.concatenate(
        [jnp.where(lane < HEAD_DIM, q, zero), jnp.where(lane < HEAD_DIM, zero, q)], axis=0
    )
    mark = jnp.where(
        lax.broadcasted_iota(jnp.int32, (2 * TILE, BLOCK), 1) == 0, 1.0, 0.0
    ).astype(BF)
    stacked = jnp.concatenate([both, mark], axis=1)
    row = lax.broadcasted_iota(jnp.int32, (2 * TILE, TILE), 0) & (TILE - 1)
    column = lax.broadcasted_iota(jnp.int32, (2 * TILE, TILE), 1)
    highest = jnp.full((2 * TILE, BLOCK), -1e30, F32)
    for c in range(CHUNKS):
        part = keys[pl.ds(pl.multiple_of((step + c) * TILE, TILE), TILE)]
        s = lax.dot_general(stacked, part, NT, preferred_element_type=F32)
        least = c * TILE - REACH
        gap = column - row + least
        if least - TILE < -WINDOW:
            s = jnp.where(gap >= -WINDOW, s, -1e30)
        if least + TILE > WINDOW:
            s = jnp.where(gap <= WINDOW, s, -1e30)
        scores[:, c * TILE : (c + 1) * TILE] = s
        highest = jnp.maximum(highest, jnp.maximum(s[:, :BLOCK], s[:, BLOCK:]))
    peak = jnp.max(highest, axis=1, keepdims=True) * LOG2E
    total = jnp.zeros((2 * TILE, 2 * BLOCK), F32)
    for c in range(CHUNKS):
        part = values[pl.ds(pl.multiple_of((step + c) * TILE, TILE), TILE)]
        powers = jnp.exp2(scores[:, c * TILE : (c + 1) * TILE] * LOG2E - peak)
        total = total + dot(powers.astype(BF), part)
    made = total[:, :BLOCK] / total[:, BLOCK:]
    out[...] = jnp.where(lane < HEAD_DIM, made[:TILE], made[TILE:]).astype(BF)


def attend(edges, queries, low, own, high):
    rows = own.shape[0]
    return pl.pallas_call(
        attend_kernel,
        out_shape=jax.ShapeDtypeStruct((rows, BLOCK), BF),
        grid_spec=pltpu.PrefetchScalarGridSpec(
            num_scalar_prefetch=1,
            grid=(rows // TILE,),
            in_specs=[pl.BlockSpec((TILE, BLOCK), lambda i, _: (i, 0)), ANY, ANY, ANY],
            out_specs=pl.BlockSpec((TILE, BLOCK), lambda i, _: (i, 0)),
            scratch_shapes=[
                pltpu.VMEM((rows + 2 * REACH, 2 * BLOCK), BF),
                pltpu.VMEM((rows + 2 * REACH, 2 * BLOCK), BF),
                pltpu.VMEM((2 * TILE, SPAN), F32),
                pltpu.SemaphoreType.DMA((6,)),
            ],
        ),
        compiler_params=params(56),
        cost_estimate=cost(10_700_000_000, 4_000_000, 10_500_000),
        name="attend",
    )(edges, queries, low, own, high)


ROWS_E = 64
ROWS_S = 64
ROWS_P = 16
PACK = ROWS_E + ROWS_S + ROWS_P


def pack_weights(position, expand, shrink, project_out):
    part = lax.dynamic_slice_in_dim(expand, position * 2 * ROWS_E, 2 * ROWS_E, 0)
    return jnp.concatenate(
        [
            jnp.concatenate([part[:ROWS_E], part[ROWS_E:]], axis=1),
            lax.dynamic_slice_in_dim(shrink, position * ROWS_S, ROWS_S, 0),
            lax.dynamic_slice_in_dim(project_out, position * ROWS_P, ROWS_P, 0),
        ],
        axis=0,
    )


def gelu(v):
    return 0.5 * v * (1.0 + jnp.tanh(0.7978845608028654 * (v + 0.044715 * v * v * v)))


def forward_kernel(table, *refs):
    parts = refs[:10]
    context, share, gain, out, expand, shrink, outward, sems = refs[10:]
    groups = ([], [], [])
    width = expand.shape[2]
    for n, part in enumerate(parts):
        first = 4 if n % 5 == 4 else 0
        count = part.shape[0]
        where = table[8 + n]
        slots = pl.ds(first, count)

        def copy(group, source, target):
            groups[group].append(
                pltpu.make_async_copy(source, target, sems.at[group, len(groups[group])])
            )

        copy(
            0,
            part.at[:, pl.ds(ROWS_E + ROWS_S, ROWS_P), :],
            outward.at[slots, pl.ds(pl.multiple_of(where * ROWS_P, ROWS_P), ROWS_P), :],
        )
        for side in range(2):
            copy(
                1,
                part.at[:, pl.ds(0, ROWS_E), pl.ds(side * width, width)],
                expand.at[
                    slots,
                    pl.ds(pl.multiple_of(where * 2 * ROWS_E + side * ROWS_E, ROWS_E), ROWS_E),
                    :,
                ],
            )
        copy(
            2,
            part.at[:, pl.ds(ROWS_E, ROWS_S), :],
            shrink.at[slots, pl.ds(pl.multiple_of(where * ROWS_S, ROWS_S), ROWS_S), :],
        )
    for group in groups:
        for c in group:
            c.start()
    for c in groups[0]:
        c.wait()
    total = dot(context[table[0]], outward[0])
    for p in range(1, 8):
        total = total + dot(context[table[p]], outward[p])
    start = jnp.concatenate([share[h] for h in range(8)], axis=1).astype(F32)
    middle = (start + total).astype(BF).astype(F32)
    average = jnp.mean(middle, axis=1, keepdims=True)
    centred = middle - average
    spread = jnp.mean(centred * centred, axis=1, keepdims=True)
    normed = (centred * lax.rsqrt(spread + EPSILON) * gain[...]).astype(BF)
    for c in groups[1]:
        c.wait()
    hidden = [gelu(dot(normed, expand[p])).astype(BF) for p in range(8)]
    for c in groups[2]:
        c.wait()
    total = middle
    for p in range(8):
        total = total + dot(hidden[p], shrink[p])
    done = total.astype(BF)
    for h in range(8):
        out[h] = done[:, h * BLOCK : (h + 1) * BLOCK]


def forward(table, parts, context, share, gain):
    rows = share.shape[1]
    width = D // 2
    return pl.pallas_call(
        forward_kernel,
        out_shape=jax.ShapeDtypeStruct((8, rows, BLOCK), BF),
        grid_spec=pltpu.PrefetchScalarGridSpec(
            num_scalar_prefetch=1,
            grid=(1,),
            in_specs=[ANY] * 10
            + [whole((8, rows, BLOCK)), whole((8, rows, BLOCK)), whole((1, D))],
            out_specs=whole((8, rows, BLOCK)),
            scratch_shapes=[
                pltpu.VMEM((8, D, width), BF),
                pltpu.VMEM((8, width, D), BF),
                pltpu.VMEM((8, BLOCK, D), BF),
                pltpu.SemaphoreType.DMA((3, 20)),
            ],
        ),
        compiler_params=params(56),
        cost_estimate=cost(4_800_000_000, 20_000_000, 1_100_000),
        name="forward",
    )(table, *parts, context, share, gain.reshape(1, D))


EACH = 8


def decode_kernel(index, low, own, high, weights, back, sums, source, sems):
    step = pl.program_id(0)
    rim = low.shape[0]

    @pl.when(step == 0)
    def _():
        copies = [
            pltpu.make_async_copy(low, source.at[pl.ds(0, rim)], sems.at[0]),
            pltpu.make_async_copy(own, source.at[pl.ds(rim, own.shape[0])], sems.at[1]),
            pltpu.make_async_copy(
                high, source.at[pl.ds(rim + own.shape[0], rim)], sems.at[2]
            ),
        ]
        for c in copies:
            c.start()
        for c in copies:
            c.wait()

    slots = weights.shape[1]
    ones = jnp.ones((BLOCK, BLOCK), BF)
    row = lax.broadcasted_iota(jnp.int32, (BLOCK, BLOCK), 0)
    column = lax.broadcasted_iota(jnp.int32, (BLOCK, BLOCK), 1)
    made = []
    for b in range(EACH):
        left = jnp.concatenate([weights[b, k] for k in range(slots)], axis=1)
        right = jnp.concatenate(
            [source[index[step * EACH + b, k]] for k in range(slots)], axis=0
        )
        made.append(dot(left, right))
        back[b * BLOCK : (b + 1) * BLOCK] = made[b]
    kinds = [m.astype(BF) for m in made] + [(m * m).astype(BF) for m in made]
    held = [
        jnp.sum(jnp.where(row == column, dot(k, ones), 0.0), axis=0, keepdims=True)
        for k in kinds
    ]
    sums[0] = jnp.concatenate(held, axis=0).astype(BF)


def decode(index, low, own, high, weights):
    count, slots = weights.shape[:2]
    blocks = own.shape[0]
    rim = low.shape[0]
    steps = count // EACH
    return pl.pallas_call(
        decode_kernel,
        out_shape=(
            jax.ShapeDtypeStruct((count * BLOCK, BLOCK), F32),
            jax.ShapeDtypeStruct((steps, 2 * EACH, BLOCK), BF),
        ),
        grid_spec=pltpu.PrefetchScalarGridSpec(
            num_scalar_prefetch=1,
            grid=(steps,),
            in_specs=[
                ANY,
                ANY,
                ANY,
                pl.BlockSpec((EACH, slots, BLOCK, BLOCK), lambda i, _: (i, 0, 0, 0)),
            ],
            out_specs=(
                pl.BlockSpec((EACH * BLOCK, BLOCK), lambda i, _: (i, 0)),
                pl.BlockSpec((1, 2 * EACH, BLOCK), lambda i, _: (i, 0, 0)),
            ),
            scratch_shapes=[
                pltpu.VMEM((blocks + 2 * rim, BLOCK, BLOCK), BF),
                pltpu.SemaphoreType.DMA((3,)),
            ],
        ),
        compiler_params=params(56),
        cost_estimate=cost(540_000_000, 10_000_000),
        name="decode",
    )(index, low, own, high, weights)


def finish_kernel(sums, back, state, gain, out):
    count = sums.shape[0]
    stats = jnp.concatenate([sums[h, 0] for h in range(count)], axis=0)
    depth = count * 2 * EACH
    row = lax.broadcasted_iota(jnp.int32, (depth, 2 * EACH * BLOCK), 0)
    column = lax.broadcasted_iota(jnp.int32, (depth, 2 * EACH * BLOCK), 1)
    pick = jnp.where((row % (2 * EACH)) == (column // BLOCK), 1.0, 0.0).astype(BF)
    spread = lax.dot_general(stats, pick, TN, preferred_element_type=F32) * (1.0 / D)
    for b in range(EACH):
        rows = slice(b * BLOCK, (b + 1) * BLOCK)
        average = spread[:, b * BLOCK : (b + 1) * BLOCK]
        squares = spread[:, (EACH + b) * BLOCK : (EACH + b + 1) * BLOCK]
        scale = lax.rsqrt(squares - average * average + EPSILON) * gain[...]
        out[rows] = (
            state[rows].astype(F32) + (back[rows] - average) * scale
        ).astype(BF)


def finish(sums, back, state, gain):
    rows = state.shape[0]
    tile = pl.BlockSpec((EACH * BLOCK, BLOCK), lambda i: (i, 0))
    return pl.pallas_call(
        finish_kernel,
        out_shape=jax.ShapeDtypeStruct((rows, BLOCK), BF),
        grid_spec=pl.GridSpec(
            grid=(rows // (EACH * BLOCK),),
            in_specs=[
                pl.BlockSpec((sums.shape[0], 1, 2 * EACH, BLOCK), lambda i: (0, i, 0, 0)),
                tile,
                tile,
                pl.BlockSpec((1, BLOCK), lambda i: (0, 0)),
            ],
            out_specs=tile,
        ),
        compiler_params=params(32),
        cost_estimate=cost(540_000_000, 8_000_000),
        name="finish",
    )(sums, back, state, gain.reshape(1, BLOCK))


def shifted(value, by):
    return lax.ppermute(value, "seq", [(i, i + by) for i in range(16) if 0 <= i + by < 16])


def among(value, axis, count, to):
    return lax.ppermute(value, axis, [(i, to(i)) for i in range(count)])


def head_ring(x):
    half = x.shape[0] // 2
    north = lambda v: among(v, "head", 8, lambda i: (i + 2) % 8)
    south = lambda v: among(v, "head", 8, lambda i: (i - 2) % 8)
    y = among(x, "head", 8, lambda i: i ^ 1)
    xa, xb = north(x), south(x)
    ya, yb = north(y), south(y)
    return (
        x, y, xa, ya, xb, yb,
        north(xa[:half]), south(xb[half:]), north(ya[:half]), south(yb[half:]),
    )


def along_z(i, by):
    return (i // 8) * 8 + ((i // 2 + by) % 4) * 2 + i % 2


UP = lambda v: among(v, "seq", 16, lambda i: along_z(i, 1))
DOWN = lambda v: among(v, "seq", 16, lambda i: along_z(i, -1))
TWIN = lambda v: among(v, "seq", 16, lambda i: i ^ 1)
NORTH = lambda v: among(v, "head", 8, lambda i: (i + 2) % 8)
SOUTH = lambda v: among(v, "head", 8, lambda i: (i - 2) % 8)


def weights_of_heads(packed):
    x = jnp.stack([packed, among(packed, "head", 8, lambda i: i ^ 1)])
    a, b = NORTH(x), SOUTH(x)
    far = jnp.stack([NORTH(a[0]), SOUTH(b[1])])
    return x, a, b, far


def on_device(
    grid_state,
    encode_index,
    encode_weights,
    first_gain,
    project_in,
    project_out,
    second_gain,
    expand_weights,
    shrink_weights,
    decode_index,
    decode_weights,
    output_gain,
):
    band = lax.axis_index("seq")
    bands = lax.axis_size("seq")
    me = lax.axis_index("head")
    mesh_blocks = encode_weights.shape[0]
    mesh_rows = mesh_blocks * BLOCK
    grid_blocks = grid_state.shape[0] // BLOCK
    rim = mesh_blocks * BLOCK
    last, first, expand, shrink, outward, inward = lax.optimization_barrier(
        (
            grid_state[-rim:], grid_state[:rim],
            expand_weights, shrink_weights, project_out, project_in,
        )
    )
    low = shifted(last, 1)
    high = shifted(first, -1)

    position = band % 8
    packed = pack_weights(position, expand, shrink, outward)
    inward = inward.reshape(8, BLOCK, 3 * BLOCK)
    low, high, inward = lax.optimization_barrier((low, high, inward))
    mine = jnp.concatenate(weights_of_heads(packed), axis=0)

    mesh_start = encode(
        encode_index - (band * grid_blocks - mesh_blocks), low, grid_state, high, encode_weights
    )
    slots = head_ring(mesh_start)
    partner = me ^ 1
    order = jnp.stack(
        [me, partner] + [(v + by) % 8 for by in (6, 2, 4) for v in (me, partner)]
    ).astype(jnp.int32)
    queries, keys_values, share = project(order, slots, first_gain, inward)
    below = shifted(keys_values[mesh_rows - REACH :], 1)
    above = shifted(keys_values[:REACH], -1)
    up, down = UP(mine), DOWN(mine)
    far_up, far_down = UP(up[:4]), DOWN(down[4:])
    edges = jnp.stack([band == 0, band == bands - 1]).astype(jnp.int32)
    context = attend(edges, queries, below, keys_values, above)
    context, far_up, far_down = lax.optimization_barrier((context, far_up, far_down))
    here = [mine, up, down, far_up, far_down]
    parts = here + [TWIN(v) for v in here]
    context = lax.all_to_all(
        context.reshape(8, mesh_rows // 8, BLOCK), "head", 0, 0, tiled=True
    )
    z, core = position // 2, position % 2
    places = [
        ((z + by) % 4) * 2 + side
        for side in (core, 1 - core)
        for by in (0, 3, 1, 2, 2)
    ]
    table = jnp.concatenate([order, jnp.stack(places).astype(jnp.int32)])
    mesh_end = forward(table, parts, context, share, second_gain)
    mesh_end = lax.all_to_all(mesh_end, "head", 0, 0, tiled=True)
    mesh_end = mesh_end.reshape(mesh_blocks, BLOCK, BLOCK)
    edge = mesh_blocks // 2
    back, sums = decode(
        decode_index - (band * mesh_blocks - edge),
        shifted(mesh_end[-edge:], 1),
        mesh_end,
        shifted(mesh_end[:edge], -1),
        decode_weights,
    )
    sums = lax.all_to_all(
        jnp.broadcast_to(sums, (8, *sums.shape)), "head", 0, 0, tiled=True
    )
    return finish(sums, back, grid_state, output_gain)


def solution(mesh):
    in_specs = (
        P("seq", "head"),
        P("seq", None),
        P("seq", None, None, None),
        P(),
        P(None, None, "head"),
        P("head", None),
        P(),
        P(None, "head"),
        P("head", None),
        P("seq", None),
        P("seq", None, None, None),
        P("head"),
    )
    return jax.shard_map(
        on_device, mesh=mesh, in_specs=in_specs, out_specs=P("seq", "head"), check_vma=False
    )
```

```python
import jax
import jax.numpy as jnp
from jax import lax
from jax.experimental import pallas as pl
from jax.experimental.pallas import tpu as pltpu
from jax.sharding import PartitionSpec as P

D = 1024
HEAD_DIM = 64
WINDOW = 1120
REACH = 1152
BLOCK = 128
EPSILON = 1e-05
LOG2E = 1.4426950408889634
BF = jnp.bfloat16
F32 = jnp.float32
NT = (((1,), (1,)), ((), ()))
TN = (((0,), (0,)), ((), ()))
MIB = 1 << 20


def params(mib):
    return pltpu.CompilerParams(
        dimension_semantics=("arbitrary",), vmem_limit_bytes=mib * MIB
    )


def dot(a, b):
    return jnp.dot(a, b, preferred_element_type=F32)


def cost(flops, moved, powers=0):
    return pl.CostEstimate(flops=flops, bytes_accessed=moved, transcendentals=powers)


ANY = pl.BlockSpec(memory_space=pl.ANY)
FAR = pl.BlockSpec(memory_space=pltpu.HBM)


def whole(shape):
    return pl.BlockSpec(shape, lambda i, *_: (0,) * len(shape))


def pieces_of(ref, target, start, count, sems, first):
    length = ref.shape[0] // count
    return [
        pltpu.make_async_copy(
            ref.at[pl.ds(n * length, length)],
            target.at[pl.ds(start + n * length, length)],
            sems.at[first + n],
        )
        for n in range(count)
    ]


def encode_kernel(index, low, own, high, weights, out, source, held, made, sems):
    rim, slots = low.shape[0], weights.shape[1]
    ahead = pieces_of(low, source, 0, 2, sems, 0)
    ahead += pieces_of(own, source, rim, 4, sems, 2)
    ahead += pieces_of(high, source, rim + own.shape[0], 2, sems, 6)
    count = weights.shape[0]
    blocks = pieces_of(weights, held, 0, count, sems, 8)
    back = pieces_of(made, out, 0, 4, sems, 8 + count)
    for c in ahead + blocks:
        c.start()
    for c in ahead:
        c.wait()
    for b in range(count):
        blocks[b].wait()
        left = jnp.concatenate([held[b, k] for k in range(slots)], axis=1)
        right = jnp.concatenate([source[index[b, k]] for k in range(slots)], axis=0)
        made[b * BLOCK : (b + 1) * BLOCK] = dot(left, right).astype(BF)
        if (b + 1) % (count // 4) == 0:
            back[b // (count // 4)].start()
    for c in back:
        c.wait()


def encode(index, low, own, high, weights):
    count, slots = weights.shape[:2]
    blocks = own.shape[0] // BLOCK
    rim = low.shape[0] // BLOCK
    shaped = [v.reshape(-1, BLOCK, BLOCK) for v in (low, own, high)]
    return pl.pallas_call(
        encode_kernel,
        out_shape=jax.ShapeDtypeStruct((count * BLOCK, BLOCK), BF),
        grid_spec=pltpu.PrefetchScalarGridSpec(
            num_scalar_prefetch=1,
            grid=(1,),
            in_specs=[ANY, FAR, ANY, FAR],
            out_specs=ANY,
            scratch_shapes=[
                pltpu.VMEM((blocks + 2 * rim, BLOCK, BLOCK), BF),
                pltpu.VMEM((count, slots, BLOCK, BLOCK), BF),
                pltpu.VMEM((count * BLOCK, BLOCK), BF),
                pltpu.SemaphoreType.DMA((12 + count,)),
            ],
        ),
        compiler_params=params(56),
        cost_estimate=cost(540_000_000, 8_000_000),
        name="encode",
    )(index, *shaped, weights)


def project_kernel(
    order, s0, s1, s2, s3, s4, s5, lo6, hi6, lo7, hi7, gain, wq, wk, wv,
    queries, keys_values, share, ordered,
):
    step = pl.program_id(0)
    half = pl.num_programs(0) // 2

    @pl.when(step == 0)
    def _():
        for p in range(8):
            ordered[p * BLOCK : (p + 1) * BLOCK] = jnp.concatenate(
                [w[order[p]] for w in (wq, wk, wv)], axis=1
            )

    early = step < half
    raw = [s[...] for s in (s0, s1, s2, s3, s4, s5)]
    raw.append(jnp.where(early, lo6[...], hi6[...]))
    raw.append(jnp.where(early, lo7[...], hi7[...]))

    @pl.when(step == order[0])
    def _():
        for p in range(8):
            share[order[p]] = raw[p]

    pieces = [r.astype(F32) for r in raw]
    total = pieces[0]
    for x in pieces[1:]:
        total = total + x
    average = jnp.sum(total, axis=1, keepdims=True) * (1.0 / D)
    pieces = [x - average for x in pieces]
    total = pieces[0] * pieces[0]
    for x in pieces[1:]:
        total = total + x * x
    spread = lax.rsqrt(jnp.sum(total, axis=1, keepdims=True) * (1.0 / D) + EPSILON)
    normed = jnp.concatenate(
        [(x * spread * gain[order[p]]).astype(BF) for p, x in enumerate(pieces)], axis=1
    )
    made = dot(normed, ordered[...]).astype(BF)
    queries[...] = (made[:, :BLOCK].astype(F32) * (HEAD_DIM**-0.5)).astype(BF)
    keys_values[...] = made[:, BLOCK:]


def project(order, slots, gain, weights):
    rows = slots[0].shape[0]
    tile = rows // 8
    full = pl.BlockSpec((tile, BLOCK), lambda i, _: (i, 0))
    early = pl.BlockSpec((tile, BLOCK), lambda i, _: (jnp.minimum(i, 3), 0))
    late = pl.BlockSpec((tile, BLOCK), lambda i, _: (jnp.maximum(i - 4, 0), 0))
    return pl.pallas_call(
        project_kernel,
        out_shape=(
            jax.ShapeDtypeStruct((rows, BLOCK), BF),
            jax.ShapeDtypeStruct((rows, 2 * BLOCK), BF),
            jax.ShapeDtypeStruct((8, tile, BLOCK), BF),
        ),
        grid_spec=pltpu.PrefetchScalarGridSpec(
            num_scalar_prefetch=1,
            grid=(8,),
            in_specs=[full] * 6
            + [early, late, early, late]
            + [whole((8, 1, BLOCK))]
            + [whole((8, BLOCK, BLOCK))] * 3,
            out_specs=(
                full,
                pl.BlockSpec((tile, 2 * BLOCK), lambda i, _: (i, 0)),
                whole((8, tile, BLOCK)),
            ),
            scratch_shapes=[pltpu.VMEM((D, 3 * BLOCK), BF)],
        ),
        compiler_params=params(56),
        cost_estimate=cost(1_600_000_000, 7_000_000),
        name="project",
    )(order, *slots, gain.reshape(8, 1, BLOCK), *weights)


TILE = 256
SPAN = TILE + 2 * REACH
CHUNKS = SPAN // TILE


def attend_kernel(edges, queries, low, own, high, out, keys, values, scores, sems):
    step = pl.program_id(0)
    rows = own.shape[0]

    @pl.when(step == 0)
    def _():
        copies = []
        for n, (part, start) in enumerate(
            ((low, 0), (own, REACH), (high, REACH + rows))
        ):
            for m, target in enumerate((keys, values)):
                copies.append(
                    pltpu.make_async_copy(
                        part.at[:, pl.ds(m * BLOCK, BLOCK)],
                        target.at[pl.ds(start, part.shape[0]), pl.ds(0, BLOCK)],
                        sems.at[2 * n + m],
                    )
                )
        for c in copies:
            c.start()
        values[:, BLOCK:] = jnp.ones((values.shape[0], BLOCK), BF)
        first = lax.broadcasted_iota(jnp.int32, (keys.shape[0], BLOCK), 1) == 0
        row = lax.broadcasted_iota(jnp.int32, (keys.shape[0], BLOCK), 0)
        absent = ((row < REACH) & (edges[0] == 1)) | (
            (row >= REACH + rows) & (edges[1] == 1)
        )
        keys[:, BLOCK:] = jnp.where(first & absent, -1e30, 0.0).astype(BF)
        for c in copies:
            c.wait()

    lane = lax.broadcasted_iota(jnp.int32, (TILE, BLOCK), 1)
    q = queries[...]
    zero = jnp.zeros_like(q)
    both = jnp.concatenate(
        [jnp.where(lane < HEAD_DIM, q, zero), jnp.where(lane < HEAD_DIM, zero, q)], axis=0
    )
    mark = jnp.where(
        lax.broadcasted_iota(jnp.int32, (2 * TILE, BLOCK), 1) == 0, 1.0, 0.0
    ).astype(BF)
    stacked = jnp.concatenate([both, mark], axis=1)
    row = lax.broadcasted_iota(jnp.int32, (2 * TILE, TILE), 0) & (TILE - 1)
    column = lax.broadcasted_iota(jnp.int32, (2 * TILE, TILE), 1)
    highest = jnp.full((2 * TILE, BLOCK), -1e30, F32)
    for c in range(CHUNKS):
        part = keys[pl.ds(pl.multiple_of((step + c) * TILE, TILE), TILE)]
        s = lax.dot_general(stacked, part, NT, preferred_element_type=F32)
        least = c * TILE - REACH
        gap = column - row + least
        if least - TILE < -WINDOW:
            s = jnp.where(gap >= -WINDOW, s, -1e30)
        if least + TILE > WINDOW:
            s = jnp.where(gap <= WINDOW, s, -1e30)
        scores[:, c * TILE : (c + 1) * TILE] = s
        highest = jnp.maximum(highest, jnp.maximum(s[:, :BLOCK], s[:, BLOCK:]))
    peak = jnp.max(highest, axis=1, keepdims=True) * LOG2E
    total = jnp.zeros((2 * TILE, 2 * BLOCK), F32)
    for c in range(CHUNKS):
        part = values[pl.ds(pl.multiple_of((step + c) * TILE, TILE), TILE)]
        powers = jnp.exp2(scores[:, c * TILE : (c + 1) * TILE] * LOG2E - peak)
        total = total + dot(powers.astype(BF), part)
    made = total[:, :BLOCK] / total[:, BLOCK:]
    out[...] = jnp.where(lane < HEAD_DIM, made[:TILE], made[TILE:]).astype(BF)


def attend(edges, queries, low, own, high):
    rows = own.shape[0]
    return pl.pallas_call(
        attend_kernel,
        out_shape=jax.ShapeDtypeStruct((rows, BLOCK), BF),
        grid_spec=pltpu.PrefetchScalarGridSpec(
            num_scalar_prefetch=1,
            grid=(rows // TILE,),
            in_specs=[pl.BlockSpec((TILE, BLOCK), lambda i, _: (i, 0)), ANY, ANY, ANY],
            out_specs=pl.BlockSpec((TILE, BLOCK), lambda i, _: (i, 0)),
            scratch_shapes=[
                pltpu.VMEM((rows + 2 * REACH, 2 * BLOCK), BF),
                pltpu.VMEM((rows + 2 * REACH, 2 * BLOCK), BF),
                pltpu.VMEM((2 * TILE, SPAN), F32),
                pltpu.SemaphoreType.DMA((6,)),
            ],
        ),
        compiler_params=params(56),
        cost_estimate=cost(10_700_000_000, 4_000_000, 10_500_000),
        name="attend",
    )(edges, queries, low, own, high)


ROWS_E = 64
ROWS_S = 64
ROWS_P = 16
PACK = ROWS_E + ROWS_S + ROWS_P


def pack_weights(position, expand, shrink, project_out):
    part = lax.dynamic_slice_in_dim(expand, position * 2 * ROWS_E, 2 * ROWS_E, 0)
    return jnp.concatenate(
        [
            jnp.concatenate([part[:ROWS_E], part[ROWS_E:]], axis=1),
            lax.dynamic_slice_in_dim(shrink, position * ROWS_S, ROWS_S, 0),
            lax.dynamic_slice_in_dim(project_out, position * ROWS_P, ROWS_P, 0),
        ],
        axis=0,
    )


def gelu(v):
    return 0.5 * v * (1.0 + jnp.tanh(0.7978845608028654 * (v + 0.044715 * v * v * v)))


def forward_kernel(table, *refs):
    parts = refs[:10]
    context, share, gain, out, expand, shrink, outward, sems = refs[10:]
    groups = ([], [], [])
    width = expand.shape[2]
    for n, part in enumerate(parts):
        first = 4 if n % 5 == 4 else 0
        count = part.shape[0]
        where = table[8 + n]
        slots = pl.ds(first, count)

        def copy(group, source, target):
            groups[group].append(
                pltpu.make_async_copy(source, target, sems.at[group, len(groups[group])])
            )

        copy(
            0,
            part.at[:, pl.ds(ROWS_E + ROWS_S, ROWS_P), :],
            outward.at[slots, pl.ds(pl.multiple_of(where * ROWS_P, ROWS_P), ROWS_P), :],
        )
        for side in range(2):
            copy(
                1,
                part.at[:, pl.ds(0, ROWS_E), pl.ds(side * width, width)],
                expand.at[
                    slots,
                    pl.ds(pl.multiple_of(where * 2 * ROWS_E + side * ROWS_E, ROWS_E), ROWS_E),
                    :,
                ],
            )
        copy(
            2,
            part.at[:, pl.ds(ROWS_E, ROWS_S), :],
            shrink.at[slots, pl.ds(pl.multiple_of(where * ROWS_S, ROWS_S), ROWS_S), :],
        )
    for group in groups:
        for c in group:
            c.start()
    for c in groups[0]:
        c.wait()
    total = dot(context[table[0]], outward[0])
    for p in range(1, 8):
        total = total + dot(context[table[p]], outward[p])
    start = jnp.concatenate([share[h] for h in range(8)], axis=1).astype(F32)
    middle = (start + total).astype(BF).astype(F32)
    average = jnp.mean(middle, axis=1, keepdims=True)
    centred = middle - average
    spread = jnp.mean(centred * centred, axis=1, keepdims=True)
    normed = (centred * lax.rsqrt(spread + EPSILON) * gain[...]).astype(BF)
    for c in groups[1]:
        c.wait()
    hidden = [gelu(dot(normed, expand[p])).astype(BF) for p in range(8)]
    for c in groups[2]:
        c.wait()
    total = middle
    for p in range(8):
        total = total + dot(hidden[p], shrink[p])
    done = total.astype(BF)
    for h in range(8):
        out[h] = done[:, h * BLOCK : (h + 1) * BLOCK]


def forward(table, parts, context, share, gain):
    rows = share.shape[1]
    width = D // 2
    return pl.pallas_call(
        forward_kernel,
        out_shape=jax.ShapeDtypeStruct((8, rows, BLOCK), BF),
        grid_spec=pltpu.PrefetchScalarGridSpec(
            num_scalar_prefetch=1,
            grid=(1,),
            in_specs=[ANY] * 10
            + [whole((8, rows, BLOCK)), whole((8, rows, BLOCK)), whole((1, D))],
            out_specs=whole((8, rows, BLOCK)),
            scratch_shapes=[
                pltpu.VMEM((8, D, width), BF),
                pltpu.VMEM((8, width, D), BF),
                pltpu.VMEM((8, BLOCK, D), BF),
                pltpu.SemaphoreType.DMA((3, 20)),
            ],
        ),
        compiler_params=params(56),
        cost_estimate=cost(4_800_000_000, 20_000_000, 1_100_000),
        name="forward",
    )(table, *parts, context, share, gain.reshape(1, D))


EACH = 8


def decode_kernel(index, low, own, high, weights, back, sums, source, held, kept, sems):
    rim, slots = low.shape[0], weights.shape[1]
    steps = weights.shape[0] // EACH
    ahead = pieces_of(low, source, 0, 1, sems, 0)
    ahead += pieces_of(own, source, rim, 2, sems, 1)
    ahead += pieces_of(high, source, rim + own.shape[0], 1, sems, 3)
    blocks = pieces_of(weights, held, 0, 2 * steps, sems, 4)
    done = pieces_of(kept, back, 0, steps, sems, 4 + 2 * steps)
    for c in ahead + blocks:
        c.start()
    for c in ahead:
        c.wait()
    ones = jnp.ones((BLOCK, BLOCK), BF)
    row = lax.broadcasted_iota(jnp.int32, (BLOCK, BLOCK), 0)
    column = lax.broadcasted_iota(jnp.int32, (BLOCK, BLOCK), 1)
    for step in range(steps):
        blocks[2 * step].wait()
        blocks[2 * step + 1].wait()
        kinds = []
        for b in range(step * EACH, (step + 1) * EACH):
            left = jnp.concatenate([held[b, k] for k in range(slots)], axis=1)
            right = jnp.concatenate([source[index[b, k]] for k in range(slots)], axis=0)
            made = dot(left, right)
            plain = made.astype(BF)
            kept[b * BLOCK : (b + 1) * BLOCK] = plain
            kinds.append((plain, (made * made).astype(BF)))
        done[step].start()
        held_sums = [
            jnp.sum(jnp.where(row == column, dot(kinds[b][n], ones), 0.0), axis=0, keepdims=True)
            for n in range(2)
            for b in range(EACH)
        ]
        sums[step] = jnp.concatenate(held_sums, axis=0).astype(BF)
    for c in done:
        c.wait()


def decode(index, low, own, high, weights):
    count, slots = weights.shape[:2]
    blocks = own.shape[0]
    rim = low.shape[0]
    steps = count // EACH
    return pl.pallas_call(
        decode_kernel,
        out_shape=(
            jax.ShapeDtypeStruct((count * BLOCK, BLOCK), BF),
            jax.ShapeDtypeStruct((steps, 2 * EACH, BLOCK), BF),
        ),
        grid_spec=pltpu.PrefetchScalarGridSpec(
            num_scalar_prefetch=1,
            grid=(1,),
            in_specs=[ANY, ANY, ANY, FAR],
            out_specs=(ANY, whole((steps, 2 * EACH, BLOCK))),
            scratch_shapes=[
                pltpu.VMEM((blocks + 2 * rim, BLOCK, BLOCK), BF),
                pltpu.VMEM((count, slots, BLOCK, BLOCK), BF),
                pltpu.VMEM((count * BLOCK, BLOCK), BF),
                pltpu.SemaphoreType.DMA((4 + 3 * steps,)),
            ],
        ),
        compiler_params=params(56),
        cost_estimate=cost(540_000_000, 10_000_000),
        name="decode",
    )(index, low, own, high, weights)


def finish_kernel(sums, back, state, gain, out, stats, kept, base, made, sems):
    steps = sums.shape[1]
    count = sums.shape[0]
    first = pieces_of(sums, stats, 0, count, sems, 0)
    backs = pieces_of(back, kept, 0, steps, sems, count)
    states = pieces_of(state, base, 0, steps, sems, count + steps)
    outs = pieces_of(made, out, 0, steps, sems, count + 2 * steps)
    for c in first:
        c.start()
    for a, b in zip(backs, states):
        a.start()
        b.start()
    depth = count * 2 * EACH
    row = lax.broadcasted_iota(jnp.int32, (depth, 2 * EACH * BLOCK), 0)
    column = lax.broadcasted_iota(jnp.int32, (depth, 2 * EACH * BLOCK), 1)
    pick = jnp.where((row % (2 * EACH)) == (column // BLOCK), 1.0 / D, 0.0).astype(BF)
    for c in first:
        c.wait()
    for step in range(steps):
        parts = jnp.concatenate([stats[h, step] for h in range(count)], axis=0)
        spread = lax.dot_general(parts, pick, TN, preferred_element_type=F32)
        backs[step].wait()
        states[step].wait()
        for b in range(EACH):
            at = (step * EACH + b) * BLOCK
            average = spread[:, b * BLOCK : (b + 1) * BLOCK]
            squares = spread[:, (EACH + b) * BLOCK : (EACH + b + 1) * BLOCK]
            scale = lax.rsqrt(squares - average * average + EPSILON) * gain[...]
            made[at : at + BLOCK] = (
                base[at : at + BLOCK].astype(F32)
                + (kept[at : at + BLOCK].astype(F32) - average) * scale
            ).astype(BF)
        outs[step].start()
    for c in outs:
        c.wait()


def finish(sums, back, state, gain):
    rows = state.shape[0]
    count, steps = sums.shape[:2]
    return pl.pallas_call(
        finish_kernel,
        out_shape=jax.ShapeDtypeStruct((rows, BLOCK), BF),
        grid_spec=pl.GridSpec(
            grid=(1,),
            in_specs=[ANY, ANY, FAR, whole((1, BLOCK))],
            out_specs=ANY,
            scratch_shapes=[
                pltpu.VMEM(sums.shape, BF),
                pltpu.VMEM((rows, BLOCK), BF),
                pltpu.VMEM((rows, BLOCK), BF),
                pltpu.VMEM((rows, BLOCK), BF),
                pltpu.SemaphoreType.DMA((count + 3 * steps,)),
            ],
        ),
        compiler_params=params(24),
        cost_estimate=cost(540_000_000, 8_000_000),
        name="finish",
    )(sums, back, state, gain.reshape(1, BLOCK))


def shifted(value, by):
    return lax.ppermute(value, "seq", [(i, i + by) for i in range(16) if 0 <= i + by < 16])


def among(value, axis, count, to):
    return lax.ppermute(value, axis, [(i, to(i)) for i in range(count)])


def along_z(i, by):
    return (i // 8) * 8 + ((i // 2 + by) % 4) * 2 + i % 2


UP = lambda v: among(v, "seq", 16, lambda i: along_z(i, 1))
DOWN = lambda v: among(v, "seq", 16, lambda i: along_z(i, -1))
TWIN = lambda v: among(v, "seq", 16, lambda i: i ^ 1)
NORTH = lambda v: among(v, "head", 8, lambda i: (i + 2) % 8)
SOUTH = lambda v: among(v, "head", 8, lambda i: (i - 2) % 8)


OVER = lambda v: among(v, "head", 8, lambda i: i ^ 1)


def on_device(
    grid_state,
    encode_index,
    encode_weights,
    first_gain,
    project_in,
    project_out,
    second_gain,
    expand_weights,
    shrink_weights,
    decode_index,
    decode_weights,
    output_gain,
):
    band = lax.axis_index("seq")
    bands = lax.axis_size("seq")
    me = lax.axis_index("head")
    mesh_blocks = encode_weights.shape[0]
    mesh_rows = mesh_blocks * BLOCK
    grid_blocks = grid_state.shape[0] // BLOCK
    rim = mesh_blocks * BLOCK
    last, first, expand, shrink, outward, inward = lax.optimization_barrier(
        (
            grid_state[-rim:], grid_state[:rim],
            expand_weights, shrink_weights, project_out, project_in,
        )
    )
    low = shifted(last, 1)
    high = shifted(first, -1)

    position = band % 8
    packed = pack_weights(position, expand, shrink, outward)
    inward = [inward[:, j, :].reshape(8, BLOCK, BLOCK) for j in range(3)]
    packed = jnp.stack([packed, OVER(packed)])
    low, high, packed, *inward = lax.optimization_barrier((low, high, packed, *inward))
    packed_a, packed_b = NORTH(packed), SOUTH(packed)

    mesh_start = encode(
        encode_index - (band * grid_blocks - mesh_blocks), low, grid_state, high, encode_weights
    )
    half = mesh_rows // 2
    x = mesh_start
    y, xa, xb = OVER(x), NORTH(x), SOUTH(x)
    xc, xd = NORTH(xa[:half]), SOUTH(xb[half:])
    ya, yb = NORTH(y), SOUTH(y)
    yc, yd = OVER(xc), OVER(xd)
    slots = (x, y, xa, ya, xb, yb, xc, xd, yc, yd)
    far = jnp.stack([NORTH(packed_a[0]), SOUTH(packed_b[1])])
    mine = jnp.concatenate([packed, packed_a, packed_b, far], axis=0)
    mine, *_ = lax.optimization_barrier((mine, ya, yb, xc, xd))
    partner = me ^ 1
    order = jnp.stack(
        [me, partner] + [(v + by) % 8 for by in (6, 2, 4) for v in (me, partner)]
    ).astype(jnp.int32)
    queries, keys_values, share = project(order, slots, first_gain, inward)
    below = shifted(keys_values[mesh_rows - REACH :], 1)
    above = shifted(keys_values[:REACH], -1)
    up, down = UP(mine), DOWN(mine)
    far_up, far_down = UP(up[:4]), DOWN(down[4:])
    edges = jnp.stack([band == 0, band == bands - 1]).astype(jnp.int32)
    context = attend(edges, queries, below, keys_values, above)
    context, far_up, far_down = lax.optimization_barrier((context, far_up, far_down))
    here = [mine, up, down, far_up, far_down]
    parts = here + [TWIN(v) for v in here]
    context = lax.all_to_all(
        context.reshape(8, mesh_rows // 8, BLOCK), "head", 0, 0, tiled=True
    )
    z, core = position // 2, position % 2
    places = [
        ((z + by) % 4) * 2 + side
        for side in (core, 1 - core)
        for by in (0, 3, 1, 2, 2)
    ]
    table = jnp.concatenate([order, jnp.stack(places).astype(jnp.int32)])
    mesh_end = forward(table, parts, context, share, second_gain)
    mesh_end = lax.all_to_all(mesh_end, "head", 0, 0, tiled=True)
    mesh_end = mesh_end.reshape(mesh_blocks, BLOCK, BLOCK)
    edge = mesh_blocks // 2
    back, sums = decode(
        decode_index - (band * mesh_blocks - edge),
        shifted(mesh_end[-edge:], 1),
        mesh_end,
        shifted(mesh_end[:edge], -1),
        decode_weights,
    )
    sums = lax.all_to_all(
        jnp.broadcast_to(sums, (8, *sums.shape)), "head", 0, 0, tiled=True
    )
    return finish(sums, back, grid_state, output_gain)


def solution(mesh):
    in_specs = (
        P("seq", "head"),
        P("seq", None),
        P("seq", None, None, None),
        P(),
        P(None, None, "head"),
        P("head", None),
        P(),
        P(None, "head"),
        P("head", None),
        P("seq", None),
        P("seq", None, None, None),
        P("head"),
    )
    return jax.shard_map(
        on_device, mesh=mesh, in_specs=in_specs, out_specs=P("seq", "head"), check_vma=False
    )
```

```python
import jax
import jax.numpy as jnp
from jax import lax
from jax.experimental import pallas as pl
from jax.experimental.pallas import tpu as pltpu
from jax.sharding import PartitionSpec as P

D = 1024
HEAD_DIM = 64
WINDOW = 1120
REACH = 1152
BLOCK = 128
EPSILON = 1e-05
LOG2E = 1.4426950408889634
BF = jnp.bfloat16
F32 = jnp.float32
NT = (((1,), (1,)), ((), ()))
TN = (((0,), (0,)), ((), ()))
MIB = 1 << 20


def params(mib):
    return pltpu.CompilerParams(
        dimension_semantics=("arbitrary",), vmem_limit_bytes=mib * MIB
    )


def dot(a, b):
    return jnp.dot(a, b, preferred_element_type=F32)


def cost(flops, moved, powers=0):
    return pl.CostEstimate(flops=flops, bytes_accessed=moved, transcendentals=powers)


ANY = pl.BlockSpec(memory_space=pl.ANY)
FAR = pl.BlockSpec(memory_space=pltpu.HBM)


def whole(shape):
    return pl.BlockSpec(shape, lambda i, *_: (0,) * len(shape))


def pieces_of(ref, target, start, count, sems, first):
    length = ref.shape[0] // count
    return [
        pltpu.make_async_copy(
            ref.at[pl.ds(n * length, length)],
            target.at[pl.ds(start + n * length, length)],
            sems.at[first + n],
        )
        for n in range(count)
    ]


def encode_kernel(index, low, own, high, weights, out, source, held, made, sems):
    rim, slots = low.shape[0], weights.shape[1]
    ahead = pieces_of(low, source, 0, 2, sems, 0)
    ahead += pieces_of(own, source, rim, 4, sems, 2)
    ahead += pieces_of(high, source, rim + own.shape[0], 2, sems, 6)
    count = weights.shape[0]
    blocks = pieces_of(weights, held, 0, count, sems, 8)
    back = pieces_of(made, out, 0, 4, sems, 8 + count)
    for c in ahead + blocks:
        c.start()
    for c in ahead:
        c.wait()
    for b in range(count):
        blocks[b].wait()
        left = jnp.concatenate([held[b, k] for k in range(slots)], axis=1)
        right = jnp.concatenate([source[index[b, k]] for k in range(slots)], axis=0)
        made[b * BLOCK : (b + 1) * BLOCK] = dot(left, right).astype(BF)
        if (b + 1) % (count // 4) == 0:
            back[b // (count // 4)].start()
    for c in back:
        c.wait()


def encode(index, low, own, high, weights):
    count, slots = weights.shape[:2]
    blocks = own.shape[0] // BLOCK
    rim = low.shape[0] // BLOCK
    shaped = [v.reshape(-1, BLOCK, BLOCK) for v in (low, own, high)]
    return pl.pallas_call(
        encode_kernel,
        out_shape=jax.ShapeDtypeStruct((count * BLOCK, BLOCK), BF),
        grid_spec=pltpu.PrefetchScalarGridSpec(
            num_scalar_prefetch=1,
            grid=(1,),
            in_specs=[ANY, FAR, ANY, FAR],
            out_specs=ANY,
            scratch_shapes=[
                pltpu.VMEM((blocks + 2 * rim, BLOCK, BLOCK), BF),
                pltpu.VMEM((count, slots, BLOCK, BLOCK), BF),
                pltpu.VMEM((count * BLOCK, BLOCK), BF),
                pltpu.SemaphoreType.DMA((12 + count,)),
            ],
        ),
        compiler_params=params(56),
        cost_estimate=cost(540_000_000, 8_000_000),
        name="encode",
    )(index, *shaped, weights)


def project_kernel(
    order, s0, s1, s2, s3, s4, s5, lo6, hi6, lo7, hi7, gain, wq, wk, wv,
    queries, keys_values, share, ordered,
):
    step = pl.program_id(0)
    half = pl.num_programs(0) // 2

    @pl.when(step == 0)
    def _():
        for p in range(8):
            ordered[p * BLOCK : (p + 1) * BLOCK] = jnp.concatenate(
                [w[order[p]] for w in (wq, wk, wv)], axis=1
            )

    early = step < half
    raw = [s[...] for s in (s0, s1, s2, s3, s4, s5)]
    raw.append(jnp.where(early, lo6[...], hi6[...]))
    raw.append(jnp.where(early, lo7[...], hi7[...]))

    tile = share.shape[1]
    per = raw[0].shape[0] // tile
    for n in range(per):

        @pl.when(order[0] == step * per + n)
        def _():
            for p in range(8):
                share[order[p]] = raw[p][n * tile : (n + 1) * tile]

    pieces = [r.astype(F32) for r in raw]
    total = pieces[0]
    for x in pieces[1:]:
        total = total + x
    average = jnp.sum(total, axis=1, keepdims=True) * (1.0 / D)
    pieces = [x - average for x in pieces]
    total = pieces[0] * pieces[0]
    for x in pieces[1:]:
        total = total + x * x
    spread = lax.rsqrt(jnp.sum(total, axis=1, keepdims=True) * (1.0 / D) + EPSILON)
    normed = jnp.concatenate(
        [(x * spread * gain[order[p]]).astype(BF) for p, x in enumerate(pieces)], axis=1
    )
    made = dot(normed, ordered[...]).astype(BF)
    queries[...] = (made[:, :BLOCK].astype(F32) * (HEAD_DIM**-0.5)).astype(BF)
    keys_values[...] = made[:, BLOCK:]


def project(order, slots, gain, weights):
    rows = slots[0].shape[0]
    tile, steps = rows // 8, 4
    each = rows // steps
    full = pl.BlockSpec((each, BLOCK), lambda i, _: (i, 0))
    early = pl.BlockSpec((each, BLOCK), lambda i, _: (jnp.minimum(i, steps // 2 - 1), 0))
    late = pl.BlockSpec((each, BLOCK), lambda i, _: (jnp.maximum(i - steps // 2, 0), 0))
    return pl.pallas_call(
        project_kernel,
        out_shape=(
            jax.ShapeDtypeStruct((rows, BLOCK), BF),
            jax.ShapeDtypeStruct((rows, 2 * BLOCK), BF),
            jax.ShapeDtypeStruct((8, tile, BLOCK), BF),
        ),
        grid_spec=pltpu.PrefetchScalarGridSpec(
            num_scalar_prefetch=1,
            grid=(steps,),
            in_specs=[full] * 6
            + [early, late, early, late]
            + [whole((8, 1, BLOCK))]
            + [whole((8, BLOCK, BLOCK))] * 3,
            out_specs=(
                full,
                pl.BlockSpec((each, 2 * BLOCK), lambda i, _: (i, 0)),
                whole((8, tile, BLOCK)),
            ),
            scratch_shapes=[pltpu.VMEM((D, 3 * BLOCK), BF)],
        ),
        compiler_params=params(56),
        cost_estimate=cost(1_600_000_000, 7_000_000),
        name="project",
    )(order, *slots, gain.reshape(8, 1, BLOCK), *weights)


TILE = 256
SPAN = TILE + 2 * REACH
CHUNKS = SPAN // TILE


def attend_kernel(edges, queries, low, own, high, out, keys, values, scores, sems):
    step = pl.program_id(0)
    rows = own.shape[0]

    @pl.when(step == 0)
    def _():
        copies = []
        for n, (part, start) in enumerate(
            ((low, 0), (own, REACH), (high, REACH + rows))
        ):
            for m, target in enumerate((keys, values)):
                copies.append(
                    pltpu.make_async_copy(
                        part.at[:, pl.ds(m * BLOCK, BLOCK)],
                        target.at[pl.ds(start, part.shape[0]), pl.ds(0, BLOCK)],
                        sems.at[2 * n + m],
                    )
                )
        for c in copies:
            c.start()
        values[:, BLOCK:] = jnp.ones((values.shape[0], BLOCK), BF)
        first = lax.broadcasted_iota(jnp.int32, (keys.shape[0], BLOCK), 1) == 0
        row = lax.broadcasted_iota(jnp.int32, (keys.shape[0], BLOCK), 0)
        absent = ((row < REACH) & (edges[0] == 1)) | (
            (row >= REACH + rows) & (edges[1] == 1)
        )
        keys[:, BLOCK:] = jnp.where(first & absent, -1e30, 0.0).astype(BF)
        for c in copies:
            c.wait()

    lane = lax.broadcasted_iota(jnp.int32, (TILE, BLOCK), 1)
    q = queries[...]
    zero = jnp.zeros_like(q)
    both = jnp.concatenate(
        [jnp.where(lane < HEAD_DIM, q, zero), jnp.where(lane < HEAD_DIM, zero, q)], axis=0
    )
    mark = jnp.where(
        lax.broadcasted_iota(jnp.int32, (2 * TILE, BLOCK), 1) == 0, 1.0, 0.0
    ).astype(BF)
    stacked = jnp.concatenate([both, mark], axis=1)
    row = lax.broadcasted_iota(jnp.int32, (2 * TILE, TILE), 0) & (TILE - 1)
    column = lax.broadcasted_iota(jnp.int32, (2 * TILE, TILE), 1)
    highest = jnp.full((2 * TILE, BLOCK), -1e30, F32)
    for c in range(CHUNKS):
        part = keys[pl.ds(pl.multiple_of((step + c) * TILE, TILE), TILE)]
        s = lax.dot_general(stacked, part, NT, preferred_element_type=F32)
        least = c * TILE - REACH
        gap = column - row + least
        if least - TILE < -WINDOW:
            s = jnp.where(gap >= -WINDOW, s, -1e30)
        if least + TILE > WINDOW:
            s = jnp.where(gap <= WINDOW, s, -1e30)
        scores[:, c * TILE : (c + 1) * TILE] = s
        highest = jnp.maximum(highest, jnp.maximum(s[:, :BLOCK], s[:, BLOCK:]))
    peak = jnp.max(highest, axis=1, keepdims=True) * LOG2E
    total = jnp.zeros((2 * TILE, 2 * BLOCK), F32)
    for c in range(CHUNKS):
        part = values[pl.ds(pl.multiple_of((step + c) * TILE, TILE), TILE)]
        powers = jnp.exp2(scores[:, c * TILE : (c + 1) * TILE] * LOG2E - peak)
        total = total + dot(powers.astype(BF), part)
    made = total[:, :BLOCK] / total[:, BLOCK:]
    out[...] = jnp.where(lane < HEAD_DIM, made[:TILE], made[TILE:]).astype(BF)


def attend(edges, queries, low, own, high):
    rows = own.shape[0]
    return pl.pallas_call(
        attend_kernel,
        out_shape=jax.ShapeDtypeStruct((rows, BLOCK), BF),
        grid_spec=pltpu.PrefetchScalarGridSpec(
            num_scalar_prefetch=1,
            grid=(rows // TILE,),
            in_specs=[pl.BlockSpec((TILE, BLOCK), lambda i, _: (i, 0)), ANY, ANY, ANY],
            out_specs=pl.BlockSpec((TILE, BLOCK), lambda i, _: (i, 0)),
            scratch_shapes=[
                pltpu.VMEM((rows + 2 * REACH, 2 * BLOCK), BF),
                pltpu.VMEM((rows + 2 * REACH, 2 * BLOCK), BF),
                pltpu.VMEM((2 * TILE, SPAN), F32),
                pltpu.SemaphoreType.DMA((6,)),
            ],
        ),
        compiler_params=params(56),
        cost_estimate=cost(10_700_000_000, 4_000_000, 10_500_000),
        name="attend",
    )(edges, queries, low, own, high)


ROWS_E = 64
ROWS_S = 64
ROWS_P = 16
PACK = ROWS_E + ROWS_S + ROWS_P


def pack_weights(position, expand, shrink, project_out):
    part = lax.dynamic_slice_in_dim(expand, position * 2 * ROWS_E, 2 * ROWS_E, 0)
    return jnp.concatenate(
        [
            jnp.concatenate([part[:ROWS_E], part[ROWS_E:]], axis=1),
            lax.dynamic_slice_in_dim(shrink, position * ROWS_S, ROWS_S, 0),
            lax.dynamic_slice_in_dim(project_out, position * ROWS_P, ROWS_P, 0),
        ],
        axis=0,
    )


def gelu(v):
    return 0.5 * v * (1.0 + jnp.tanh(0.7978845608028654 * (v + 0.044715 * v * v * v)))


def forward_kernel(table, *refs):
    parts = refs[:8]
    context, share, gain, out, expand, shrink, outward, sems = refs[8:]
    groups = ([], [], [])
    width = expand.shape[3]
    for n, part in enumerate(parts):
        where = table[8 + n]
        for side in range(2):
            slot = 1 - side if n % 4 == 3 else side

            def copy(group, source, target):
                groups[group].append(
                    pltpu.make_async_copy(source, target, sems.at[group, len(groups[group])])
                )

            copy(
                0,
                part.at[:, side, pl.ds(ROWS_E + ROWS_S, ROWS_P), :],
                outward.at[
                    :, slot, pl.ds(pl.multiple_of(where * ROWS_P, ROWS_P), ROWS_P), :
                ],
            )
            for piece in range(2):
                copy(
                    1,
                    part.at[:, side, pl.ds(0, ROWS_E), pl.ds(piece * width, width)],
                    expand.at[
                        :,
                        slot,
                        pl.ds(
                            pl.multiple_of(where * 2 * ROWS_E + piece * ROWS_E, ROWS_E), ROWS_E
                        ),
                        :,
                    ],
                )
            copy(
                2,
                part.at[:, side, pl.ds(ROWS_E, ROWS_S), :],
                shrink.at[:, slot, pl.ds(pl.multiple_of(where * ROWS_S, ROWS_S), ROWS_S), :],
            )
    for group in groups:
        for c in group:
            c.start()
    for c in groups[0]:
        c.wait()
    total = dot(context[table[0]], outward[0, 0])
    for p in range(1, 8):
        total = total + dot(context[table[p]], outward[p // 2, p % 2])
    start = jnp.concatenate([share[h] for h in range(8)], axis=1).astype(F32)
    middle = (start + total).astype(BF).astype(F32)
    average = jnp.mean(middle, axis=1, keepdims=True)
    centred = middle - average
    spread = jnp.mean(centred * centred, axis=1, keepdims=True)
    normed = (centred * lax.rsqrt(spread + EPSILON) * gain[...]).astype(BF)
    for c in groups[1]:
        c.wait()
    hidden = [gelu(dot(normed, expand[p // 2, p % 2])).astype(BF) for p in range(8)]
    for c in groups[2]:
        c.wait()
    total = middle
    for p in range(8):
        total = total + dot(hidden[p], shrink[p // 2, p % 2])
    done = total.astype(BF)
    for h in range(8):
        out[h] = done[:, h * BLOCK : (h + 1) * BLOCK]


def forward(table, parts, context, share, gain):
    rows = share.shape[1]
    width = D // 2
    return pl.pallas_call(
        forward_kernel,
        out_shape=jax.ShapeDtypeStruct((8, rows, BLOCK), BF),
        grid_spec=pltpu.PrefetchScalarGridSpec(
            num_scalar_prefetch=1,
            grid=(1,),
            in_specs=[ANY] * 8
            + [whole((8, rows, BLOCK)), whole((8, rows, BLOCK)), whole((1, D))],
            out_specs=whole((8, rows, BLOCK)),
            scratch_shapes=[
                pltpu.VMEM((4, 2, D, width), BF),
                pltpu.VMEM((4, 2, width, D), BF),
                pltpu.VMEM((4, 2, BLOCK, D), BF),
                pltpu.SemaphoreType.DMA((3, 32)),
            ],
        ),
        compiler_params=params(56),
        cost_estimate=cost(4_800_000_000, 20_000_000, 1_100_000),
        name="forward",
    )(table, *parts, context, share, gain.reshape(1, D))


EACH = 8


def decode_kernel(index, low, own, high, weights, back, sums, source, held, kept, sems):
    rim, slots = low.shape[0], weights.shape[1]
    steps = weights.shape[0] // EACH
    ahead = pieces_of(low, source, 0, 1, sems, 0)
    ahead += pieces_of(own, source, rim, 2, sems, 1)
    ahead += pieces_of(high, source, rim + own.shape[0], 1, sems, 3)
    blocks = pieces_of(weights, held, 0, 2 * steps, sems, 4)
    done = pieces_of(kept, back, 0, steps, sems, 4 + 2 * steps)
    for c in ahead + blocks:
        c.start()
    for c in ahead:
        c.wait()
    ones = jnp.ones((BLOCK, BLOCK), BF)
    row = lax.broadcasted_iota(jnp.int32, (BLOCK, BLOCK), 0)
    column = lax.broadcasted_iota(jnp.int32, (BLOCK, BLOCK), 1)
    for step in range(steps):
        blocks[2 * step].wait()
        blocks[2 * step + 1].wait()
        kinds = []
        for b in range(step * EACH, (step + 1) * EACH):
            left = jnp.concatenate([held[b, k] for k in range(slots)], axis=1)
            right = jnp.concatenate([source[index[b, k]] for k in range(slots)], axis=0)
            made = dot(left, right)
            plain = made.astype(BF)
            kept[b * BLOCK : (b + 1) * BLOCK] = plain
            kinds.append((plain, (made * made).astype(BF)))
        done[step].start()
        held_sums = [
            jnp.sum(jnp.where(row == column, dot(kinds[b][n], ones), 0.0), axis=0, keepdims=True)
            for n in range(2)
            for b in range(EACH)
        ]
        sums[step] = jnp.concatenate(held_sums, axis=0).astype(BF)
    for c in done:
        c.wait()


def decode(index, low, own, high, weights):
    count, slots = weights.shape[:2]
    blocks = own.shape[0]
    rim = low.shape[0]
    steps = count // EACH
    return pl.pallas_call(
        decode_kernel,
        out_shape=(
            jax.ShapeDtypeStruct((count * BLOCK, BLOCK), BF),
            jax.ShapeDtypeStruct((steps, 2 * EACH, BLOCK), BF),
        ),
        grid_spec=pltpu.PrefetchScalarGridSpec(
            num_scalar_prefetch=1,
            grid=(1,),
            in_specs=[ANY, ANY, ANY, FAR],
            out_specs=(ANY, whole((steps, 2 * EACH, BLOCK))),
            scratch_shapes=[
                pltpu.VMEM((blocks + 2 * rim, BLOCK, BLOCK), BF),
                pltpu.VMEM((count, slots, BLOCK, BLOCK), BF),
                pltpu.VMEM((count * BLOCK, BLOCK), BF),
                pltpu.SemaphoreType.DMA((4 + 3 * steps,)),
            ],
        ),
        compiler_params=params(56),
        cost_estimate=cost(540_000_000, 10_000_000),
        name="decode",
    )(index, low, own, high, weights)


def finish_kernel(sums, back, state, gain, out, stats, kept, base, made, sems):
    steps = sums.shape[1]
    count = sums.shape[0]
    first = pieces_of(sums, stats, 0, count, sems, 0)
    backs = pieces_of(back, kept, 0, steps, sems, count)
    states = pieces_of(state, base, 0, steps, sems, count + steps)
    outs = pieces_of(made, out, 0, steps, sems, count + 2 * steps)
    for c in first:
        c.start()
    for a, b in zip(backs, states):
        a.start()
        b.start()
    depth = count * 2 * EACH
    row = lax.broadcasted_iota(jnp.int32, (depth, 2 * EACH * BLOCK), 0)
    column = lax.broadcasted_iota(jnp.int32, (depth, 2 * EACH * BLOCK), 1)
    pick = jnp.where((row % (2 * EACH)) == (column // BLOCK), 1.0 / D, 0.0).astype(BF)
    for c in first:
        c.wait()
    for step in range(steps):
        parts = jnp.concatenate([stats[h, step] for h in range(count)], axis=0)
        spread = lax.dot_general(parts, pick, TN, preferred_element_type=F32)
        backs[step].wait()
        states[step].wait()
        for b in range(EACH):
            at = (step * EACH + b) * BLOCK
            average = spread[:, b * BLOCK : (b + 1) * BLOCK]
            squares = spread[:, (EACH + b) * BLOCK : (EACH + b + 1) * BLOCK]
            scale = lax.rsqrt(squares - average * average + EPSILON) * gain[...]
            made[at : at + BLOCK] = (
                base[at : at + BLOCK].astype(F32)
                + (kept[at : at + BLOCK].astype(F32) - average) * scale
            ).astype(BF)
        outs[step].start()
    for c in outs:
        c.wait()


def finish(sums, back, state, gain):
    rows = state.shape[0]
    count, steps = sums.shape[:2]
    return pl.pallas_call(
        finish_kernel,
        out_shape=jax.ShapeDtypeStruct((rows, BLOCK), BF),
        grid_spec=pl.GridSpec(
            grid=(1,),
            in_specs=[ANY, ANY, FAR, whole((1, BLOCK))],
            out_specs=ANY,
            scratch_shapes=[
                pltpu.VMEM(sums.shape, BF),
                pltpu.VMEM((rows, BLOCK), BF),
                pltpu.VMEM((rows, BLOCK), BF),
                pltpu.VMEM((rows, BLOCK), BF),
                pltpu.SemaphoreType.DMA((count + 3 * steps,)),
            ],
        ),
        compiler_params=params(24),
        cost_estimate=cost(540_000_000, 8_000_000),
        name="finish",
    )(sums, back, state, gain.reshape(1, BLOCK))


def shifted(value, by):
    return lax.ppermute(value, "seq", [(i, i + by) for i in range(16) if 0 <= i + by < 16])


def among(value, axis, count, to):
    return lax.ppermute(value, axis, [(i, to(i)) for i in range(count)])


def along_z(i, by):
    return (i // 8) * 8 + ((i // 2 + by) % 4) * 2 + i % 2


UP = lambda v: among(v, "seq", 16, lambda i: along_z(i, 1))
DOWN = lambda v: among(v, "seq", 16, lambda i: along_z(i, -1))
ACROSS = lambda v: among(v, ("seq", "head"), 128, lambda i: i ^ 65)
TWIN = lambda v: among(v, "seq", 16, lambda i: i ^ 1)
NORTH = lambda v: among(v, "head", 8, lambda i: (i + 2) % 8)
SOUTH = lambda v: among(v, "head", 8, lambda i: (i - 2) % 8)
OVER = lambda v: among(v, "head", 8, lambda i: i ^ 1)


def on_device(
    grid_state,
    encode_index,
    encode_weights,
    first_gain,
    project_in,
    project_out,
    second_gain,
    expand_weights,
    shrink_weights,
    decode_index,
    decode_weights,
    output_gain,
):
    band = lax.axis_index("seq")
    bands = lax.axis_size("seq")
    me = lax.axis_index("head")
    mesh_blocks = encode_weights.shape[0]
    mesh_rows = mesh_blocks * BLOCK
    grid_blocks = grid_state.shape[0] // BLOCK
    rim = mesh_blocks * BLOCK
    last, first, expand, shrink, outward, inward = lax.optimization_barrier(
        (
            grid_state[-rim:], grid_state[:rim],
            expand_weights, shrink_weights, project_out, project_in,
        )
    )
    low = shifted(last, 1)
    high = shifted(first, -1)

    core, place = band % 2, (band // 2 + 2 * (band // 8)) % 4
    position = place * 2 + core
    packed = pack_weights(position, expand, shrink, outward)
    inward = [inward[:, j, :].reshape(8, BLOCK, BLOCK) for j in range(3)]
    packed = jnp.stack([packed, OVER(packed)])
    low, high, *inward = lax.optimization_barrier((low, high, *inward))
    packed_a, packed_b = NORTH(packed), SOUTH(packed)

    mesh_start = encode(
        encode_index - (band * grid_blocks - mesh_blocks), low, grid_state, high, encode_weights
    )
    half = mesh_rows // 2
    x = mesh_start
    y, xa, xb = lax.optimization_barrier((OVER(x), NORTH(x), SOUTH(x)))
    xc, xd = NORTH(xa[:half]), SOUTH(xb[half:])
    ya, yb = NORTH(y), SOUTH(y)
    yc, yd = OVER(xc), OVER(xd)
    slots = (x, y, xa, ya, xb, yb, xc, xd, yc, yd)
    packed_a, packed_b, *_ = lax.optimization_barrier(
        (packed_a, packed_b, xc, xd, ya, yb)
    )
    far = jnp.stack([NORTH(packed_a[0]), SOUTH(packed_b[1])])
    mine = jnp.stack([packed, packed_a, packed_b, far])
    partner = me ^ 1
    order = jnp.stack(
        [me, partner] + [(v + by) % 8 for by in (6, 2, 4) for v in (me, partner)]
    ).astype(jnp.int32)
    queries, keys_values, share = project(order, slots, first_gain, inward)
    below = shifted(keys_values[mesh_rows - REACH :], 1)
    above = shifted(keys_values[:REACH], -1)
    others = [UP(mine), DOWN(mine), ACROSS(mine)]
    edges = jnp.stack([band == 0, band == bands - 1]).astype(jnp.int32)
    context = attend(edges, queries, below, keys_values, above)
    context, *others = lax.optimization_barrier((context, *others))
    here = [mine, *others]
    parts = here + [TWIN(v) for v in here]
    context = lax.all_to_all(
        context.reshape(8, mesh_rows // 8, BLOCK), "head", 0, 0, tiled=True
    )
    places = [
        ((place + by) % 4) * 2 + side for side in (core, 1 - core) for by in (0, 3, 1, 2)
    ]
    table = jnp.concatenate([order, jnp.stack(places).astype(jnp.int32)])
    mesh_end = forward(table, parts, context, share, second_gain)
    mesh_end = lax.all_to_all(mesh_end, "head", 0, 0, tiled=True)
    mesh_end = mesh_end.reshape(mesh_blocks, BLOCK, BLOCK)
    edge = mesh_blocks // 2
    back, sums = decode(
        decode_index - (band * mesh_blocks - edge),
        shifted(mesh_end[-edge:], 1),
        mesh_end,
        shifted(mesh_end[:edge], -1),
        decode_weights,
    )
    sums = lax.all_to_all(
        jnp.broadcast_to(sums, (8, *sums.shape)), "head", 0, 0, tiled=True
    )
    return finish(sums, back, grid_state, output_gain)


def solution(mesh):
    in_specs = (
        P("seq", "head"),
        P("seq", None),
        P("seq", None, None, None),
        P(),
        P(None, None, "head"),
        P("head", None),
        P(),
        P(None, "head"),
        P("head", None),
        P("seq", None),
        P("seq", None, None, None),
        P("head"),
    )
    return jax.shard_map(
        on_device, mesh=mesh, in_specs=in_specs, out_specs=P("seq", "head"), check_vma=False
    )
```

```python
import jax
import jax.numpy as jnp
from jax import lax
from jax.experimental import pallas as pl
from jax.experimental.pallas import tpu as pltpu
from jax.sharding import PartitionSpec as P

D = 1024
HEAD_DIM = 64
WINDOW = 1120
REACH = 1152
BLOCK = 128
EPSILON = 1e-05
LOG2E = 1.4426950408889634
BF = jnp.bfloat16
F32 = jnp.float32
NT = (((1,), (1,)), ((), ()))
TN = (((0,), (0,)), ((), ()))
MIB = 1 << 20


def params(mib):
    return pltpu.CompilerParams(
        dimension_semantics=("arbitrary",), vmem_limit_bytes=mib * MIB
    )


def dot(a, b):
    return jnp.dot(a, b, preferred_element_type=F32)


def cost(flops, moved, powers=0):
    return pl.CostEstimate(flops=flops, bytes_accessed=moved, transcendentals=powers)


ANY = pl.BlockSpec(memory_space=pl.ANY)
FAR = pl.BlockSpec(memory_space=pltpu.HBM)


def whole(shape):
    return pl.BlockSpec(shape, lambda i, *_: (0,) * len(shape))


def pieces_of(ref, target, start, count, sems, first):
    length = ref.shape[0] // count
    return [
        pltpu.make_async_copy(
            ref.at[pl.ds(n * length, length)],
            target.at[pl.ds(start + n * length, length)],
            sems.at[first + n],
        )
        for n in range(count)
    ]


def encode_kernel(index, low, own, high, weights, out, source, held, made, sems):
    rim, slots = low.shape[0], weights.shape[1]
    ahead = pieces_of(low, source, 0, 2, sems, 0)
    ahead += pieces_of(own, source, rim, 4, sems, 2)
    ahead += pieces_of(high, source, rim + own.shape[0], 2, sems, 6)
    count = weights.shape[0]
    blocks = pieces_of(weights, held, 0, count, sems, 8)
    back = pieces_of(made, out, 0, 4, sems, 8 + count)
    for c in ahead + blocks:
        c.start()
    for c in ahead:
        c.wait()
    for b in range(count):
        blocks[b].wait()
        left = jnp.concatenate([held[b, k] for k in range(slots)], axis=1)
        right = jnp.concatenate([source[index[b, k]] for k in range(slots)], axis=0)
        made[b * BLOCK : (b + 1) * BLOCK] = dot(left, right).astype(BF)
        if (b + 1) % (count // 4) == 0:
            back[b // (count // 4)].start()
    for c in back:
        c.wait()


def encode(index, low, own, high, weights):
    count, slots = weights.shape[:2]
    blocks = own.shape[0] // BLOCK
    rim = low.shape[0] // BLOCK
    shaped = [v.reshape(-1, BLOCK, BLOCK) for v in (low, own, high)]
    return pl.pallas_call(
        encode_kernel,
        out_shape=jax.ShapeDtypeStruct((count * BLOCK, BLOCK), BF),
        grid_spec=pltpu.PrefetchScalarGridSpec(
            num_scalar_prefetch=1,
            grid=(1,),
            in_specs=[ANY, FAR, ANY, FAR],
            out_specs=ANY,
            scratch_shapes=[
                pltpu.VMEM((blocks + 2 * rim, BLOCK, BLOCK), BF),
                pltpu.VMEM((count, slots, BLOCK, BLOCK), BF),
                pltpu.VMEM((count * BLOCK, BLOCK), BF),
                pltpu.SemaphoreType.DMA((12 + count,)),
            ],
        ),
        compiler_params=params(56),
        cost_estimate=cost(540_000_000, 8_000_000),
        name="encode",
    )(index, *shaped, weights)


def project_kernel(
    order, s0, s1, s2, s3, s4, s5, s6, s7, gain, wq, wk, wv,
    queries, keys_values, share, ordered,
):
    step = pl.program_id(0)

    @pl.when(step == 0)
    def _():
        for p in range(8):
            ordered[p * BLOCK : (p + 1) * BLOCK] = jnp.concatenate(
                [w[order[p]] for w in (wq, wk, wv)], axis=1
            )

    raw = [s[...] for s in (s0, s1, s2, s3, s4, s5, s6, s7)]

    tile = share.shape[1]
    per = raw[0].shape[0] // tile
    for n in range(per):

        @pl.when(order[0] == step * per + n)
        def _():
            for p in range(8):
                share[order[p]] = raw[p][n * tile : (n + 1) * tile]

    pieces = [r.astype(F32) for r in raw]
    total = pieces[0]
    for x in pieces[1:]:
        total = total + x
    average = jnp.sum(total, axis=1, keepdims=True) * (1.0 / D)
    pieces = [x - average for x in pieces]
    total = pieces[0] * pieces[0]
    for x in pieces[1:]:
        total = total + x * x
    spread = lax.rsqrt(jnp.sum(total, axis=1, keepdims=True) * (1.0 / D) + EPSILON)
    normed = jnp.concatenate(
        [(x * spread * gain[order[p]]).astype(BF) for p, x in enumerate(pieces)], axis=1
    )
    made = dot(normed, ordered[...]).astype(BF)
    queries[...] = (made[:, :BLOCK].astype(F32) * (HEAD_DIM**-0.5)).astype(BF)
    keys_values[...] = made[:, BLOCK:]


def project(order, slots, gain, weights):
    rows = slots[0].shape[0]
    tile, steps = rows // 8, 4
    each = rows // steps
    full = pl.BlockSpec((each, BLOCK), lambda i, _: (i, 0))
    second = pl.BlockSpec((each, BLOCK), lambda i, _: (i + steps // 2, 0))
    return pl.pallas_call(
        project_kernel,
        out_shape=(
            jax.ShapeDtypeStruct((rows, BLOCK), BF),
            jax.ShapeDtypeStruct((rows, 2 * BLOCK), BF),
            jax.ShapeDtypeStruct((8, tile, BLOCK), BF),
        ),
        grid_spec=pltpu.PrefetchScalarGridSpec(
            num_scalar_prefetch=1,
            grid=(steps,),
            in_specs=[full, full, full, second, full, second, full, full]
            + [whole((8, 1, BLOCK))]
            + [whole((8, BLOCK, BLOCK))] * 3,
            out_specs=(
                full,
                pl.BlockSpec((each, 2 * BLOCK), lambda i, _: (i, 0)),
                whole((8, tile, BLOCK)),
            ),
            scratch_shapes=[pltpu.VMEM((D, 3 * BLOCK), BF)],
        ),
        compiler_params=params(56),
        name="project",
    )(order, *slots, gain.reshape(8, 1, BLOCK), *weights)


TILE = 256
SPAN = TILE + 2 * REACH
CHUNKS = SPAN // TILE


def attend_kernel(edges, queries, low, own, high, out, keys, values, scores, sems):
    step = pl.program_id(0)
    rows = own.shape[0]

    @pl.when(step == 0)
    def _():
        copies = []
        for n, (part, start) in enumerate(
            ((low, 0), (own, REACH), (high, REACH + rows))
        ):
            for m, target in enumerate((keys, values)):
                copies.append(
                    pltpu.make_async_copy(
                        part.at[:, pl.ds(m * BLOCK, BLOCK)],
                        target.at[pl.ds(start, part.shape[0]), pl.ds(0, BLOCK)],
                        sems.at[2 * n + m],
                    )
                )
        for c in copies:
            c.start()
        values[:, BLOCK:] = jnp.ones((values.shape[0], BLOCK), BF)
        first = lax.broadcasted_iota(jnp.int32, (keys.shape[0], BLOCK), 1) == 0
        row = lax.broadcasted_iota(jnp.int32, (keys.shape[0], BLOCK), 0)
        absent = ((row < REACH) & (edges[0] == 1)) | (
            (row >= REACH + rows) & (edges[1] == 1)
        )
        keys[:, BLOCK:] = jnp.where(first & absent, -1e30, 0.0).astype(BF)
        for c in copies:
            c.wait()

    lane = lax.broadcasted_iota(jnp.int32, (TILE, BLOCK), 1)
    q = queries[...]
    zero = jnp.zeros_like(q)
    both = jnp.concatenate(
        [jnp.where(lane < HEAD_DIM, q, zero), jnp.where(lane < HEAD_DIM, zero, q)], axis=0
    )
    mark = jnp.where(
        lax.broadcasted_iota(jnp.int32, (2 * TILE, BLOCK), 1) == 0, 1.0, 0.0
    ).astype(BF)
    stacked = jnp.concatenate([both, mark], axis=1)
    row = lax.broadcasted_iota(jnp.int32, (2 * TILE, TILE), 0) & (TILE - 1)
    column = lax.broadcasted_iota(jnp.int32, (2 * TILE, TILE), 1)
    highest = jnp.full((2 * TILE, BLOCK), -1e30, F32)
    for c in range(CHUNKS):
        part = keys[pl.ds(pl.multiple_of((step + c) * TILE, TILE), TILE)]
        s = lax.dot_general(stacked, part, NT, preferred_element_type=F32)
        least = c * TILE - REACH
        gap = column - row + least
        if least - TILE < -WINDOW:
            s = jnp.where(gap >= -WINDOW, s, -1e30)
        if least + TILE > WINDOW:
            s = jnp.where(gap <= WINDOW, s, -1e30)
        scores[:, c * TILE : (c + 1) * TILE] = s
        highest = jnp.maximum(highest, jnp.maximum(s[:, :BLOCK], s[:, BLOCK:]))
    peak = jnp.max(highest, axis=1, keepdims=True) * LOG2E
    total = jnp.zeros((2 * TILE, 2 * BLOCK), F32)
    for c in range(CHUNKS):
        part = values[pl.ds(pl.multiple_of((step + c) * TILE, TILE), TILE)]
        powers = jnp.exp2(scores[:, c * TILE : (c + 1) * TILE] * LOG2E - peak)
        total = total + dot(powers.astype(BF), part)
    made = total[:, :BLOCK] / total[:, BLOCK:]
    out[...] = jnp.where(lane < HEAD_DIM, made[:TILE], made[TILE:]).astype(BF)


def attend(edges, queries, low, own, high):
    rows = own.shape[0]
    return pl.pallas_call(
        attend_kernel,
        out_shape=jax.ShapeDtypeStruct((rows, BLOCK), BF),
        grid_spec=pltpu.PrefetchScalarGridSpec(
            num_scalar_prefetch=1,
            grid=(rows // TILE,),
            in_specs=[pl.BlockSpec((TILE, BLOCK), lambda i, _: (i, 0)), ANY, ANY, ANY],
            out_specs=pl.BlockSpec((TILE, BLOCK), lambda i, _: (i, 0)),
            scratch_shapes=[
                pltpu.VMEM((rows + 2 * REACH, 2 * BLOCK), BF),
                pltpu.VMEM((rows + 2 * REACH, 2 * BLOCK), BF),
                pltpu.VMEM((2 * TILE, SPAN), F32),
                pltpu.SemaphoreType.DMA((6,)),
            ],
        ),
        compiler_params=params(56),
        name="attend",
    )(edges, queries, low, own, high)


ROWS_E = 64
ROWS_S = 64
ROWS_P = 16
PACK = ROWS_E + ROWS_S + ROWS_P


def pack_weights(position, expand, shrink, project_out):
    part = lax.dynamic_slice_in_dim(expand, position * 2 * ROWS_E, 2 * ROWS_E, 0)
    return jnp.concatenate(
        [
            jnp.concatenate([part[:ROWS_E], part[ROWS_E:]], axis=1),
            lax.dynamic_slice_in_dim(shrink, position * ROWS_S, ROWS_S, 0),
            lax.dynamic_slice_in_dim(project_out, position * ROWS_P, ROWS_P, 0),
        ],
        axis=0,
    )


def gelu(v):
    return 0.5 * v * (1.0 + jnp.tanh(0.7978845608028654 * (v + 0.044715 * v * v * v)))


def forward_kernel(table, *refs):
    parts = refs[:8]
    context, share, gain, out, expand, shrink, outward, sems = refs[8:]
    groups = ([], [], [])
    width = expand.shape[3]
    for n, part in enumerate(parts):
        where = table[8 + n]
        for side in range(2):
            slot = 1 - side if n % 4 == 3 else side

            def copy(group, source, target):
                groups[group].append(
                    pltpu.make_async_copy(source, target, sems.at[group, len(groups[group])])
                )

            copy(
                0,
                part.at[:, side, pl.ds(ROWS_E + ROWS_S, ROWS_P), :],
                outward.at[
                    :, slot, pl.ds(pl.multiple_of(where * ROWS_P, ROWS_P), ROWS_P), :
                ],
            )
            for piece in range(2):
                copy(
                    1,
                    part.at[:, side, pl.ds(0, ROWS_E), pl.ds(piece * width, width)],
                    expand.at[
                        :,
                        slot,
                        pl.ds(
                            pl.multiple_of(where * 2 * ROWS_E + piece * ROWS_E, ROWS_E), ROWS_E
                        ),
                        :,
                    ],
                )
            copy(
                2,
                part.at[:, side, pl.ds(ROWS_E, ROWS_S), :],
                shrink.at[:, slot, pl.ds(pl.multiple_of(where * ROWS_S, ROWS_S), ROWS_S), :],
            )
    for group in groups:
        for c in group:
            c.start()
    for c in groups[0]:
        c.wait()
    total = dot(context[table[0]], outward[0, 0])
    for p in range(1, 8):
        total = total + dot(context[table[p]], outward[p // 2, p % 2])
    start = jnp.concatenate([share[h] for h in range(8)], axis=1).astype(F32)
    middle = (start + total).astype(BF).astype(F32)
    average = jnp.mean(middle, axis=1, keepdims=True)
    centred = middle - average
    spread = jnp.mean(centred * centred, axis=1, keepdims=True)
    normed = (centred * lax.rsqrt(spread + EPSILON) * gain[...]).astype(BF)
    for c in groups[1]:
        c.wait()
    hidden = [gelu(dot(normed, expand[p // 2, p % 2])).astype(BF) for p in range(8)]
    for c in groups[2]:
        c.wait()
    total = middle
    for p in range(8):
        total = total + dot(hidden[p], shrink[p // 2, p % 2])
    done = total.astype(BF)
    for h in range(8):
        out[h] = done[:, h * BLOCK : (h + 1) * BLOCK]


def forward(table, parts, context, share, gain):
    rows = share.shape[1]
    width = D // 2
    return pl.pallas_call(
        forward_kernel,
        out_shape=jax.ShapeDtypeStruct((8, rows, BLOCK), BF),
        grid_spec=pltpu.PrefetchScalarGridSpec(
            num_scalar_prefetch=1,
            grid=(1,),
            in_specs=[ANY] * 8
            + [whole((8, rows, BLOCK)), whole((8, rows, BLOCK)), whole((1, D))],
            out_specs=whole((8, rows, BLOCK)),
            scratch_shapes=[
                pltpu.VMEM((4, 2, D, width), BF),
                pltpu.VMEM((4, 2, width, D), BF),
                pltpu.VMEM((4, 2, BLOCK, D), BF),
                pltpu.SemaphoreType.DMA((3, 32)),
            ],
        ),
        compiler_params=params(56),
        cost_estimate=cost(4_800_000_000, 20_000_000, 1_100_000),
        name="forward",
    )(table, *parts, context, share, gain.reshape(1, D))


EACH = 8


def decode_kernel(index, low, own, high, weights, back, sums, source, held, kept, sems):
    rim, slots = low.shape[0], weights.shape[1]
    steps = weights.shape[0] // EACH
    ahead = pieces_of(low, source, 0, 1, sems, 0)
    ahead += pieces_of(own, source, rim, 2, sems, 1)
    ahead += pieces_of(high, source, rim + own.shape[0], 1, sems, 3)
    blocks = pieces_of(weights, held, 0, 2 * steps, sems, 4)
    done = pieces_of(kept, back, 0, steps, sems, 4 + 2 * steps)
    for c in ahead + blocks:
        c.start()
    for c in ahead:
        c.wait()
    ones = jnp.ones((BLOCK, BLOCK), BF)
    row = lax.broadcasted_iota(jnp.int32, (BLOCK, BLOCK), 0)
    column = lax.broadcasted_iota(jnp.int32, (BLOCK, BLOCK), 1)
    for step in range(steps):
        blocks[2 * step].wait()
        blocks[2 * step + 1].wait()
        kinds = []
        for b in range(step * EACH, (step + 1) * EACH):
            left = jnp.concatenate([held[b, k] for k in range(slots)], axis=1)
            right = jnp.concatenate([source[index[b, k]] for k in range(slots)], axis=0)
            made = dot(left, right)
            plain = made.astype(BF)
            kept[b * BLOCK : (b + 1) * BLOCK] = plain
            kinds.append((plain, (made * made).astype(BF)))
        done[step].start()
        held_sums = [
            jnp.sum(jnp.where(row == column, dot(kinds[b][n], ones), 0.0), axis=0, keepdims=True)
            for n in range(2)
            for b in range(EACH)
        ]
        sums[step] = jnp.concatenate(held_sums, axis=0).astype(BF)
    for c in done:
        c.wait()


def decode(index, low, own, high, weights):
    count, slots = weights.shape[:2]
    blocks = own.shape[0]
    rim = low.shape[0]
    steps = count // EACH
    return pl.pallas_call(
        decode_kernel,
        out_shape=(
            jax.ShapeDtypeStruct((count * BLOCK, BLOCK), BF),
            jax.ShapeDtypeStruct((steps, 2 * EACH, BLOCK), BF),
        ),
        grid_spec=pltpu.PrefetchScalarGridSpec(
            num_scalar_prefetch=1,
            grid=(1,),
            in_specs=[ANY, ANY, ANY, FAR],
            out_specs=(ANY, whole((steps, 2 * EACH, BLOCK))),
            scratch_shapes=[
                pltpu.VMEM((blocks + 2 * rim, BLOCK, BLOCK), BF),
                pltpu.VMEM((count, slots, BLOCK, BLOCK), BF),
                pltpu.VMEM((count * BLOCK, BLOCK), BF),
                pltpu.SemaphoreType.DMA((4 + 3 * steps,)),
            ],
        ),
        compiler_params=params(56),
        cost_estimate=cost(540_000_000, 10_000_000),
        name="decode",
    )(index, low, own, high, weights)


def finish_kernel(sums, back, state, gain, out, stats, kept, base, made, sems):
    steps = sums.shape[1]
    count = sums.shape[0]
    first = pieces_of(sums, stats, 0, count, sems, 0)
    backs = pieces_of(back, kept, 0, steps, sems, count)
    states = pieces_of(state, base, 0, steps, sems, count + steps)
    outs = pieces_of(made, out, 0, steps, sems, count + 2 * steps)
    for c in first:
        c.start()
    for a, b in zip(backs, states):
        a.start()
        b.start()
    depth = count * 2 * EACH
    row = lax.broadcasted_iota(jnp.int32, (depth, 2 * EACH * BLOCK), 0)
    column = lax.broadcasted_iota(jnp.int32, (depth, 2 * EACH * BLOCK), 1)
    pick = jnp.where((row % (2 * EACH)) == (column // BLOCK), 1.0 / D, 0.0).astype(BF)
    for c in first:
        c.wait()
    for step in range(steps):
        parts = jnp.concatenate([stats[h, step] for h in range(count)], axis=0)
        spread = lax.dot_general(parts, pick, TN, preferred_element_type=F32)
        backs[step].wait()
        states[step].wait()
        for b in range(EACH):
            at = (step * EACH + b) * BLOCK
            average = spread[:, b * BLOCK : (b + 1) * BLOCK]
            squares = spread[:, (EACH + b) * BLOCK : (EACH + b + 1) * BLOCK]
            scale = lax.rsqrt(squares - average * average + EPSILON) * gain[...]
            made[at : at + BLOCK] = (
                base[at : at + BLOCK].astype(F32)
                + (kept[at : at + BLOCK].astype(F32) - average) * scale
            ).astype(BF)
        outs[step].start()
    for c in outs:
        c.wait()


def finish(sums, back, state, gain):
    rows = state.shape[0]
    count, steps = sums.shape[:2]
    return pl.pallas_call(
        finish_kernel,
        out_shape=jax.ShapeDtypeStruct((rows, BLOCK), BF),
        grid_spec=pl.GridSpec(
            grid=(1,),
            in_specs=[ANY, ANY, FAR, whole((1, BLOCK))],
            out_specs=ANY,
            scratch_shapes=[
                pltpu.VMEM(sums.shape, BF),
                pltpu.VMEM((rows, BLOCK), BF),
                pltpu.VMEM((rows, BLOCK), BF),
                pltpu.VMEM((rows, BLOCK), BF),
                pltpu.SemaphoreType.DMA((count + 3 * steps,)),
            ],
        ),
        compiler_params=params(24),
        cost_estimate=cost(540_000_000, 8_000_000),
        name="finish",
    )(sums, back, state, gain.reshape(1, BLOCK))


def shifted(value, by):
    return lax.ppermute(value, "seq", [(i, i + by) for i in range(16) if 0 <= i + by < 16])


def among(value, axis, count, to):
    return lax.ppermute(value, axis, [(i, to(i)) for i in range(count)])


def along_z(i, by):
    return (i // 8) * 8 + ((i // 2 + by) % 4) * 2 + i % 2


UP = lambda v: among(v, "seq", 16, lambda i: along_z(i, 1))
DOWN = lambda v: among(v, "seq", 16, lambda i: along_z(i, -1))
ACROSS = lambda v: among(v, ("seq", "head"), 128, lambda i: i ^ 65)
TWIN = lambda v: among(v, "seq", 16, lambda i: i ^ 1)
NORTH = lambda v: among(v, "head", 8, lambda i: (i + 2) % 8)
SOUTH = lambda v: among(v, "head", 8, lambda i: (i - 2) % 8)
OVER = lambda v: among(v, "head", 8, lambda i: i ^ 1)


def on_device(
    grid_state,
    encode_index,
    encode_weights,
    first_gain,
    project_in,
    project_out,
    second_gain,
    expand_weights,
    shrink_weights,
    decode_index,
    decode_weights,
    output_gain,
):
    band = lax.axis_index("seq")
    bands = lax.axis_size("seq")
    me = lax.axis_index("head")
    mesh_blocks = encode_weights.shape[0]
    mesh_rows = mesh_blocks * BLOCK
    grid_blocks = grid_state.shape[0] // BLOCK
    rim = mesh_blocks * BLOCK
    last, first, expand, shrink, outward, inward = lax.optimization_barrier(
        (
            grid_state[-rim:], grid_state[:rim],
            expand_weights, shrink_weights, project_out, project_in,
        )
    )
    low = shifted(last, 1)
    high = shifted(first, -1)

    core, place = band % 2, (band // 2 + 2 * (band // 8)) % 4
    position = place * 2 + core
    packed = pack_weights(position, expand, shrink, outward)
    inward = [inward[:, j, :].reshape(8, BLOCK, BLOCK) for j in range(3)]
    packed = jnp.stack([packed, OVER(packed)])
    low, high, packed, *inward = lax.optimization_barrier((low, high, packed, *inward))
    packed_a, packed_b = NORTH(packed), SOUTH(packed)

    mesh_start = encode(
        encode_index - (band * grid_blocks - mesh_blocks), low, grid_state, high, encode_weights
    )
    half = mesh_rows // 2
    x, packed_a, packed_b = lax.optimization_barrier((mesh_start, packed_a, packed_b))
    y, xa, xb, far_a, far_b = lax.optimization_barrier(
        (OVER(x), NORTH(x), SOUTH(x), NORTH(packed_a[0]), SOUTH(packed_b[1]))
    )
    mine = jnp.stack([packed, packed_a, packed_b, jnp.stack([far_a, far_b])])
    mine, y, xa, xb = lax.optimization_barrier((mine, y, xa, xb))
    others = [UP(mine), DOWN(mine), ACROSS(mine)]
    from_south = NORTH(jnp.concatenate([xa[:half], y]))
    from_north = SOUTH(jnp.concatenate([xb[half:], y]))
    xc = jnp.concatenate([from_south[:half], from_north[:half]])
    slots = (x, y, xa, from_south, xb, from_north, xc, OVER(xc))
    partner = me ^ 1
    order = jnp.stack(
        [me, partner] + [(v + by) % 8 for by in (6, 2, 4) for v in (me, partner)]
    ).astype(jnp.int32)
    queries, keys_values, share = project(order, slots, first_gain, inward)
    below = shifted(keys_values[mesh_rows - REACH :], 1)
    above = shifted(keys_values[:REACH], -1)
    edges = jnp.stack([band == 0, band == bands - 1]).astype(jnp.int32)
    context = attend(edges, queries, below, keys_values, above)
    context, *here = lax.optimization_barrier((context, mine, *others))
    parts = here + [TWIN(v) for v in here]
    context = lax.all_to_all(
        context.reshape(8, mesh_rows // 8, BLOCK), "head", 0, 0, tiled=True
    )
    places = [
        ((place + by) % 4) * 2 + side for side in (core, 1 - core) for by in (0, 3, 1, 2)
    ]
    table = jnp.concatenate([order, jnp.stack(places).astype(jnp.int32)])
    mesh_end = forward(table, parts, context, share, second_gain)
    mesh_end = lax.all_to_all(mesh_end, "head", 0, 0, tiled=True)
    mesh_end = mesh_end.reshape(mesh_blocks, BLOCK, BLOCK)
    edge = mesh_blocks // 2
    back, sums = decode(
        decode_index - (band * mesh_blocks - edge),
        shifted(mesh_end[-edge:], 1),
        mesh_end,
        shifted(mesh_end[:edge], -1),
        decode_weights,
    )
    sums = lax.all_to_all(
        jnp.broadcast_to(sums, (8, *sums.shape)), "head", 0, 0, tiled=True
    )
    return finish(sums, back, grid_state, output_gain)


def solution(mesh):
    in_specs = (
        P("seq", "head"),
        P("seq", None),
        P("seq", None, None, None),
        P(),
        P(None, None, "head"),
        P("head", None),
        P(),
        P(None, "head"),
        P("head", None),
        P("seq", None),
        P("seq", None, None, None),
        P("head"),
    )
    return jax.shard_map(
        on_device, mesh=mesh, in_specs=in_specs, out_specs=P("seq", "head"), check_vma=False
    )
```

```python
import jax
import jax.numpy as jnp
from jax import lax
from jax.experimental import pallas as pl
from jax.experimental.pallas import tpu as pltpu
from jax.sharding import PartitionSpec as P

D = 1024
HEAD_DIM = 64
WINDOW = 1120
REACH = 1152
BLOCK = 128
EPSILON = 1e-05
LOG2E = 1.4426950408889634
BF = jnp.bfloat16
F32 = jnp.float32
NT = (((1,), (1,)), ((), ()))
TN = (((0,), (0,)), ((), ()))
MIB = 1 << 20


def params(mib):
    return pltpu.CompilerParams(
        dimension_semantics=("arbitrary",), vmem_limit_bytes=mib * MIB
    )


def dot(a, b):
    return jnp.dot(a, b, preferred_element_type=F32)


def cost(flops, moved, powers=0):
    return pl.CostEstimate(flops=flops, bytes_accessed=moved, transcendentals=powers)


ANY = pl.BlockSpec(memory_space=pl.ANY)
FAR = pl.BlockSpec(memory_space=pltpu.HBM)


def whole(shape):
    return pl.BlockSpec(shape, lambda i, *_: (0,) * len(shape))


def pieces_of(ref, target, start, count, sems, first):
    length = ref.shape[0] // count
    return [
        pltpu.make_async_copy(
            ref.at[pl.ds(n * length, length)],
            target.at[pl.ds(start + n * length, length)],
            sems.at[first + n],
        )
        for n in range(count)
    ]


def encode_kernel(index, low, own, high, weights, out, source, held, made, sems):
    rim, slots = low.shape[0], weights.shape[1]
    ahead = pieces_of(low, source, 0, 2, sems, 0)
    ahead += pieces_of(own, source, rim, 4, sems, 2)
    ahead += pieces_of(high, source, rim + own.shape[0], 2, sems, 6)
    count = weights.shape[0]
    blocks = pieces_of(weights, held, 0, count, sems, 8)
    back = pieces_of(made, out, 0, 4, sems, 8 + count)
    for c in ahead + blocks:
        c.start()
    for c in ahead:
        c.wait()
    for b in range(count):
        blocks[b].wait()
        left = jnp.concatenate([held[b, k] for k in range(slots)], axis=1)
        right = jnp.concatenate([source[index[b, k]] for k in range(slots)], axis=0)
        made[b * BLOCK : (b + 1) * BLOCK] = dot(left, right).astype(BF)
        if (b + 1) % (count // 4) == 0:
            back[b // (count // 4)].start()
    for c in back:
        c.wait()


def encode(index, low, own, high, weights):
    count, slots = weights.shape[:2]
    blocks = own.shape[0] // BLOCK
    rim = low.shape[0] // BLOCK
    shaped = [v.reshape(-1, BLOCK, BLOCK) for v in (low, own, high)]
    return pl.pallas_call(
        encode_kernel,
        out_shape=jax.ShapeDtypeStruct((count * BLOCK, BLOCK), BF),
        grid_spec=pltpu.PrefetchScalarGridSpec(
            num_scalar_prefetch=1,
            grid=(1,),
            in_specs=[ANY, FAR, ANY, FAR],
            out_specs=ANY,
            scratch_shapes=[
                pltpu.VMEM((blocks + 2 * rim, BLOCK, BLOCK), BF),
                pltpu.VMEM((count, slots, BLOCK, BLOCK), BF),
                pltpu.VMEM((count * BLOCK, BLOCK), BF),
                pltpu.SemaphoreType.DMA((12 + count,)),
            ],
        ),
        compiler_params=params(56),
        cost_estimate=cost(540_000_000, 8_000_000),
        name="encode",
    )(index, *shaped, weights)


def project_kernel(
    order, s0, s1, s2, s3, s4, s5, s6, s7, gain, wq, wk, wv,
    queries, keys_values, share, ordered,
):
    step = pl.program_id(0)

    @pl.when(step == 0)
    def _():
        for p in range(8):
            ordered[p * BLOCK : (p + 1) * BLOCK] = jnp.concatenate(
                [w[order[p]] for w in (wq, wk, wv)], axis=1
            )

    raw = [s[...] for s in (s0, s1, s2, s3, s4, s5, s6, s7)]

    tile = share.shape[1]
    per = raw[0].shape[0] // tile
    for n in range(per):

        @pl.when(order[0] == step * per + n)
        def _():
            for p in range(8):
                share[order[p]] = raw[p][n * tile : (n + 1) * tile]

    pieces = [r.astype(F32) for r in raw]
    total = pieces[0]
    for x in pieces[1:]:
        total = total + x
    average = jnp.sum(total, axis=1, keepdims=True) * (1.0 / D)
    pieces = [x - average for x in pieces]
    total = pieces[0] * pieces[0]
    for x in pieces[1:]:
        total = total + x * x
    spread = lax.rsqrt(jnp.sum(total, axis=1, keepdims=True) * (1.0 / D) + EPSILON)
    normed = jnp.concatenate(
        [(x * spread * gain[order[p]]).astype(BF) for p, x in enumerate(pieces)], axis=1
    )
    made = dot(normed, ordered[...]).astype(BF)
    queries[...] = (made[:, :BLOCK].astype(F32) * (HEAD_DIM**-0.5)).astype(BF)
    keys_values[...] = made[:, BLOCK:]


def project(order, slots, gain, weights):
    rows = slots[0].shape[0]
    tile, steps = rows // 8, 4
    each = rows // steps
    full = pl.BlockSpec((each, BLOCK), lambda i, _: (i, 0))
    second = pl.BlockSpec((each, BLOCK), lambda i, _: (i + steps // 2, 0))
    return pl.pallas_call(
        project_kernel,
        out_shape=(
            jax.ShapeDtypeStruct((rows, BLOCK), BF),
            jax.ShapeDtypeStruct((rows, 2 * BLOCK), BF),
            jax.ShapeDtypeStruct((8, tile, BLOCK), BF),
        ),
        grid_spec=pltpu.PrefetchScalarGridSpec(
            num_scalar_prefetch=1,
            grid=(steps,),
            in_specs=[full, full, full, second, full, second, full, full]
            + [whole((8, 1, BLOCK))]
            + [whole((8, BLOCK, BLOCK))] * 3,
            out_specs=(
                full,
                pl.BlockSpec((each, 2 * BLOCK), lambda i, _: (i, 0)),
                whole((8, tile, BLOCK)),
            ),
            scratch_shapes=[pltpu.VMEM((D, 3 * BLOCK), BF)],
        ),
        compiler_params=params(56),
        name="project",
    )(order, *slots, gain.reshape(8, 1, BLOCK), *weights)


TILE = 256
SPAN = TILE + 2 * REACH
CHUNKS = SPAN // TILE


def attend_kernel(edges, queries, low, own, high, out, keys, values, scores, sems):
    step = pl.program_id(0)
    rows = own.shape[0]

    @pl.when(step == 0)
    def _():
        copies = []
        for n, (part, start) in enumerate(
            ((low, 0), (own, REACH), (high, REACH + rows))
        ):
            for m, target in enumerate((keys, values)):
                copies.append(
                    pltpu.make_async_copy(
                        part.at[:, pl.ds(m * BLOCK, BLOCK)],
                        target.at[pl.ds(start, part.shape[0]), pl.ds(0, BLOCK)],
                        sems.at[2 * n + m],
                    )
                )
        for c in copies:
            c.start()
        values[:, BLOCK:] = jnp.ones((values.shape[0], BLOCK), BF)
        first = lax.broadcasted_iota(jnp.int32, (keys.shape[0], BLOCK), 1) == 0
        row = lax.broadcasted_iota(jnp.int32, (keys.shape[0], BLOCK), 0)
        absent = ((row < REACH) & (edges[0] == 1)) | (
            (row >= REACH + rows) & (edges[1] == 1)
        )
        keys[:, BLOCK:] = jnp.where(first & absent, -1e30, 0.0).astype(BF)
        for c in copies:
            c.wait()

    lane = lax.broadcasted_iota(jnp.int32, (TILE, BLOCK), 1)
    q = queries[...]
    zero = jnp.zeros_like(q)
    both = jnp.concatenate(
        [jnp.where(lane < HEAD_DIM, q, zero), jnp.where(lane < HEAD_DIM, zero, q)], axis=0
    )
    mark = jnp.where(
        lax.broadcasted_iota(jnp.int32, (2 * TILE, BLOCK), 1) == 0, 1.0, 0.0
    ).astype(BF)
    stacked = jnp.concatenate([both, mark], axis=1)
    row = lax.broadcasted_iota(jnp.int32, (2 * TILE, TILE), 0) & (TILE - 1)
    column = lax.broadcasted_iota(jnp.int32, (2 * TILE, TILE), 1)
    highest = jnp.full((2 * TILE, BLOCK), -1e30, F32)
    for c in range(CHUNKS):
        part = keys[pl.ds(pl.multiple_of((step + c) * TILE, TILE), TILE)]
        s = lax.dot_general(stacked, part, NT, preferred_element_type=F32)
        least = c * TILE - REACH
        gap = column - row + least
        if least - TILE < -WINDOW:
            s = jnp.where(gap >= -WINDOW, s, -1e30)
        if least + TILE > WINDOW:
            s = jnp.where(gap <= WINDOW, s, -1e30)
        scores[:, c * TILE : (c + 1) * TILE] = s
        highest = jnp.maximum(highest, jnp.maximum(s[:, :BLOCK], s[:, BLOCK:]))
    peak = jnp.max(highest, axis=1, keepdims=True) * LOG2E
    total = jnp.zeros((2 * TILE, 2 * BLOCK), F32)
    for c in range(CHUNKS):
        part = values[pl.ds(pl.multiple_of((step + c) * TILE, TILE), TILE)]
        powers = jnp.exp2(scores[:, c * TILE : (c + 1) * TILE] * LOG2E - peak)
        total = total + dot(powers.astype(BF), part)
    made = total[:, :BLOCK] / total[:, BLOCK:]
    out[...] = jnp.where(lane < HEAD_DIM, made[:TILE], made[TILE:]).astype(BF)


def attend(edges, queries, low, own, high):
    rows = own.shape[0]
    return pl.pallas_call(
        attend_kernel,
        out_shape=jax.ShapeDtypeStruct((rows, BLOCK), BF),
        grid_spec=pltpu.PrefetchScalarGridSpec(
            num_scalar_prefetch=1,
            grid=(rows // TILE,),
            in_specs=[pl.BlockSpec((TILE, BLOCK), lambda i, _: (i, 0)), ANY, ANY, ANY],
            out_specs=pl.BlockSpec((TILE, BLOCK), lambda i, _: (i, 0)),
            scratch_shapes=[
                pltpu.VMEM((rows + 2 * REACH, 2 * BLOCK), BF),
                pltpu.VMEM((rows + 2 * REACH, 2 * BLOCK), BF),
                pltpu.VMEM((2 * TILE, SPAN), F32),
                pltpu.SemaphoreType.DMA((6,)),
            ],
        ),
        compiler_params=params(56),
        name="attend",
    )(edges, queries, low, own, high)


ROWS_E = 64
ROWS_S = 64
ROWS_P = 16
PACK = ROWS_E + ROWS_S + ROWS_P


def pack_weights(position, expand, shrink, project_out):
    part = lax.dynamic_slice_in_dim(expand, position * 2 * ROWS_E, 2 * ROWS_E, 0)
    return jnp.concatenate(
        [
            jnp.concatenate([part[:ROWS_E], part[ROWS_E:]], axis=1),
            lax.dynamic_slice_in_dim(shrink, position * ROWS_S, ROWS_S, 0),
            lax.dynamic_slice_in_dim(project_out, position * ROWS_P, ROWS_P, 0),
        ],
        axis=0,
    )


def gelu(v):
    return 0.5 * v * (1.0 + jnp.tanh(0.7978845608028654 * (v + 0.044715 * v * v * v)))


def forward_kernel(table, *refs):
    parts = refs[:8]
    context, share, gain, out, expand, shrink, outward, sems = refs[8:]
    groups = ([], [], [])
    width = expand.shape[3]
    for n, part in enumerate(parts):
        where = table[8 + n]
        for side in range(2):
            slot = 1 - side if n % 4 == 3 else side

            def copy(group, source, target):
                groups[group].append(
                    pltpu.make_async_copy(source, target, sems.at[group, len(groups[group])])
                )

            copy(
                0,
                part.at[:, side, pl.ds(ROWS_E + ROWS_S, ROWS_P), :],
                outward.at[
                    :, slot, pl.ds(pl.multiple_of(where * ROWS_P, ROWS_P), ROWS_P), :
                ],
            )
            for piece in range(2):
                copy(
                    1,
                    part.at[:, side, pl.ds(0, ROWS_E), pl.ds(piece * width, width)],
                    expand.at[
                        :,
                        slot,
                        pl.ds(
                            pl.multiple_of(where * 2 * ROWS_E + piece * ROWS_E, ROWS_E), ROWS_E
                        ),
                        :,
                    ],
                )
            copy(
                2,
                part.at[:, side, pl.ds(ROWS_E, ROWS_S), :],
                shrink.at[:, slot, pl.ds(pl.multiple_of(where * ROWS_S, ROWS_S), ROWS_S), :],
            )
    for group in groups:
        for c in group:
            c.start()
    for c in groups[0]:
        c.wait()
    total = dot(context[table[0]], outward[0, 0])
    for p in range(1, 8):
        total = total + dot(context[table[p]], outward[p // 2, p % 2])
    start = jnp.concatenate([share[h] for h in range(8)], axis=1).astype(F32)
    middle = (start + total).astype(BF).astype(F32)
    average = jnp.mean(middle, axis=1, keepdims=True)
    centred = middle - average
    spread = jnp.mean(centred * centred, axis=1, keepdims=True)
    normed = (centred * lax.rsqrt(spread + EPSILON) * gain[...]).astype(BF)
    for c in groups[1]:
        c.wait()
    hidden = [gelu(dot(normed, expand[p // 2, p % 2])).astype(BF) for p in range(8)]
    for c in groups[2]:
        c.wait()
    total = middle
    for p in range(8):
        total = total + dot(hidden[p], shrink[p // 2, p % 2])
    done = total.astype(BF)
    for h in range(8):
        out[h] = done[:, h * BLOCK : (h + 1) * BLOCK]


def forward(table, parts, context, share, gain):
    rows = share.shape[1]
    width = D // 2
    return pl.pallas_call(
        forward_kernel,
        out_shape=jax.ShapeDtypeStruct((8, rows, BLOCK), BF),
        grid_spec=pltpu.PrefetchScalarGridSpec(
            num_scalar_prefetch=1,
            grid=(1,),
            in_specs=[ANY] * 8
            + [whole((8, rows, BLOCK)), whole((8, rows, BLOCK)), whole((1, D))],
            out_specs=whole((8, rows, BLOCK)),
            scratch_shapes=[
                pltpu.VMEM((4, 2, D, width), BF),
                pltpu.VMEM((4, 2, width, D), BF),
                pltpu.VMEM((4, 2, BLOCK, D), BF),
                pltpu.SemaphoreType.DMA((3, 32)),
            ],
        ),
        compiler_params=params(56),
        cost_estimate=cost(4_800_000_000, 20_000_000, 1_100_000),
        name="forward",
    )(table, *parts, context, share, gain.reshape(1, D))


EACH = 8


def decode_kernel(index, low, own, high, weights, back, sums, source, held, kept, sems):
    rim, slots = low.shape[0], weights.shape[1]
    steps = weights.shape[0] // EACH
    ahead = pieces_of(low, source, 0, 1, sems, 0)
    ahead += pieces_of(own, source, rim, 2, sems, 1)
    ahead += pieces_of(high, source, rim + own.shape[0], 1, sems, 3)
    blocks = pieces_of(weights, held, 0, 2 * steps, sems, 4)
    done = pieces_of(kept, back, 0, steps, sems, 4 + 2 * steps)
    for c in ahead + blocks:
        c.start()
    for c in ahead:
        c.wait()
    ones = jnp.ones((BLOCK, BLOCK), BF)
    row = lax.broadcasted_iota(jnp.int32, (BLOCK, BLOCK), 0)
    column = lax.broadcasted_iota(jnp.int32, (BLOCK, BLOCK), 1)
    for step in range(steps):
        blocks[2 * step].wait()
        blocks[2 * step + 1].wait()
        kinds = []
        for b in range(step * EACH, (step + 1) * EACH):
            left = jnp.concatenate([held[b, k] for k in range(slots)], axis=1)
            right = jnp.concatenate([source[index[b, k]] for k in range(slots)], axis=0)
            made = dot(left, right)
            plain = made.astype(BF)
            kept[b * BLOCK : (b + 1) * BLOCK] = plain
            kinds.append((plain, (made * made).astype(BF)))
        done[step].start()
        held_sums = [
            jnp.sum(jnp.where(row == column, dot(kinds[b][n], ones), 0.0), axis=0, keepdims=True)
            for n in range(2)
            for b in range(EACH)
        ]
        sums[step] = jnp.concatenate(held_sums, axis=0).astype(BF)
    for c in done:
        c.wait()


def decode(index, low, own, high, weights):
    count, slots = weights.shape[:2]
    blocks = own.shape[0]
    rim = low.shape[0]
    steps = count // EACH
    return pl.pallas_call(
        decode_kernel,
        out_shape=(
            jax.ShapeDtypeStruct((count * BLOCK, BLOCK), BF),
            jax.ShapeDtypeStruct((steps, 2 * EACH, BLOCK), BF),
        ),
        grid_spec=pltpu.PrefetchScalarGridSpec(
            num_scalar_prefetch=1,
            grid=(1,),
            in_specs=[ANY, ANY, ANY, FAR],
            out_specs=(ANY, whole((steps, 2 * EACH, BLOCK))),
            scratch_shapes=[
                pltpu.VMEM((blocks + 2 * rim, BLOCK, BLOCK), BF),
                pltpu.VMEM((count, slots, BLOCK, BLOCK), BF),
                pltpu.VMEM((count * BLOCK, BLOCK), BF),
                pltpu.SemaphoreType.DMA((4 + 3 * steps,)),
            ],
        ),
        compiler_params=params(56),
        cost_estimate=cost(540_000_000, 10_000_000),
        name="decode",
    )(index, low, own, high, weights)


def finish_kernel(sums, back, state, gain, out, stats, kept, base, made, sems):
    steps = sums.shape[1]
    count = sums.shape[0]
    first = pieces_of(sums, stats, 0, count, sems, 0)
    backs = pieces_of(back, kept, 0, steps, sems, count)
    states = pieces_of(state, base, 0, steps, sems, count + steps)
    outs = pieces_of(made, out, 0, steps, sems, count + 2 * steps)
    for c in first:
        c.start()
    for a, b in zip(backs, states):
        a.start()
        b.start()
    depth = count * 2 * EACH
    row = lax.broadcasted_iota(jnp.int32, (depth, 2 * EACH * BLOCK), 0)
    column = lax.broadcasted_iota(jnp.int32, (depth, 2 * EACH * BLOCK), 1)
    pick = jnp.where((row % (2 * EACH)) == (column // BLOCK), 1.0 / D, 0.0).astype(BF)
    for c in first:
        c.wait()
    for step in range(steps):
        parts = jnp.concatenate([stats[h, step] for h in range(count)], axis=0)
        spread = lax.dot_general(parts, pick, TN, preferred_element_type=F32)
        backs[step].wait()
        states[step].wait()
        for b in range(EACH):
            at = (step * EACH + b) * BLOCK
            average = spread[:, b * BLOCK : (b + 1) * BLOCK]
            squares = spread[:, (EACH + b) * BLOCK : (EACH + b + 1) * BLOCK]
            scale = lax.rsqrt(squares - average * average + EPSILON) * gain[...]
            made[at : at + BLOCK] = (
                base[at : at + BLOCK].astype(F32)
                + (kept[at : at + BLOCK].astype(F32) - average) * scale
            ).astype(BF)
        outs[step].start()
    for c in outs:
        c.wait()


def finish(sums, back, state, gain):
    rows = state.shape[0]
    count, steps = sums.shape[:2]
    return pl.pallas_call(
        finish_kernel,
        out_shape=jax.ShapeDtypeStruct((rows, BLOCK), BF),
        grid_spec=pl.GridSpec(
            grid=(1,),
            in_specs=[ANY, ANY, FAR, whole((1, BLOCK))],
            out_specs=ANY,
            scratch_shapes=[
                pltpu.VMEM(sums.shape, BF),
                pltpu.VMEM((rows, BLOCK), BF),
                pltpu.VMEM((rows, BLOCK), BF),
                pltpu.VMEM((rows, BLOCK), BF),
                pltpu.SemaphoreType.DMA((count + 3 * steps,)),
            ],
        ),
        compiler_params=params(24),
        cost_estimate=cost(540_000_000, 8_000_000),
        name="finish",
    )(sums, back, state, gain.reshape(1, BLOCK))


def shifted(value, by):
    return lax.ppermute(value, "seq", [(i, i + by) for i in range(16) if 0 <= i + by < 16])


def among(value, axis, count, to):
    return lax.ppermute(value, axis, [(i, to(i)) for i in range(count)])


def along_z(i, by):
    return (i // 8) * 8 + ((i // 2 + by) % 4) * 2 + i % 2


UP = lambda v: among(v, "seq", 16, lambda i: along_z(i, 1))
DOWN = lambda v: among(v, "seq", 16, lambda i: along_z(i, -1))
ACROSS = lambda v: among(v, ("seq", "head"), 128, lambda i: i ^ 65)
TWIN = lambda v: among(v, "seq", 16, lambda i: i ^ 1)
NORTH = lambda v: among(v, "head", 8, lambda i: (i + 2) % 8)
SOUTH = lambda v: among(v, "head", 8, lambda i: (i - 2) % 8)
OVER = lambda v: among(v, "head", 8, lambda i: i ^ 1)


def on_device(
    grid_state,
    encode_index,
    encode_weights,
    first_gain,
    project_in,
    project_out,
    second_gain,
    expand_weights,
    shrink_weights,
    decode_index,
    decode_weights,
    output_gain,
):
    band = lax.axis_index("seq")
    bands = lax.axis_size("seq")
    me = lax.axis_index("head")
    mesh_blocks = encode_weights.shape[0]
    mesh_rows = mesh_blocks * BLOCK
    grid_blocks = grid_state.shape[0] // BLOCK
    rim = mesh_blocks * BLOCK
    core, place = band % 2, (band // 2 + 2 * (band // 8)) % 4
    position = place * 2 + core
    packed = pack_weights(position, expand_weights, shrink_weights, project_out)
    last, first, packed = lax.optimization_barrier(
        (grid_state[-rim:], grid_state[:rim], packed)
    )
    low = shifted(last, 1)
    high = shifted(first, -1)
    swapped, north, south = OVER(packed), NORTH(packed), SOUTH(packed)
    swapped_north, swapped_south = NORTH(swapped), SOUTH(swapped)
    far, swapped_far = NORTH(north), SOUTH(swapped_south)
    inward = [project_in[:, j, :].reshape(8, BLOCK, BLOCK) for j in range(3)]
    low, high, *inward = lax.optimization_barrier((low, high, *inward))
    mesh_start = encode(
        encode_index - (band * grid_blocks - mesh_blocks), low, grid_state, high, encode_weights
    )
    half = mesh_rows // 2
    mine = jnp.stack(
        [
            jnp.stack(pair)
            for pair in (
                (packed, swapped),
                (north, swapped_north),
                (south, swapped_south),
                (far, swapped_far),
            )
        ]
    )
    x, mine = lax.optimization_barrier((mesh_start, mine))
    up, down = UP(mine), DOWN(mine)
    y, xa, xb, mine = lax.optimization_barrier((OVER(x), NORTH(x), SOUTH(x), mine))
    across = ACROSS(mine)
    from_south = NORTH(jnp.concatenate([xa[:half], y]))
    from_north = SOUTH(jnp.concatenate([xb[half:], y]))
    xc = jnp.concatenate([from_south[:half], from_north[:half]])
    slots = (x, y, xa, from_south, xb, from_north, xc, OVER(xc))
    partner = me ^ 1
    order = jnp.stack(
        [me, partner] + [(v + by) % 8 for by in (6, 2, 4) for v in (me, partner)]
    ).astype(jnp.int32)
    queries, keys_values, share = project(order, slots, first_gain, inward)
    upper, lower, up, down = lax.optimization_barrier(
        (keys_values[mesh_rows - REACH :], keys_values[:REACH], up, down)
    )
    below = shifted(upper, 1)
    above = shifted(lower, -1)
    edges = jnp.stack([band == 0, band == bands - 1]).astype(jnp.int32)
    context = attend(edges, queries, below, keys_values, above)
    context, *here = lax.optimization_barrier((context, mine, up, down, across))
    parts = here + [TWIN(v) for v in here]
    context = lax.all_to_all(
        context.reshape(8, mesh_rows // 8, BLOCK), "head", 0, 0, tiled=True
    )
    places = [
        ((place + by) % 4) * 2 + side for side in (core, 1 - core) for by in (0, 3, 1, 2)
    ]
    table = jnp.concatenate([order, jnp.stack(places).astype(jnp.int32)])
    mesh_end = forward(table, parts, context, share, second_gain)
    mesh_end = lax.all_to_all(mesh_end, "head", 0, 0, tiled=True)
    mesh_end = mesh_end.reshape(mesh_blocks, BLOCK, BLOCK)
    edge = mesh_blocks // 2
    back, sums = decode(
        decode_index - (band * mesh_blocks - edge),
        shifted(mesh_end[-edge:], 1),
        mesh_end,
        shifted(mesh_end[:edge], -1),
        decode_weights,
    )
    sums = lax.all_to_all(
        jnp.broadcast_to(sums, (8, *sums.shape)), "head", 0, 0, tiled=True
    )
    return finish(sums, back, grid_state, output_gain)


def solution(mesh):
    in_specs = (
        P("seq", "head"),
        P("seq", None),
        P("seq", None, None, None),
        P(),
        P(None, None, "head"),
        P("head", None),
        P(),
        P(None, "head"),
        P("head", None),
        P("seq", None),
        P("seq", None, None, None),
        P("head"),
    )
    return jax.shard_map(
        on_device, mesh=mesh, in_specs=in_specs, out_specs=P("seq", "head"), check_vma=False
    )
```

```python
import jax
import jax.numpy as jnp
from jax import lax
from jax.experimental import pallas as pl
from jax.experimental.pallas import tpu as pltpu
from jax.sharding import PartitionSpec as P

D = 1024
HEAD_DIM = 64
WINDOW = 1120
REACH = 1152
BLOCK = 128
EPSILON = 1e-05
LOG2E = 1.4426950408889634
BF = jnp.bfloat16
F32 = jnp.float32
NT = (((1,), (1,)), ((), ()))
TN = (((0,), (0,)), ((), ()))
MIB = 1 << 20


def params(mib):
    return pltpu.CompilerParams(
        dimension_semantics=("arbitrary",), vmem_limit_bytes=mib * MIB
    )


def dot(a, b):
    return jnp.dot(a, b, preferred_element_type=F32)


def cost(flops, moved, powers=0):
    return pl.CostEstimate(flops=flops, bytes_accessed=moved, transcendentals=powers)


ANY = pl.BlockSpec(memory_space=pl.ANY)
FAR = pl.BlockSpec(memory_space=pltpu.HBM)


def whole(shape):
    return pl.BlockSpec(shape, lambda i, *_: (0,) * len(shape))


def pieces_of(ref, target, start, count, sems, first):
    length = ref.shape[0] // count
    return [
        pltpu.make_async_copy(
            ref.at[pl.ds(n * length, length)],
            target.at[pl.ds(start + n * length, length)],
            sems.at[first + n],
        )
        for n in range(count)
    ]


def encode_kernel(index, low, own, high, weights, out, source, held, made, sems):
    rim, slots = low.shape[0], weights.shape[1]
    ahead = pieces_of(low, source, 0, 2, sems, 0)
    ahead += pieces_of(own, source, rim, 4, sems, 2)
    ahead += pieces_of(high, source, rim + own.shape[0], 2, sems, 6)
    count = weights.shape[0]
    blocks = pieces_of(weights, held, 0, count, sems, 8)
    back = pieces_of(made, out, 0, 4, sems, 8 + count)
    for c in ahead + blocks:
        c.start()
    for c in ahead:
        c.wait()
    for b in range(count):
        blocks[b].wait()
        left = jnp.concatenate([held[b, k] for k in range(slots)], axis=1)
        right = jnp.concatenate([source[index[b, k]] for k in range(slots)], axis=0)
        made[b * BLOCK : (b + 1) * BLOCK] = dot(left, right).astype(BF)
        if (b + 1) % (count // 4) == 0:
            back[b // (count // 4)].start()
    for c in back:
        c.wait()


def encode(index, low, own, high, weights):
    count, slots = weights.shape[:2]
    blocks = own.shape[0] // BLOCK
    rim = low.shape[0] // BLOCK
    shaped = [v.reshape(-1, BLOCK, BLOCK) for v in (low, own, high)]
    return pl.pallas_call(
        encode_kernel,
        out_shape=jax.ShapeDtypeStruct((count * BLOCK, BLOCK), BF),
        grid_spec=pltpu.PrefetchScalarGridSpec(
            num_scalar_prefetch=1,
            grid=(1,),
            in_specs=[ANY, FAR, ANY, FAR],
            out_specs=ANY,
            scratch_shapes=[
                pltpu.VMEM((blocks + 2 * rim, BLOCK, BLOCK), BF),
                pltpu.VMEM((count, slots, BLOCK, BLOCK), BF),
                pltpu.VMEM((count * BLOCK, BLOCK), BF),
                pltpu.SemaphoreType.DMA((12 + count,)),
            ],
        ),
        compiler_params=params(56),
        cost_estimate=cost(540_000_000, 8_000_000),
        name="encode",
    )(index, *shaped, weights)


def project_kernel(
    order, s0, s1, s2, s3, s4, s5, s6, s7, gain, wq, wk, wv,
    queries, keys_values, share, ordered,
):
    step = pl.program_id(0)

    @pl.when(step == 0)
    def _():
        for p in range(8):
            ordered[p * BLOCK : (p + 1) * BLOCK] = jnp.concatenate(
                [w[order[p]] for w in (wq, wk, wv)], axis=1
            )

    raw = [s[...] for s in (s0, s1, s2, s3, s4, s5, s6, s7)]

    tile = share.shape[1]
    per = raw[0].shape[0] // tile
    for n in range(per):

        @pl.when(order[0] == step * per + n)
        def _():
            for p in range(8):
                share[order[p]] = raw[p][n * tile : (n + 1) * tile]

    pieces = [r.astype(F32) for r in raw]
    total = pieces[0]
    for x in pieces[1:]:
        total = total + x
    average = jnp.sum(total, axis=1, keepdims=True) * (1.0 / D)
    pieces = [x - average for x in pieces]
    total = pieces[0] * pieces[0]
    for x in pieces[1:]:
        total = total + x * x
    spread = lax.rsqrt(jnp.sum(total, axis=1, keepdims=True) * (1.0 / D) + EPSILON)
    normed = jnp.concatenate(
        [(x * spread * gain[order[p]]).astype(BF) for p, x in enumerate(pieces)], axis=1
    )
    made = dot(normed, ordered[...])
    queries[...] = (made[:, :BLOCK] * (HEAD_DIM**-0.5 * LOG2E)).astype(BF)
    keys_values[...] = made[:, BLOCK:].astype(BF)


def project(order, slots, gain, weights):
    rows = slots[0].shape[0]
    tile, steps = rows // 8, 4
    each = rows // steps
    full = pl.BlockSpec((each, BLOCK), lambda i, _: (i, 0))
    second = pl.BlockSpec((each, BLOCK), lambda i, _: (i + steps // 2, 0))
    return pl.pallas_call(
        project_kernel,
        out_shape=(
            jax.ShapeDtypeStruct((rows, BLOCK), BF),
            jax.ShapeDtypeStruct((rows, 2 * BLOCK), BF),
            jax.ShapeDtypeStruct((8, tile, BLOCK), BF),
        ),
        grid_spec=pltpu.PrefetchScalarGridSpec(
            num_scalar_prefetch=1,
            grid=(steps,),
            in_specs=[full, full, full, second, full, second, full, full]
            + [whole((8, 1, BLOCK))]
            + [whole((8, BLOCK, BLOCK))] * 3,
            out_specs=(
                full,
                pl.BlockSpec((each, 2 * BLOCK), lambda i, _: (i, 0)),
                whole((8, tile, BLOCK)),
            ),
            scratch_shapes=[pltpu.VMEM((D, 3 * BLOCK), BF)],
        ),
        compiler_params=params(56),
        name="project",
    )(order, *slots, gain.reshape(8, 1, BLOCK), *weights)


TILE = 256
CHUNKS = 11
MIDDLE = CHUNKS // 2


def columns_of(part, keys, values, start, count, sems, first):
    length = part.shape[0] // count
    copies = []
    for n in range(count):
        rows = pl.ds(n * length, length)
        for m, target in enumerate((keys, values)):
            copies.append(
                pltpu.make_async_copy(
                    part.at[rows, pl.ds(m * BLOCK, BLOCK)],
                    target.at[pl.ds(start + n * length, length), pl.ds(0, BLOCK)],
                    sems.at[first + 2 * n + m],
                )
            )
    return copies


def chunk(c):
    return (BLOCK, BLOCK) if c == 0 else (0, BLOCK) if c == CHUNKS - 1 else (0, TILE)


def stacked_heads(q):
    lane = lax.broadcasted_iota(jnp.int32, q.shape, 1)
    zero = jnp.zeros_like(q)
    return jnp.concatenate(
        [jnp.where(lane < HEAD_DIM, q, zero), jnp.where(lane < HEAD_DIM, zero, q)], axis=0
    )


def score_chunk(c, stacked, keys, start, scores, highest):
    skip, width = chunk(c)
    part = keys[pl.ds(pl.multiple_of(start, BLOCK), width)]
    s = lax.dot_general(stacked, part, NT, preferred_element_type=F32)
    if c <= 1 or c >= CHUNKS - 2:
        row = lax.broadcasted_iota(jnp.int32, s.shape, 0) & (TILE - 1)
        gap = lax.broadcasted_iota(jnp.int32, s.shape, 1) - row + (c - MIDDLE) * TILE + skip
        s = jnp.where(gap >= -WINDOW if c <= 1 else gap <= WINDOW, s, -1e30)
    scores[:, c * TILE : c * TILE + width] = s
    best = s[:, :BLOCK]
    if width == TILE:
        best = jnp.maximum(best, s[:, BLOCK:])
    highest[...] = jnp.maximum(highest[...], best)


def value_chunk(c, peak, values, start, scores, total):
    _, width = chunk(c)
    part = values[pl.ds(pl.multiple_of(start, BLOCK), width)]
    powers = jnp.exp2(scores[:, c * TILE : c * TILE + width] - peak)
    total[...] += dot(powers.astype(BF), part)


def near_kernel(queries, own, out, keys, values, scores, highest, total, sems):
    step = pl.program_id(0)
    blocks = pl.num_programs(0)

    @pl.when(step == 0)
    def _():
        copies = columns_of(own, keys, values, 0, 4, sems, 0)
        for c in copies:
            c.start()
        values[:, BLOCK:] = jnp.ones((values.shape[0], BLOCK), BF)
        for c in copies:
            c.wait()

    stacked = stacked_heads(queries[...])
    highest[...] = jnp.full(highest.shape, -1e30, F32)
    total[...] = jnp.zeros(total.shape, F32)
    for c in range(CHUNKS):
        block = step + c - MIDDLE

        @pl.when((block >= 0) & (block < blocks))
        def _():
            score_chunk(c, stacked, keys, block * TILE + chunk(c)[0], scores, highest)

    peak = jnp.max(highest[...], axis=1, keepdims=True)
    for c in range(CHUNKS):
        block = step + c - MIDDLE

        @pl.when((block >= 0) & (block < blocks))
        def _():
            value_chunk(c, peak, values, block * TILE + chunk(c)[0], scores, total)

    lane = lax.broadcasted_iota(jnp.int32, (2 * TILE, BLOCK), 1)
    made = total[...]
    out[:, :BLOCK] = made[:, :BLOCK]
    out[:, BLOCK:] = jnp.where(lane < HEAD_DIM, made[:, BLOCK:], peak)


def far_kernel(edges, queries, near, low, high, out, keys, values, scores, highest, total, sems):
    step = pl.program_id(0)
    blocks = pl.num_programs(0)

    @pl.when(step == 0)
    def _():
        copies = columns_of(low, keys, values, 0, 3, sems, 0)
        copies += columns_of(high, keys, values, REACH, 3, sems, 6)
        for c in copies:
            c.start()
        values[:, BLOCK:] = jnp.ones((values.shape[0], BLOCK), BF)
        for c in copies:
            c.wait()

    stacked = stacked_heads(queries[...])
    before = near[:, BLOCK + HEAD_DIM : BLOCK + HEAD_DIM + 1]
    highest[...] = jnp.broadcast_to(before, highest.shape)
    places = {}
    for c in range(CHUNKS):
        if c == MIDDLE:
            continue
        block = step + c - MIDDLE
        if c < MIDDLE:
            there = (block < 0) & (edges[0] == 0)
            start = block * TILE + REACH + chunk(c)[0]
        else:
            there = (block >= blocks) & (edges[1] == 0)
            start = REACH + (block - blocks) * TILE
        places[c] = there, start

        @pl.when(there)
        def _():
            score_chunk(c, stacked, keys, start, scores, highest)

    peak = jnp.max(highest[...], axis=1, keepdims=True)
    scale = jnp.exp2(before - peak)
    total[:, :BLOCK] = near[:, :BLOCK] * scale
    total[:, BLOCK:] = jnp.broadcast_to(near[:, BLOCK : BLOCK + 1] * scale, (2 * TILE, BLOCK))
    for c, (there, start) in places.items():

        @pl.when(there)
        def _():
            value_chunk(c, peak, values, start, scores, total)

    lane = lax.broadcasted_iota(jnp.int32, (TILE, BLOCK), 1)
    made = total[:, :BLOCK] / total[:, BLOCK:]
    out[...] = jnp.where(lane < HEAD_DIM, made[:TILE], made[TILE:]).astype(BF)


def attention_scratch(rows, copies):
    return [
        pltpu.VMEM((rows, BLOCK), BF),
        pltpu.VMEM((rows, 2 * BLOCK), BF),
        pltpu.VMEM((2 * TILE, CHUNKS * TILE), F32),
        pltpu.VMEM((2 * TILE, BLOCK), F32),
        pltpu.VMEM((2 * TILE, 2 * BLOCK), F32),
        pltpu.SemaphoreType.DMA((copies,)),
    ]


def attend_near(queries, own):
    rows = own.shape[0]
    return pl.pallas_call(
        near_kernel,
        out_shape=jax.ShapeDtypeStruct((2 * rows, 2 * BLOCK), F32),
        grid_spec=pl.GridSpec(
            grid=(rows // TILE,),
            in_specs=[pl.BlockSpec((TILE, BLOCK), lambda i: (i, 0)), ANY],
            out_specs=pl.BlockSpec((2 * TILE, 2 * BLOCK), lambda i: (i, 0)),
            scratch_shapes=attention_scratch(rows, 8),
        ),
        compiler_params=params(40),
        cost_estimate=cost(7_000_000_000, 6_000_000, 7_000_000),
        name="attend_near",
    )(queries, own)


def attend_far(edges, queries, near, low, high):
    rows = queries.shape[0]
    return pl.pallas_call(
        far_kernel,
        out_shape=jax.ShapeDtypeStruct((rows, BLOCK), BF),
        grid_spec=pltpu.PrefetchScalarGridSpec(
            num_scalar_prefetch=1,
            grid=(rows // TILE,),
            in_specs=[
                pl.BlockSpec((TILE, BLOCK), lambda i, _: (i, 0)),
                pl.BlockSpec((2 * TILE, 2 * BLOCK), lambda i, _: (i, 0)),
                ANY,
                ANY,
            ],
            out_specs=pl.BlockSpec((TILE, BLOCK), lambda i, _: (i, 0)),
            scratch_shapes=attention_scratch(2 * REACH, 12),
        ),
        compiler_params=params(40),
        name="attend_far",
    )(edges, queries, near, low, high)


ROWS_E = 64
ROWS_S = 64
ROWS_P = 16
PACK = ROWS_E + ROWS_S + ROWS_P


def pack_weights(position, expand, shrink, project_out):
    part = lax.dynamic_slice_in_dim(expand, position * 2 * ROWS_E, 2 * ROWS_E, 0)
    return jnp.concatenate(
        [
            jnp.concatenate([part[:ROWS_E], part[ROWS_E:]], axis=1),
            lax.dynamic_slice_in_dim(shrink, position * ROWS_S, ROWS_S, 0),
            lax.dynamic_slice_in_dim(project_out, position * ROWS_P, ROWS_P, 0),
        ],
        axis=0,
    )


def gelu(v):
    return 0.5 * v * (1.0 + jnp.tanh(0.7978845608028654 * (v + 0.044715 * v * v * v)))


def forward_kernel(table, *refs):
    parts = refs[:8]
    context, share, gain, out, expand, shrink, outward, sems = refs[8:]
    groups = ([], [], [])
    width = expand.shape[3]
    for n, part in enumerate(parts):
        where = table[8 + n]
        for side in range(2):
            slot = 1 - side if n % 4 == 3 else side

            def copy(group, source, target):
                groups[group].append(
                    pltpu.make_async_copy(source, target, sems.at[group, len(groups[group])])
                )

            copy(
                0,
                part.at[:, side, pl.ds(ROWS_E + ROWS_S, ROWS_P), :],
                outward.at[
                    :, slot, pl.ds(pl.multiple_of(where * ROWS_P, ROWS_P), ROWS_P), :
                ],
            )
            for piece in range(2):
                copy(
                    1,
                    part.at[:, side, pl.ds(0, ROWS_E), pl.ds(piece * width, width)],
                    expand.at[
                        :,
                        slot,
                        pl.ds(
                            pl.multiple_of(where * 2 * ROWS_E + piece * ROWS_E, ROWS_E), ROWS_E
                        ),
                        :,
                    ],
                )
            copy(
                2,
                part.at[:, side, pl.ds(ROWS_E, ROWS_S), :],
                shrink.at[:, slot, pl.ds(pl.multiple_of(where * ROWS_S, ROWS_S), ROWS_S), :],
            )
    for group in groups:
        for c in group:
            c.start()
    for c in groups[0]:
        c.wait()
    total = dot(context[table[0]], outward[0, 0])
    for p in range(1, 8):
        total = total + dot(context[table[p]], outward[p // 2, p % 2])
    start = jnp.concatenate([share[h] for h in range(8)], axis=1).astype(F32)
    middle = (start + total).astype(BF).astype(F32)
    average = jnp.mean(middle, axis=1, keepdims=True)
    centred = middle - average
    spread = jnp.mean(centred * centred, axis=1, keepdims=True)
    normed = (centred * lax.rsqrt(spread + EPSILON) * gain[...]).astype(BF)
    for c in groups[1]:
        c.wait()
    hidden = [gelu(dot(normed, expand[p // 2, p % 2])).astype(BF) for p in range(8)]
    for c in groups[2]:
        c.wait()
    total = middle
    for p in range(8):
        total = total + dot(hidden[p], shrink[p // 2, p % 2])
    done = total.astype(BF)
    for h in range(8):
        out[h] = done[:, h * BLOCK : (h + 1) * BLOCK]


def forward(table, parts, context, share, gain):
    rows = share.shape[1]
    width = D // 2
    return pl.pallas_call(
        forward_kernel,
        out_shape=jax.ShapeDtypeStruct((8, rows, BLOCK), BF),
        grid_spec=pltpu.PrefetchScalarGridSpec(
            num_scalar_prefetch=1,
            grid=(1,),
            in_specs=[ANY] * 8
            + [whole((8, rows, BLOCK)), whole((8, rows, BLOCK)), whole((1, D))],
            out_specs=whole((8, rows, BLOCK)),
            scratch_shapes=[
                pltpu.VMEM((4, 2, D, width), BF),
                pltpu.VMEM((4, 2, width, D), BF),
                pltpu.VMEM((4, 2, BLOCK, D), BF),
                pltpu.SemaphoreType.DMA((3, 32)),
            ],
        ),
        compiler_params=params(56),
        cost_estimate=cost(4_800_000_000, 20_000_000, 1_100_000),
        name="forward",
    )(table, *parts, context, share, gain.reshape(1, D))


EACH = 8


def decode_kernel(index, low, own, high, weights, back, sums, source, held, kept, sems):
    rim, slots = low.shape[0], weights.shape[1]
    steps = weights.shape[0] // EACH
    ahead = pieces_of(low, source, 0, 1, sems, 0)
    ahead += pieces_of(own, source, rim, 2, sems, 1)
    ahead += pieces_of(high, source, rim + own.shape[0], 1, sems, 3)
    blocks = pieces_of(weights, held, 0, 2 * steps, sems, 4)
    done = pieces_of(kept, back, 0, steps, sems, 4 + 2 * steps)
    for c in ahead + blocks:
        c.start()
    for c in ahead:
        c.wait()
    ones = jnp.ones((BLOCK, BLOCK), BF)
    row = lax.broadcasted_iota(jnp.int32, (BLOCK, BLOCK), 0)
    column = lax.broadcasted_iota(jnp.int32, (BLOCK, BLOCK), 1)
    for step in range(steps):
        blocks[2 * step].wait()
        blocks[2 * step + 1].wait()
        kinds = []
        for b in range(step * EACH, (step + 1) * EACH):
            left = jnp.concatenate([held[b, k] for k in range(slots)], axis=1)
            right = jnp.concatenate([source[index[b, k]] for k in range(slots)], axis=0)
            made = dot(left, right)
            plain = made.astype(BF)
            kept[b * BLOCK : (b + 1) * BLOCK] = plain
            kinds.append((plain, (made * made).astype(BF)))
        done[step].start()
        wide = dot(jnp.concatenate([k[n] for n in range(2) for k in kinds], axis=0), ones)
        held_sums = [
            jnp.sum(
                jnp.where(row == column, wide[n * BLOCK : (n + 1) * BLOCK], 0.0),
                axis=0,
                keepdims=True,
            )
            for n in range(2 * EACH)
        ]
        sums[step] = jnp.concatenate(held_sums, axis=0).astype(BF)
    for c in done:
        c.wait()


def decode(index, low, own, high, weights):
    count, slots = weights.shape[:2]
    blocks = own.shape[0]
    rim = low.shape[0]
    steps = count // EACH
    return pl.pallas_call(
        decode_kernel,
        out_shape=(
            jax.ShapeDtypeStruct((count * BLOCK, BLOCK), BF),
            jax.ShapeDtypeStruct((steps, 2 * EACH, BLOCK), BF),
        ),
        grid_spec=pltpu.PrefetchScalarGridSpec(
            num_scalar_prefetch=1,
            grid=(1,),
            in_specs=[ANY, ANY, ANY, FAR],
            out_specs=(ANY, whole((steps, 2 * EACH, BLOCK))),
            scratch_shapes=[
                pltpu.VMEM((blocks + 2 * rim, BLOCK, BLOCK), BF),
                pltpu.VMEM((count, slots, BLOCK, BLOCK), BF),
                pltpu.VMEM((count * BLOCK, BLOCK), BF),
                pltpu.SemaphoreType.DMA((4 + 3 * steps,)),
            ],
        ),
        compiler_params=params(56),
        cost_estimate=cost(540_000_000, 10_000_000),
        name="decode",
    )(index, low, own, high, weights)


def finish_kernel(sums, back, state, gain, out, stats, kept, base, made, sems):
    steps = sums.shape[1]
    count = sums.shape[0]
    first = pieces_of(sums, stats, 0, count, sems, 0)
    backs = pieces_of(back, kept, 0, steps, sems, count)
    states = pieces_of(state, base, 0, steps, sems, count + steps)
    outs = pieces_of(made, out, 0, steps, sems, count + 2 * steps)
    for c in first:
        c.start()
    for a, b in zip(backs, states):
        a.start()
        b.start()
    depth = count * 2 * EACH
    row = lax.broadcasted_iota(jnp.int32, (depth, 2 * EACH * BLOCK), 0)
    column = lax.broadcasted_iota(jnp.int32, (depth, 2 * EACH * BLOCK), 1)
    pick = jnp.where((row % (2 * EACH)) == (column // BLOCK), 1.0 / D, 0.0).astype(BF)
    for c in first:
        c.wait()
    for step in range(steps):
        parts = jnp.concatenate([stats[h, step] for h in range(count)], axis=0)
        spread = lax.dot_general(parts, pick, TN, preferred_element_type=F32)
        backs[step].wait()
        states[step].wait()
        for b in range(EACH):
            at = (step * EACH + b) * BLOCK
            average = spread[:, b * BLOCK : (b + 1) * BLOCK]
            squares = spread[:, (EACH + b) * BLOCK : (EACH + b + 1) * BLOCK]
            scale = lax.rsqrt(squares - average * average + EPSILON) * gain[...]
            made[at : at + BLOCK] = (
                base[at : at + BLOCK].astype(F32)
                + (kept[at : at + BLOCK].astype(F32) - average) * scale
            ).astype(BF)
        outs[step].start()
    for c in outs:
        c.wait()


def finish(sums, back, state, gain):
    rows = state.shape[0]
    count, steps = sums.shape[:2]
    return pl.pallas_call(
        finish_kernel,
        out_shape=jax.ShapeDtypeStruct((rows, BLOCK), BF),
        grid_spec=pl.GridSpec(
            grid=(1,),
            in_specs=[ANY, ANY, FAR, whole((1, BLOCK))],
            out_specs=ANY,
            scratch_shapes=[
                pltpu.VMEM(sums.shape, BF),
                pltpu.VMEM((rows, BLOCK), BF),
                pltpu.VMEM((rows, BLOCK), BF),
                pltpu.VMEM((rows, BLOCK), BF),
                pltpu.SemaphoreType.DMA((count + 3 * steps,)),
            ],
        ),
        compiler_params=params(56),
        cost_estimate=cost(540_000_000, 8_000_000),
        name="finish",
    )(sums, back, state, gain.reshape(1, BLOCK))


def shifted(value, by):
    return lax.ppermute(value, "seq", [(i, i + by) for i in range(16) if 0 <= i + by < 16])


def among(value, axis, count, to):
    return lax.ppermute(value, axis, [(i, to(i)) for i in range(count)])


def along_z(i, by):
    return (i // 8) * 8 + ((i // 2 + by) % 4) * 2 + i % 2


UP = lambda v: among(v, "seq", 16, lambda i: along_z(i, 1))
DOWN = lambda v: among(v, "seq", 16, lambda i: along_z(i, -1))
ACROSS = lambda v: among(v, ("seq", "head"), 128, lambda i: i ^ 65)
TWIN = lambda v: among(v, "seq", 16, lambda i: i ^ 1)
NORTH = lambda v: among(v, "head", 8, lambda i: (i + 2) % 8)
SOUTH = lambda v: among(v, "head", 8, lambda i: (i - 2) % 8)
OVER = lambda v: among(v, "head", 8, lambda i: i ^ 1)


def on_device(
    grid_state,
    encode_index,
    encode_weights,
    first_gain,
    project_in,
    project_out,
    second_gain,
    expand_weights,
    shrink_weights,
    decode_index,
    decode_weights,
    output_gain,
):
    band = lax.axis_index("seq")
    bands = lax.axis_size("seq")
    me = lax.axis_index("head")
    mesh_blocks = encode_weights.shape[0]
    mesh_rows = mesh_blocks * BLOCK
    grid_blocks = grid_state.shape[0] // BLOCK
    rim = mesh_blocks * BLOCK
    core, place = band % 2, (band // 2 + 2 * (band // 8)) % 4
    position = place * 2 + core
    packed = pack_weights(position, expand_weights, shrink_weights, project_out)
    last, first, packed = lax.optimization_barrier(
        (grid_state[-rim:], grid_state[:rim], packed)
    )
    low = shifted(last, 1)
    high = shifted(first, -1)
    swapped, north, south = OVER(packed), NORTH(packed), SOUTH(packed)
    swapped_north, swapped_south = NORTH(swapped), SOUTH(swapped)
    far, swapped_far = NORTH(north), SOUTH(swapped_south)
    inward = [project_in[:, j, :].reshape(8, BLOCK, BLOCK) for j in range(3)]
    low, high, *inward = lax.optimization_barrier((low, high, *inward))
    mesh_start = encode(
        encode_index - (band * grid_blocks - mesh_blocks), low, grid_state, high, encode_weights
    )
    half = mesh_rows // 2
    mine = jnp.stack(
        [
            jnp.stack(pair)
            for pair in (
                (packed, swapped),
                (north, swapped_north),
                (south, swapped_south),
                (far, swapped_far),
            )
        ]
    )
    x, mine = lax.optimization_barrier((mesh_start, mine))
    up, down = UP(mine), DOWN(mine)
    y, xa, xb, mine = lax.optimization_barrier((OVER(x), NORTH(x), SOUTH(x), mine))
    across = ACROSS(mine)
    from_south = NORTH(jnp.concatenate([xa[:half], y]))
    from_north = SOUTH(jnp.concatenate([xb[half:], y]))
    xc = jnp.concatenate([from_south[:half], from_north[:half]])
    slots = (x, y, xa, from_south, xb, from_north, xc, OVER(xc))
    partner = me ^ 1
    order = jnp.stack(
        [me, partner] + [(v + by) % 8 for by in (6, 2, 4) for v in (me, partner)]
    ).astype(jnp.int32)
    queries, keys_values, share = project(order, slots, first_gain, inward)
    queries, upper, lower, up, down = lax.optimization_barrier(
        (queries, keys_values[mesh_rows - REACH :], keys_values[:REACH], up, down)
    )
    below = shifted(upper, 1)
    above = shifted(lower, -1)
    edges = jnp.stack([band == 0, band == bands - 1]).astype(jnp.int32)
    near = attend_near(queries, keys_values)
    context = attend_far(edges, queries, near, below, above)
    context, *here = lax.optimization_barrier((context, mine, up, down, across))
    parts = here + [TWIN(v) for v in here]
    context = lax.all_to_all(
        context.reshape(8, mesh_rows // 8, BLOCK), "head", 0, 0, tiled=True
    )
    places = [
        ((place + by) % 4) * 2 + side for side in (core, 1 - core) for by in (0, 3, 1, 2)
    ]
    table = jnp.concatenate([order, jnp.stack(places).astype(jnp.int32)])
    mesh_end = forward(table, parts, context, share, second_gain)
    mesh_end = lax.all_to_all(mesh_end, "head", 0, 0, tiled=True)
    mesh_end = mesh_end.reshape(mesh_blocks, BLOCK, BLOCK)
    edge = mesh_blocks // 2
    back, sums = decode(
        decode_index - (band * mesh_blocks - edge),
        shifted(mesh_end[-edge:], 1),
        mesh_end,
        shifted(mesh_end[:edge], -1),
        decode_weights,
    )
    sums = lax.all_to_all(
        jnp.broadcast_to(sums, (8, *sums.shape)), "head", 0, 0, tiled=True
    )
    return finish(sums, back, grid_state, output_gain)


def solution(mesh):
    in_specs = (
        P("seq", "head"),
        P("seq", None),
        P("seq", None, None, None),
        P(),
        P(None, None, "head"),
        P("head", None),
        P(),
        P(None, "head"),
        P("head", None),
        P("seq", None),
        P("seq", None, None, None),
        P("head"),
    )
    return jax.shard_map(
        on_device, mesh=mesh, in_specs=in_specs, out_specs=P("seq", "head"), check_vma=False
    )
```

```python
import jax
import jax.numpy as jnp
from jax import lax
from jax.experimental import pallas as pl
from jax.experimental.pallas import tpu as pltpu
from jax.sharding import PartitionSpec as P

D = 1024
HEAD_DIM = 64
WINDOW = 1120
REACH = 1152
BLOCK = 128
EPSILON = 1e-05
LOG2E = 1.4426950408889634
BF = jnp.bfloat16
F32 = jnp.float32
NT = (((1,), (1,)), ((), ()))
TN = (((0,), (0,)), ((), ()))
MIB = 1 << 20


def params(mib):
    return pltpu.CompilerParams(
        dimension_semantics=("arbitrary",), vmem_limit_bytes=mib * MIB
    )


def dot(a, b):
    return jnp.dot(a, b, preferred_element_type=F32)


def cost(flops, moved, powers=0):
    return pl.CostEstimate(flops=flops, bytes_accessed=moved, transcendentals=powers)


ANY = pl.BlockSpec(memory_space=pl.ANY)
FAR = pl.BlockSpec(memory_space=pltpu.HBM)


def whole(shape):
    return pl.BlockSpec(shape, lambda i, *_: (0,) * len(shape))


def pieces_of(ref, target, start, count, sems, first):
    length = ref.shape[0] // count
    return [
        pltpu.make_async_copy(
            ref.at[pl.ds(n * length, length)],
            target.at[pl.ds(start + n * length, length)],
            sems.at[first + n],
        )
        for n in range(count)
    ]


def encode_kernel(index, low, own, high, weights, out, source, held, made, sems):
    rim, slots = low.shape[0], weights.shape[1]
    ahead = pieces_of(low, source, 0, 2, sems, 0)
    ahead += pieces_of(own, source, rim, 4, sems, 2)
    ahead += pieces_of(high, source, rim + own.shape[0], 2, sems, 6)
    count = weights.shape[0]
    blocks = pieces_of(weights, held, 0, count, sems, 8)
    back = pieces_of(made, out, 0, 4, sems, 8 + count)
    for c in ahead + blocks:
        c.start()
    for c in ahead:
        c.wait()
    for b in range(count):
        blocks[b].wait()
        left = jnp.concatenate([held[b, k] for k in range(slots)], axis=1)
        right = jnp.concatenate([source[index[b, k]] for k in range(slots)], axis=0)
        made[b * BLOCK : (b + 1) * BLOCK] = dot(left, right).astype(BF)
        if (b + 1) % (count // 4) == 0:
            back[b // (count // 4)].start()
    for c in back:
        c.wait()


def encode(index, low, own, high, weights):
    count, slots = weights.shape[:2]
    blocks = own.shape[0] // BLOCK
    rim = low.shape[0] // BLOCK
    shaped = [v.reshape(-1, BLOCK, BLOCK) for v in (low, own, high)]
    return pl.pallas_call(
        encode_kernel,
        out_shape=jax.ShapeDtypeStruct((count * BLOCK, BLOCK), BF),
        grid_spec=pltpu.PrefetchScalarGridSpec(
            num_scalar_prefetch=1,
            grid=(1,),
            in_specs=[ANY, FAR, ANY, FAR],
            out_specs=ANY,
            scratch_shapes=[
                pltpu.VMEM((blocks + 2 * rim, BLOCK, BLOCK), BF),
                pltpu.VMEM((count, slots, BLOCK, BLOCK), BF),
                pltpu.VMEM((count * BLOCK, BLOCK), BF),
                pltpu.SemaphoreType.DMA((12 + count,)),
            ],
        ),
        compiler_params=params(56),
        cost_estimate=cost(540_000_000, 8_000_000),
        name="encode",
    )(index, *shaped, weights)


def project_kernel(
    order, s0, s1, s2, s3, s4, s5, s6, s7, gain, wq, wk, wv,
    queries, keys_values, share, ordered,
):
    step = pl.program_id(0)

    @pl.when(step == 0)
    def _():
        for p in range(8):
            ordered[p * BLOCK : (p + 1) * BLOCK] = jnp.concatenate(
                [w[order[p]] for w in (wq, wk, wv)], axis=1
            )

    raw = [s[...] for s in (s0, s1, s2, s3, s4, s5, s6, s7)]

    tile = share.shape[1]
    per = raw[0].shape[0] // tile
    for n in range(per):

        @pl.when(order[0] == step * per + n)
        def _():
            for p in range(8):
                share[order[p]] = raw[p][n * tile : (n + 1) * tile]

    pieces = [r.astype(F32) for r in raw]
    total = pieces[0]
    for x in pieces[1:]:
        total = total + x
    average = jnp.sum(total, axis=1, keepdims=True) * (1.0 / D)
    pieces = [x - average for x in pieces]
    total = pieces[0] * pieces[0]
    for x in pieces[1:]:
        total = total + x * x
    spread = lax.rsqrt(jnp.sum(total, axis=1, keepdims=True) * (1.0 / D) + EPSILON)
    normed = jnp.concatenate(
        [(x * spread * gain[order[p]]).astype(BF) for p, x in enumerate(pieces)], axis=1
    )
    made = dot(normed, ordered[...])
    queries[...] = (made[:, :BLOCK] * (HEAD_DIM**-0.5 * LOG2E)).astype(BF)
    keys_values[...] = made[:, BLOCK:].astype(BF)


def project(order, slots, gain, weights):
    rows = slots[0].shape[0]
    tile, steps = rows // 8, 4
    each = rows // steps
    full = pl.BlockSpec((each, BLOCK), lambda i, _: (i, 0))
    second = pl.BlockSpec((each, BLOCK), lambda i, _: (i + steps // 2, 0))
    return pl.pallas_call(
        project_kernel,
        out_shape=(
            jax.ShapeDtypeStruct((rows, BLOCK), BF),
            jax.ShapeDtypeStruct((rows, 2 * BLOCK), BF),
            jax.ShapeDtypeStruct((8, tile, BLOCK), BF),
        ),
        grid_spec=pltpu.PrefetchScalarGridSpec(
            num_scalar_prefetch=1,
            grid=(steps,),
            in_specs=[full, full, full, second, full, second, full, full]
            + [whole((8, 1, BLOCK))]
            + [whole((8, BLOCK, BLOCK))] * 3,
            out_specs=(
                full,
                pl.BlockSpec((each, 2 * BLOCK), lambda i, _: (i, 0)),
                whole((8, tile, BLOCK)),
            ),
            scratch_shapes=[pltpu.VMEM((D, 3 * BLOCK), BF)],
        ),
        compiler_params=params(56),
        name="project",
    )(order, *slots, gain.reshape(8, 1, BLOCK), *weights)


TILE = 256
SPAN = TILE + 2 * REACH
CHUNKS = SPAN // TILE


def attend_kernel(edges, queries, low, own, high, out, keys, values, scores, powers, sems):
    step = pl.program_id(0)
    rows = own.shape[0]

    @pl.when(step == 0)
    def _():
        copies = []
        for n, (part, start) in enumerate(
            ((low, 0), (own, REACH), (high, REACH + rows))
        ):
            for m, target in enumerate((keys, values)):
                copies.append(
                    pltpu.make_async_copy(
                        part.at[:, pl.ds(m * BLOCK, BLOCK)],
                        target.at[pl.ds(start, part.shape[0]), pl.ds(0, BLOCK)],
                        sems.at[2 * n + m],
                    )
                )
        for c in copies:
            c.start()
        first = lax.broadcasted_iota(jnp.int32, (keys.shape[0], BLOCK), 1) == 0
        row = lax.broadcasted_iota(jnp.int32, (keys.shape[0], BLOCK), 0)
        absent = ((row < REACH) & (edges[0] == 1)) | (
            (row >= REACH + rows) & (edges[1] == 1)
        )
        keys[:, BLOCK:] = jnp.where(first & absent, -1e30, 0.0).astype(BF)
        for c in copies:
            c.wait()
        both = values[:, :BLOCK]
        left = lax.broadcasted_iota(jnp.int32, both.shape, 1) < HEAD_DIM
        ones = jnp.ones_like(both)
        values[:, :BLOCK] = jnp.where(left, both, ones)
        values[:, BLOCK:] = jnp.where(left, ones, both)

    lane = lax.broadcasted_iota(jnp.int32, (TILE, BLOCK), 1)
    q = queries[...]
    zero = jnp.zeros_like(q)
    both = jnp.concatenate(
        [jnp.where(lane < HEAD_DIM, q, zero), jnp.where(lane < HEAD_DIM, zero, q)], axis=0
    )
    mark = jnp.where(
        lax.broadcasted_iota(jnp.int32, (2 * TILE, BLOCK), 1) == 0, 1.0, 0.0
    ).astype(BF)
    stacked = jnp.concatenate([both, mark], axis=1)
    row = lax.broadcasted_iota(jnp.int32, (2 * TILE, TILE), 0) & (TILE - 1)
    column = lax.broadcasted_iota(jnp.int32, (2 * TILE, TILE), 1)
    highest = jnp.full((2 * TILE, BLOCK), -1e30, F32)
    for c in range(CHUNKS):
        part = keys[pl.ds(pl.multiple_of((step + c) * TILE, TILE), TILE)]
        s = lax.dot_general(stacked, part, NT, preferred_element_type=F32)
        least = c * TILE - REACH
        gap = column - row + least
        if least - TILE < -WINDOW:
            s = jnp.where(gap >= -WINDOW, s, -1e30)
        if least + TILE > WINDOW:
            s = jnp.where(gap <= WINDOW, s, -1e30)
        scores[:, c * TILE : (c + 1) * TILE] = s
        highest = jnp.maximum(highest, jnp.maximum(s[:, :BLOCK], s[:, BLOCK:]))
    peak = jnp.max(highest, axis=1, keepdims=True)
    span = pl.ds(pl.multiple_of(step * TILE, TILE), SPAN)
    totals = []
    for h in range(2):
        rows_of = slice(h * TILE, (h + 1) * TILE)
        for c in range(CHUNKS):
            at = slice(c * TILE, (c + 1) * TILE)
            powers[rows_of, at] = jnp.exp2(scores[rows_of, at] - peak[rows_of]).astype(BF)
        totals.append(dot(powers[rows_of], values[span, h * BLOCK : (h + 1) * BLOCK]))
    made = jnp.where(lane < HEAD_DIM, totals[0], totals[1])
    sums = jnp.where(lane < HEAD_DIM, totals[1], totals[0])
    out[...] = (made / pltpu.roll(sums, HEAD_DIM, 1)).astype(BF)


def attend(edges, queries, low, own, high):
    rows = own.shape[0]
    return pl.pallas_call(
        attend_kernel,
        out_shape=jax.ShapeDtypeStruct((rows, BLOCK), BF),
        grid_spec=pltpu.PrefetchScalarGridSpec(
            num_scalar_prefetch=1,
            grid=(rows // TILE,),
            in_specs=[pl.BlockSpec((TILE, BLOCK), lambda i, _: (i, 0)), ANY, ANY, ANY],
            out_specs=pl.BlockSpec((TILE, BLOCK), lambda i, _: (i, 0)),
            scratch_shapes=[
                pltpu.VMEM((rows + 2 * REACH, 2 * BLOCK), BF),
                pltpu.VMEM((rows + 2 * REACH, 2 * BLOCK), BF),
                pltpu.VMEM((2 * TILE, SPAN), F32),
                pltpu.VMEM((2 * TILE, SPAN), BF),
                pltpu.SemaphoreType.DMA((6,)),
            ],
        ),
        compiler_params=params(56),
        name="attend",
    )(edges, queries, low, own, high)


ROWS_E = 64
ROWS_S = 64
ROWS_P = 16
PACK = ROWS_E + ROWS_S + ROWS_P


def pack_weights(position, expand, shrink, project_out):
    part = lax.dynamic_slice_in_dim(expand, position * 2 * ROWS_E, 2 * ROWS_E, 0)
    return jnp.concatenate(
        [
            jnp.concatenate([part[:ROWS_E], part[ROWS_E:]], axis=1),
            lax.dynamic_slice_in_dim(shrink, position * ROWS_S, ROWS_S, 0),
            lax.dynamic_slice_in_dim(project_out, position * ROWS_P, ROWS_P, 0),
        ],
        axis=0,
    )


def gelu(v):
    return 0.5 * v * (1.0 + jnp.tanh(0.7978845608028654 * (v + 0.044715 * v * v * v)))


def forward_kernel(table, *refs):
    parts = refs[:8]
    context, share, gain, out, expand, shrink, outward, sems = refs[8:]
    groups = ([], [], [])
    width = expand.shape[3]
    for n, part in enumerate(parts):
        where = table[8 + n]
        for side in range(2):
            slot = 1 - side if n % 4 == 3 else side

            def copy(group, source, target):
                groups[group].append(
                    pltpu.make_async_copy(source, target, sems.at[group, len(groups[group])])
                )

            copy(
                0,
                part.at[:, side, pl.ds(ROWS_E + ROWS_S, ROWS_P), :],
                outward.at[
                    :, slot, pl.ds(pl.multiple_of(where * ROWS_P, ROWS_P), ROWS_P), :
                ],
            )
            for piece in range(2):
                copy(
                    1,
                    part.at[:, side, pl.ds(0, ROWS_E), pl.ds(piece * width, width)],
                    expand.at[
                        :,
                        slot,
                        pl.ds(
                            pl.multiple_of(where * 2 * ROWS_E + piece * ROWS_E, ROWS_E), ROWS_E
                        ),
                        :,
                    ],
                )
            copy(
                2,
                part.at[:, side, pl.ds(ROWS_E, ROWS_S), :],
                shrink.at[:, slot, pl.ds(pl.multiple_of(where * ROWS_S, ROWS_S), ROWS_S), :],
            )
    for group in groups:
        for c in group:
            c.start()
    for c in groups[0]:
        c.wait()
    total = dot(context[table[0]], outward[0, 0])
    for p in range(1, 8):
        total = total + dot(context[table[p]], outward[p // 2, p % 2])
    start = jnp.concatenate([share[h] for h in range(8)], axis=1).astype(F32)
    middle = (start + total).astype(BF).astype(F32)
    average = jnp.mean(middle, axis=1, keepdims=True)
    centred = middle - average
    spread = jnp.mean(centred * centred, axis=1, keepdims=True)
    normed = (centred * lax.rsqrt(spread + EPSILON) * gain[...]).astype(BF)
    for c in groups[1]:
        c.wait()
    hidden = [gelu(dot(normed, expand[p // 2, p % 2])).astype(BF) for p in range(8)]
    for c in groups[2]:
        c.wait()
    total = middle
    for p in range(8):
        total = total + dot(hidden[p], shrink[p // 2, p % 2])
    done = total.astype(BF)
    for h in range(8):
        out[h] = done[:, h * BLOCK : (h + 1) * BLOCK]


def forward(table, parts, context, share, gain):
    rows = share.shape[1]
    width = D // 2
    return pl.pallas_call(
        forward_kernel,
        out_shape=jax.ShapeDtypeStruct((8, rows, BLOCK), BF),
        grid_spec=pltpu.PrefetchScalarGridSpec(
            num_scalar_prefetch=1,
            grid=(1,),
            in_specs=[ANY] * 8
            + [whole((8, rows, BLOCK)), whole((8, rows, BLOCK)), whole((1, D))],
            out_specs=whole((8, rows, BLOCK)),
            scratch_shapes=[
                pltpu.VMEM((4, 2, D, width), BF),
                pltpu.VMEM((4, 2, width, D), BF),
                pltpu.VMEM((4, 2, BLOCK, D), BF),
                pltpu.SemaphoreType.DMA((3, 32)),
            ],
        ),
        compiler_params=params(56),
        cost_estimate=cost(4_800_000_000, 20_000_000, 1_100_000),
        name="forward",
    )(table, *parts, context, share, gain.reshape(1, D))


EACH = 8


def decode_kernel(index, low, own, high, weights, back, sums, source, held, kept, sems):
    rim, slots = low.shape[0], weights.shape[1]
    steps = weights.shape[0] // EACH
    ahead = pieces_of(low, source, 0, 1, sems, 0)
    ahead += pieces_of(own, source, rim, 2, sems, 1)
    ahead += pieces_of(high, source, rim + own.shape[0], 1, sems, 3)
    blocks = pieces_of(weights, held, 0, 2 * steps, sems, 4)
    done = pieces_of(kept, back, 0, steps, sems, 4 + 2 * steps)
    for c in ahead + blocks:
        c.start()
    for c in ahead:
        c.wait()
    row = lax.broadcasted_iota(jnp.int32, (BLOCK, BLOCK), 0)
    column = lax.broadcasted_iota(jnp.int32, (BLOCK, BLOCK), 1)
    for step in range(steps):
        blocks[2 * step].wait()
        blocks[2 * step + 1].wait()
        kinds = []
        for b in range(step * EACH, (step + 1) * EACH):
            left = jnp.concatenate([held[b, k] for k in range(slots)], axis=1)
            right = jnp.concatenate([source[index[b, k]] for k in range(slots)], axis=0)
            made = dot(left, right)
            kept[b * BLOCK : (b + 1) * BLOCK] = made.astype(BF)
            kinds.append((made, made * made))
        done[step].start()
        held_sums = [
            jnp.sum(
                jnp.where(row == column, jnp.sum(kinds[b][n], axis=1, keepdims=True), 0.0),
                axis=0,
                keepdims=True,
            )
            for n in range(2)
            for b in range(EACH)
        ]
        sums[step] = jnp.concatenate(held_sums, axis=0).astype(BF)
    for c in done:
        c.wait()


def decode(index, low, own, high, weights):
    count, slots = weights.shape[:2]
    blocks = own.shape[0]
    rim = low.shape[0]
    steps = count // EACH
    return pl.pallas_call(
        decode_kernel,
        out_shape=(
            jax.ShapeDtypeStruct((count * BLOCK, BLOCK), BF),
            jax.ShapeDtypeStruct((steps, 2 * EACH, BLOCK), BF),
        ),
        grid_spec=pltpu.PrefetchScalarGridSpec(
            num_scalar_prefetch=1,
            grid=(1,),
            in_specs=[ANY, ANY, ANY, FAR],
            out_specs=(ANY, whole((steps, 2 * EACH, BLOCK))),
            scratch_shapes=[
                pltpu.VMEM((blocks + 2 * rim, BLOCK, BLOCK), BF),
                pltpu.VMEM((count, slots, BLOCK, BLOCK), BF),
                pltpu.VMEM((count * BLOCK, BLOCK), BF),
                pltpu.SemaphoreType.DMA((4 + 3 * steps,)),
            ],
        ),
        compiler_params=params(56),
        cost_estimate=cost(540_000_000, 10_000_000),
        name="decode",
    )(index, low, own, high, weights)


def finish_kernel(sums, back, state, gain, out, stats, kept, base, made, sems):
    steps = sums.shape[1]
    count = sums.shape[0]
    first = pieces_of(sums, stats, 0, count, sems, 0)
    backs = pieces_of(back, kept, 0, steps, sems, count)
    states = pieces_of(state, base, 0, steps, sems, count + steps)
    outs = pieces_of(made, out, 0, steps, sems, count + 2 * steps)
    for c in first:
        c.start()
    for a, b in zip(backs, states):
        a.start()
        b.start()
    depth = count * 2 * EACH
    row = lax.broadcasted_iota(jnp.int32, (depth, 2 * EACH * BLOCK), 0)
    column = lax.broadcasted_iota(jnp.int32, (depth, 2 * EACH * BLOCK), 1)
    pick = jnp.where((row % (2 * EACH)) == (column // BLOCK), 1.0 / D, 0.0).astype(BF)
    for c in first:
        c.wait()
    for step in range(steps):
        parts = jnp.concatenate([stats[h, step] for h in range(count)], axis=0)
        spread = lax.dot_general(parts, pick, TN, preferred_element_type=F32)
        backs[step].wait()
        states[step].wait()
        for b in range(EACH):
            at = (step * EACH + b) * BLOCK
            average = spread[:, b * BLOCK : (b + 1) * BLOCK]
            squares = spread[:, (EACH + b) * BLOCK : (EACH + b + 1) * BLOCK]
            scale = lax.rsqrt(squares - average * average + EPSILON) * gain[...]
            made[at : at + BLOCK] = (
                base[at : at + BLOCK].astype(F32)
                + (kept[at : at + BLOCK].astype(F32) - average) * scale
            ).astype(BF)
        outs[step].start()
    for c in outs:
        c.wait()


def finish(sums, back, state, gain):
    rows = state.shape[0]
    count, steps = sums.shape[:2]
    return pl.pallas_call(
        finish_kernel,
        out_shape=jax.ShapeDtypeStruct((rows, BLOCK), BF),
        grid_spec=pl.GridSpec(
            grid=(1,),
            in_specs=[ANY, ANY, FAR, whole((1, BLOCK))],
            out_specs=ANY,
            scratch_shapes=[
                pltpu.VMEM(sums.shape, BF),
                pltpu.VMEM((rows, BLOCK), BF),
                pltpu.VMEM((rows, BLOCK), BF),
                pltpu.VMEM((rows, BLOCK), BF),
                pltpu.SemaphoreType.DMA((count + 3 * steps,)),
            ],
        ),
        compiler_params=params(56),
        cost_estimate=cost(540_000_000, 8_000_000),
        name="finish",
    )(sums, back, state, gain.reshape(1, BLOCK))


def shifted(value, by):
    return lax.ppermute(value, "seq", [(i, i + by) for i in range(16) if 0 <= i + by < 16])


def among(value, axis, count, to):
    return lax.ppermute(value, axis, [(i, to(i)) for i in range(count)])


def along_z(i, by):
    return (i // 8) * 8 + ((i // 2 + by) % 4) * 2 + i % 2


UP = lambda v: among(v, "seq", 16, lambda i: along_z(i, 1))
DOWN = lambda v: among(v, "seq", 16, lambda i: along_z(i, -1))
ACROSS = lambda v: among(v, ("seq", "head"), 128, lambda i: i ^ 65)
TWIN = lambda v: among(v, "seq", 16, lambda i: i ^ 1)
NORTH = lambda v: among(v, "head", 8, lambda i: (i + 2) % 8)
SOUTH = lambda v: among(v, "head", 8, lambda i: (i - 2) % 8)
OVER = lambda v: among(v, "head", 8, lambda i: i ^ 1)


def on_device(
    grid_state,
    encode_index,
    encode_weights,
    first_gain,
    project_in,
    project_out,
    second_gain,
    expand_weights,
    shrink_weights,
    decode_index,
    decode_weights,
    output_gain,
):
    band = lax.axis_index("seq")
    bands = lax.axis_size("seq")
    me = lax.axis_index("head")
    mesh_blocks = encode_weights.shape[0]
    mesh_rows = mesh_blocks * BLOCK
    grid_blocks = grid_state.shape[0] // BLOCK
    rim = mesh_blocks * BLOCK
    core, place = band % 2, (band // 2 + 2 * (band // 8)) % 4
    position = place * 2 + core
    packed = pack_weights(position, expand_weights, shrink_weights, project_out)
    last, first, packed = lax.optimization_barrier(
        (grid_state[-rim:], grid_state[:rim], packed)
    )
    low = shifted(last, 1)
    high = shifted(first, -1)
    swapped, north, south = OVER(packed), NORTH(packed), SOUTH(packed)
    swapped_north, swapped_south = NORTH(swapped), SOUTH(swapped)
    far, swapped_far = NORTH(north), SOUTH(swapped_south)
    inward = [project_in[:, j, :].reshape(8, BLOCK, BLOCK) for j in range(3)]
    low, high, *inward = lax.optimization_barrier((low, high, *inward))
    mesh_start = encode(
        encode_index - (band * grid_blocks - mesh_blocks), low, grid_state, high, encode_weights
    )
    half = mesh_rows // 2
    mine = jnp.stack(
        [
            jnp.stack(pair)
            for pair in (
                (packed, swapped),
                (north, swapped_north),
                (south, swapped_south),
                (far, swapped_far),
            )
        ]
    )
    x, mine = lax.optimization_barrier((mesh_start, mine))
    up, down = UP(mine), DOWN(mine)
    y, xa, xb, mine = lax.optimization_barrier((OVER(x), NORTH(x), SOUTH(x), mine))
    across = ACROSS(mine)
    from_south = NORTH(jnp.concatenate([xa[:half], y]))
    from_north = SOUTH(jnp.concatenate([xb[half:], y]))
    xc = jnp.concatenate([from_south[:half], from_north[:half]])
    slots = (x, y, xa, from_south, xb, from_north, xc, OVER(xc))
    partner = me ^ 1
    order = jnp.stack(
        [me, partner] + [(v + by) % 8 for by in (6, 2, 4) for v in (me, partner)]
    ).astype(jnp.int32)
    queries, keys_values, share = project(order, slots, first_gain, inward)
    upper, lower, up, down = lax.optimization_barrier(
        (keys_values[mesh_rows - REACH :], keys_values[:REACH], up, down)
    )
    below = shifted(upper, 1)
    above = shifted(lower, -1)
    edges = jnp.stack([band == 0, band == bands - 1]).astype(jnp.int32)
    context = attend(edges, queries, below, keys_values, above)
    context, *here = lax.optimization_barrier((context, mine, up, down, across))
    parts = here + [TWIN(v) for v in here]
    context = lax.all_to_all(
        context.reshape(8, mesh_rows // 8, BLOCK), "head", 0, 0, tiled=True
    )
    places = [
        ((place + by) % 4) * 2 + side for side in (core, 1 - core) for by in (0, 3, 1, 2)
    ]
    table = jnp.concatenate([order, jnp.stack(places).astype(jnp.int32)])
    mesh_end = forward(table, parts, context, share, second_gain)
    mesh_end = lax.all_to_all(mesh_end, "head", 0, 0, tiled=True)
    mesh_end = mesh_end.reshape(mesh_blocks, BLOCK, BLOCK)
    edge = mesh_blocks // 2
    back, sums = decode(
        decode_index - (band * mesh_blocks - edge),
        shifted(mesh_end[-edge:], 1),
        mesh_end,
        shifted(mesh_end[:edge], -1),
        decode_weights,
    )
    sums = lax.all_to_all(
        jnp.broadcast_to(sums, (8, *sums.shape)), "head", 0, 0, tiled=True
    )
    return finish(sums, back, grid_state, output_gain)


def solution(mesh):
    in_specs = (
        P("seq", "head"),
        P("seq", None),
        P("seq", None, None, None),
        P(),
        P(None, None, "head"),
        P("head", None),
        P(),
        P(None, "head"),
        P("head", None),
        P("seq", None),
        P("seq", None, None, None),
        P("head"),
    )
    return jax.shard_map(
        on_device, mesh=mesh, in_specs=in_specs, out_specs=P("seq", "head"), check_vma=False
    )
```

```python
import jax
import jax.numpy as jnp
from jax import lax
from jax.experimental import pallas as pl
from jax.experimental.pallas import tpu as pltpu
from jax.sharding import PartitionSpec as P

D = 1024
HEAD_DIM = 64
WINDOW = 1120
REACH = 1152
BLOCK = 128
EPSILON = 1e-05
LOG2E = 1.4426950408889634
BF = jnp.bfloat16
F32 = jnp.float32
NT = (((1,), (1,)), ((), ()))
TN = (((0,), (0,)), ((), ()))
MIB = 1 << 20


def params(mib):
    return pltpu.CompilerParams(
        dimension_semantics=("arbitrary",), vmem_limit_bytes=mib * MIB
    )


def dot(a, b):
    return jnp.dot(a, b, preferred_element_type=F32)


def cost(flops, moved, powers=0):
    return pl.CostEstimate(flops=flops, bytes_accessed=moved, transcendentals=powers)


ANY = pl.BlockSpec(memory_space=pl.ANY)
FAR = pl.BlockSpec(memory_space=pltpu.HBM)


def whole(shape):
    return pl.BlockSpec(shape, lambda i, *_: (0,) * len(shape))


def pieces_of(ref, target, start, count, sems, first):
    length = ref.shape[0] // count
    return [
        pltpu.make_async_copy(
            ref.at[pl.ds(n * length, length)],
            target.at[pl.ds(start + n * length, length)],
            sems.at[first + n],
        )
        for n in range(count)
    ]


def encode_kernel(index, low, own, high, weights, out, source, held, made, sems):
    rim, slots = low.shape[0], weights.shape[1]
    ahead = pieces_of(low, source, 0, 2, sems, 0)
    ahead += pieces_of(own, source, rim, 4, sems, 2)
    ahead += pieces_of(high, source, rim + own.shape[0], 2, sems, 6)
    count = weights.shape[0]
    blocks = pieces_of(weights, held, 0, count, sems, 8)
    back = pieces_of(made, out, 0, 4, sems, 8 + count)
    for c in ahead + blocks:
        c.start()
    for c in ahead:
        c.wait()
    for b in range(count):
        blocks[b].wait()
        left = jnp.concatenate([held[b, k] for k in range(slots)], axis=1)
        right = jnp.concatenate([source[index[b, k]] for k in range(slots)], axis=0)
        made[b * BLOCK : (b + 1) * BLOCK] = dot(left, right).astype(BF)
        if (b + 1) % (count // 4) == 0:
            back[b // (count // 4)].start()
    for c in back:
        c.wait()


def encode(index, low, own, high, weights):
    count, slots = weights.shape[:2]
    blocks = own.shape[0] // BLOCK
    rim = low.shape[0] // BLOCK
    shaped = [v.reshape(-1, BLOCK, BLOCK) for v in (low, own, high)]
    return pl.pallas_call(
        encode_kernel,
        out_shape=jax.ShapeDtypeStruct((count * BLOCK, BLOCK), BF),
        grid_spec=pltpu.PrefetchScalarGridSpec(
            num_scalar_prefetch=1,
            grid=(1,),
            in_specs=[ANY, FAR, ANY, FAR],
            out_specs=ANY,
            scratch_shapes=[
                pltpu.VMEM((blocks + 2 * rim, BLOCK, BLOCK), BF),
                pltpu.VMEM((count, slots, BLOCK, BLOCK), BF),
                pltpu.VMEM((count * BLOCK, BLOCK), BF),
                pltpu.SemaphoreType.DMA((12 + count,)),
            ],
        ),
        compiler_params=params(56),
        cost_estimate=cost(540_000_000, 8_000_000),
        name="encode",
    )(index, *shaped, weights)


def project_kernel(
    order, s0, s1, s2, s3, s4, s5, s6, s7, gain, wq, wk, wv,
    queries, keys_values, share, ordered,
):
    step = pl.program_id(0)

    @pl.when(step == 0)
    def _():
        for p in range(8):
            ordered[p * BLOCK : (p + 1) * BLOCK] = jnp.concatenate(
                [w[order[p]] for w in (wq, wk, wv)], axis=1
            )

    raw = [s[...] for s in (s0, s1, s2, s3, s4, s5, s6, s7)]

    tile = share.shape[1]
    per = raw[0].shape[0] // tile
    for n in range(per):

        @pl.when(order[0] == step * per + n)
        def _():
            for p in range(8):
                share[order[p]] = raw[p][n * tile : (n + 1) * tile]

    pieces = [r.astype(F32) for r in raw]
    total = pieces[0]
    for x in pieces[1:]:
        total = total + x
    average = jnp.sum(total, axis=1, keepdims=True) * (1.0 / D)
    pieces = [x - average for x in pieces]
    total = pieces[0] * pieces[0]
    for x in pieces[1:]:
        total = total + x * x
    spread = lax.rsqrt(jnp.sum(total, axis=1, keepdims=True) * (1.0 / D) + EPSILON)
    normed = jnp.concatenate(
        [(x * spread * gain[order[p]]).astype(BF) for p, x in enumerate(pieces)], axis=1
    )
    made = dot(normed, ordered[...])
    queries[...] = (made[:, :BLOCK] * (HEAD_DIM**-0.5 * LOG2E)).astype(BF)
    keys_values[...] = made[:, BLOCK:].astype(BF)


def project(order, slots, gain, weights):
    rows = slots[0].shape[0]
    tile, steps = rows // 8, 4
    each = rows // steps
    full = pl.BlockSpec((each, BLOCK), lambda i, _: (i, 0))
    second = pl.BlockSpec((each, BLOCK), lambda i, _: (i + steps // 2, 0))
    return pl.pallas_call(
        project_kernel,
        out_shape=(
            jax.ShapeDtypeStruct((rows, BLOCK), BF),
            jax.ShapeDtypeStruct((rows, 2 * BLOCK), BF),
            jax.ShapeDtypeStruct((8, tile, BLOCK), BF),
        ),
        grid_spec=pltpu.PrefetchScalarGridSpec(
            num_scalar_prefetch=1,
            grid=(steps,),
            in_specs=[full, full, full, second, full, second, full, full]
            + [whole((8, 1, BLOCK))]
            + [whole((8, BLOCK, BLOCK))] * 3,
            out_specs=(
                full,
                pl.BlockSpec((each, 2 * BLOCK), lambda i, _: (i, 0)),
                whole((8, tile, BLOCK)),
            ),
            scratch_shapes=[pltpu.VMEM((D, 3 * BLOCK), BF)],
        ),
        compiler_params=params(56),
        name="project",
    )(order, *slots, gain.reshape(8, 1, BLOCK), *weights)


TILE = 256
SPAN = TILE + 2 * REACH
CHUNKS = SPAN // TILE


def attend_kernel(edges, queries, low, own, high, out, keys, values, scores, powers, sems):
    step = pl.program_id(0)
    rows = own.shape[0]

    @pl.when(step == 0)
    def _():
        copies = []
        for n, (part, start) in enumerate(
            ((low, 0), (own, REACH), (high, REACH + rows))
        ):
            for m, target in enumerate((keys, values)):
                copies.append(
                    pltpu.make_async_copy(
                        part.at[:, pl.ds(m * BLOCK, BLOCK)],
                        target.at[pl.ds(start, part.shape[0]), pl.ds(0, BLOCK)],
                        sems.at[2 * n + m],
                    )
                )
        for c in copies:
            c.start()
        first = lax.broadcasted_iota(jnp.int32, (keys.shape[0], BLOCK), 1) == 0
        row = lax.broadcasted_iota(jnp.int32, (keys.shape[0], BLOCK), 0)
        absent = ((row < REACH) & (edges[0] == 1)) | (
            (row >= REACH + rows) & (edges[1] == 1)
        )
        keys[:, BLOCK:] = jnp.where(first & absent, -1e30, 0.0).astype(BF)
        for c in copies:
            c.wait()
        both = values[:, :BLOCK]
        left = lax.broadcasted_iota(jnp.int32, both.shape, 1) < HEAD_DIM
        ones = jnp.ones_like(both)
        values[:, :BLOCK] = jnp.where(left, both, ones)
        values[:, BLOCK:] = jnp.where(left, ones, both)

    lane = lax.broadcasted_iota(jnp.int32, (TILE, BLOCK), 1)
    q = queries[...]
    zero = jnp.zeros_like(q)
    both = jnp.concatenate(
        [jnp.where(lane < HEAD_DIM, q, zero), jnp.where(lane < HEAD_DIM, zero, q)], axis=0
    )
    mark = jnp.where(
        lax.broadcasted_iota(jnp.int32, (2 * TILE, BLOCK), 1) == 0, 1.0, 0.0
    ).astype(BF)
    stacked = jnp.concatenate([both, mark], axis=1)
    row = lax.broadcasted_iota(jnp.int32, (2 * TILE, TILE), 0) & (TILE - 1)
    column = lax.broadcasted_iota(jnp.int32, (2 * TILE, TILE), 1)
    highest = jnp.full((2 * TILE, BLOCK), -1e30, F32)
    for c in range(CHUNKS):
        part = keys[pl.ds(pl.multiple_of((step + c) * TILE, TILE), TILE)]
        s = lax.dot_general(stacked, part, NT, preferred_element_type=F32)
        least = c * TILE - REACH
        gap = column - row + least
        if least - TILE < -WINDOW:
            s = jnp.where(gap >= -WINDOW, s, -1e30)
        if least + TILE > WINDOW:
            s = jnp.where(gap <= WINDOW, s, -1e30)
        scores[:, c * TILE : (c + 1) * TILE] = s
        highest = jnp.maximum(highest, jnp.maximum(s[:, :BLOCK], s[:, BLOCK:]))
    peak = jnp.max(highest, axis=1, keepdims=True)
    span = pl.ds(pl.multiple_of(step * TILE, TILE), SPAN)
    totals = []
    for h in range(2):
        rows_of = slice(h * TILE, (h + 1) * TILE)
        for c in range(CHUNKS):
            at = slice(c * TILE, (c + 1) * TILE)
            powers[rows_of, at] = jnp.exp2(scores[rows_of, at] - peak[rows_of]).astype(BF)
        totals.append(dot(powers[rows_of], values[span, h * BLOCK : (h + 1) * BLOCK]))
    made = jnp.where(lane < HEAD_DIM, totals[0], totals[1])
    sums = jnp.where(lane < HEAD_DIM, totals[1], totals[0])
    out[...] = (made / pltpu.roll(sums, HEAD_DIM, 1)).astype(BF)


def attend(edges, queries, low, own, high):
    rows = own.shape[0]
    return pl.pallas_call(
        attend_kernel,
        out_shape=jax.ShapeDtypeStruct((rows, BLOCK), BF),
        grid_spec=pltpu.PrefetchScalarGridSpec(
            num_scalar_prefetch=1,
            grid=(rows // TILE,),
            in_specs=[pl.BlockSpec((TILE, BLOCK), lambda i, _: (i, 0)), ANY, ANY, ANY],
            out_specs=pl.BlockSpec((TILE, BLOCK), lambda i, _: (i, 0)),
            scratch_shapes=[
                pltpu.VMEM((rows + 2 * REACH, 2 * BLOCK), BF),
                pltpu.VMEM((rows + 2 * REACH, 2 * BLOCK), BF),
                pltpu.VMEM((2 * TILE, SPAN), F32),
                pltpu.VMEM((2 * TILE, SPAN), BF),
                pltpu.SemaphoreType.DMA((6,)),
            ],
        ),
        compiler_params=params(56),
        name="attend",
    )(edges, queries, low, own, high)


ROWS_E = 64
ROWS_S = 64
ROWS_P = 16
PACK = ROWS_E + ROWS_S + ROWS_P


def pack_weights(position, expand, shrink, project_out):
    part = lax.dynamic_slice_in_dim(expand, position * 2 * ROWS_E, 2 * ROWS_E, 0)
    return jnp.concatenate(
        [
            jnp.concatenate([part[:ROWS_E], part[ROWS_E:]], axis=1),
            lax.dynamic_slice_in_dim(shrink, position * ROWS_S, ROWS_S, 0),
            lax.dynamic_slice_in_dim(project_out, position * ROWS_P, ROWS_P, 0),
        ],
        axis=0,
    )


def gelu(v):
    return 0.5 * v * (1.0 + jnp.tanh(0.7978845608028654 * (v + 0.044715 * v * v * v)))


def forward_kernel(table, *refs):
    parts = refs[:10]
    context, share, gain, out, expand, shrink, outward, sems = refs[10:]
    groups = ([], [], [])
    width = expand.shape[3]

    def copy(group, source, target):
        groups[group].append(
            pltpu.make_async_copy(source, target, sems.at[group, len(groups[group])])
        )

    for n, part in enumerate(parts):
        place = table[8 + 4 * (n // 5) + min(n % 5, 3)]
        pairs = pl.ds(2 if n % 5 == 4 else 0, part.shape[0])
        swaps = ((0, 1), (1, 0)) if n % 5 >= 3 else ((slice(None), slice(None)),)
        for side, slot in swaps:
            copy(
                0,
                part.at[:, side, pl.ds(ROWS_E + ROWS_S, ROWS_P), :],
                outward.at[
                    pairs, slot, pl.ds(pl.multiple_of(place * ROWS_P, ROWS_P), ROWS_P), :
                ],
            )
            for piece in range(2):
                start = pl.multiple_of(place * 2 * ROWS_E + piece * ROWS_E, ROWS_E)
                copy(
                    1,
                    part.at[:, side, pl.ds(0, ROWS_E), pl.ds(piece * width, width)],
                    expand.at[pairs, slot, pl.ds(start, ROWS_E), :],
                )
            copy(
                2,
                part.at[:, side, pl.ds(ROWS_E, ROWS_S), :],
                shrink.at[
                    pairs, slot, pl.ds(pl.multiple_of(place * ROWS_S, ROWS_S), ROWS_S), :
                ],
            )
    for group in groups:
        for c in group:
            c.start()
    for c in groups[0]:
        c.wait()
    total = dot(context[table[0]], outward[0, 0])
    for p in range(1, 8):
        total = total + dot(context[table[p]], outward[p // 2, p % 2])
    start = jnp.concatenate([share[h] for h in range(8)], axis=1).astype(F32)
    middle = (start + total).astype(BF).astype(F32)
    average = jnp.mean(middle, axis=1, keepdims=True)
    centred = middle - average
    spread = jnp.mean(centred * centred, axis=1, keepdims=True)
    normed = (centred * lax.rsqrt(spread + EPSILON) * gain[...]).astype(BF)
    for c in groups[1]:
        c.wait()
    hidden = [gelu(dot(normed, expand[p // 2, p % 2])).astype(BF) for p in range(8)]
    for c in groups[2]:
        c.wait()
    total = middle
    for p in range(8):
        total = total + dot(hidden[p], shrink[p // 2, p % 2])
    done = total.astype(BF)
    for h in range(8):
        out[h] = done[:, h * BLOCK : (h + 1) * BLOCK]


def forward(table, parts, context, share, gain):
    rows = share.shape[1]
    width = D // 2
    return pl.pallas_call(
        forward_kernel,
        out_shape=jax.ShapeDtypeStruct((8, rows, BLOCK), BF),
        grid_spec=pltpu.PrefetchScalarGridSpec(
            num_scalar_prefetch=1,
            grid=(1,),
            in_specs=[ANY] * 10
            + [whole((8, rows, BLOCK)), whole((8, rows, BLOCK)), whole((1, D))],
            out_specs=whole((8, rows, BLOCK)),
            scratch_shapes=[
                pltpu.VMEM((4, 2, D, width), BF),
                pltpu.VMEM((4, 2, width, D), BF),
                pltpu.VMEM((4, 2, BLOCK, D), BF),
                pltpu.SemaphoreType.DMA((3, 32)),
            ],
        ),
        compiler_params=params(56),
        cost_estimate=cost(4_800_000_000, 20_000_000, 1_100_000),
        name="forward",
    )(table, *parts, context, share, gain.reshape(1, D))


EACH = 8


def decode_kernel(index, low, own, high, weights, back, sums, source, held, kept, sems):
    rim, slots = low.shape[0], weights.shape[1]
    steps = weights.shape[0] // EACH
    ahead = pieces_of(low, source, 0, 1, sems, 0)
    ahead += pieces_of(own, source, rim, 2, sems, 1)
    ahead += pieces_of(high, source, rim + own.shape[0], 1, sems, 3)
    blocks = pieces_of(weights, held, 0, 2 * steps, sems, 4)
    done = pieces_of(kept, back, 0, steps, sems, 4 + 2 * steps)
    for c in ahead + blocks:
        c.start()
    for c in ahead:
        c.wait()
    row = lax.broadcasted_iota(jnp.int32, (BLOCK, BLOCK), 0)
    column = lax.broadcasted_iota(jnp.int32, (BLOCK, BLOCK), 1)
    for step in range(steps):
        blocks[2 * step].wait()
        blocks[2 * step + 1].wait()
        kinds = []
        for b in range(step * EACH, (step + 1) * EACH):
            left = jnp.concatenate([held[b, k] for k in range(slots)], axis=1)
            right = jnp.concatenate([source[index[b, k]] for k in range(slots)], axis=0)
            made = dot(left, right)
            kept[b * BLOCK : (b + 1) * BLOCK] = made.astype(BF)
            kinds.append((made, made * made))
        done[step].start()
        held_sums = [
            jnp.sum(
                jnp.where(row == column, jnp.sum(kinds[b][n], axis=1, keepdims=True), 0.0),
                axis=0,
                keepdims=True,
            )
            for n in range(2)
            for b in range(EACH)
        ]
        sums[step] = jnp.concatenate(held_sums, axis=0).astype(BF)
    for c in done:
        c.wait()


def decode(index, low, own, high, weights):
    count, slots = weights.shape[:2]
    blocks = own.shape[0]
    rim = low.shape[0]
    steps = count // EACH
    return pl.pallas_call(
        decode_kernel,
        out_shape=(
            jax.ShapeDtypeStruct((count * BLOCK, BLOCK), BF),
            jax.ShapeDtypeStruct((steps, 2 * EACH, BLOCK), BF),
        ),
        grid_spec=pltpu.PrefetchScalarGridSpec(
            num_scalar_prefetch=1,
            grid=(1,),
            in_specs=[ANY, ANY, ANY, FAR],
            out_specs=(ANY, whole((steps, 2 * EACH, BLOCK))),
            scratch_shapes=[
                pltpu.VMEM((blocks + 2 * rim, BLOCK, BLOCK), BF),
                pltpu.VMEM((count, slots, BLOCK, BLOCK), BF),
                pltpu.VMEM((count * BLOCK, BLOCK), BF),
                pltpu.SemaphoreType.DMA((4 + 3 * steps,)),
            ],
        ),
        compiler_params=params(56),
        cost_estimate=cost(540_000_000, 10_000_000),
        name="decode",
    )(index, low, own, high, weights)


def finish_kernel(sums, back, state, gain, out, stats, kept, base, made, sems):
    steps = sums.shape[1]
    count = sums.shape[0]
    first = pieces_of(sums, stats, 0, count, sems, 0)
    backs = pieces_of(back, kept, 0, steps, sems, count)
    states = pieces_of(state, base, 0, steps, sems, count + steps)
    outs = pieces_of(made, out, 0, steps, sems, count + 2 * steps)
    for c in first:
        c.start()
    for a, b in zip(backs, states):
        a.start()
        b.start()
    depth = count * 2 * EACH
    row = lax.broadcasted_iota(jnp.int32, (depth, 2 * EACH * BLOCK), 0)
    column = lax.broadcasted_iota(jnp.int32, (depth, 2 * EACH * BLOCK), 1)
    pick = jnp.where((row % (2 * EACH)) == (column // BLOCK), 1.0 / D, 0.0).astype(BF)
    for c in first:
        c.wait()
    for step in range(steps):
        parts = jnp.concatenate([stats[h, step] for h in range(count)], axis=0)
        spread = lax.dot_general(parts, pick, TN, preferred_element_type=F32)
        backs[step].wait()
        states[step].wait()
        for b in range(EACH):
            at = (step * EACH + b) * BLOCK
            average = spread[:, b * BLOCK : (b + 1) * BLOCK]
            squares = spread[:, (EACH + b) * BLOCK : (EACH + b + 1) * BLOCK]
            scale = lax.rsqrt(squares - average * average + EPSILON) * gain[...]
            made[at : at + BLOCK] = (
                base[at : at + BLOCK].astype(F32)
                + (kept[at : at + BLOCK].astype(F32) - average) * scale
            ).astype(BF)
        outs[step].start()
    for c in outs:
        c.wait()


def finish(sums, back, state, gain):
    rows = state.shape[0]
    count, steps = sums.shape[:2]
    return pl.pallas_call(
        finish_kernel,
        out_shape=jax.ShapeDtypeStruct((rows, BLOCK), BF),
        grid_spec=pl.GridSpec(
            grid=(1,),
            in_specs=[ANY, ANY, FAR, whole((1, BLOCK))],
            out_specs=ANY,
            scratch_shapes=[
                pltpu.VMEM(sums.shape, BF),
                pltpu.VMEM((rows, BLOCK), BF),
                pltpu.VMEM((rows, BLOCK), BF),
                pltpu.VMEM((rows, BLOCK), BF),
                pltpu.SemaphoreType.DMA((count + 3 * steps,)),
            ],
        ),
        compiler_params=params(56),
        cost_estimate=cost(540_000_000, 8_000_000),
        name="finish",
    )(sums, back, state, gain.reshape(1, BLOCK))


def shifted(value, by):
    return lax.ppermute(value, "seq", [(i, i + by) for i in range(16) if 0 <= i + by < 16])


def among(value, axis, count, to):
    return lax.ppermute(value, axis, [(i, to(i)) for i in range(count)])


def along_z(i, by):
    return (i // 8) * 8 + ((i // 2 + by) % 4) * 2 + i % 2


UP = lambda v: among(v, "seq", 16, lambda i: along_z(i, 1))
DOWN = lambda v: among(v, "seq", 16, lambda i: along_z(i, -1))
ACROSS = lambda v: among(v, ("seq", "head"), 128, lambda i: i ^ 65)
TWIN = lambda v: among(v, "seq", 16, lambda i: i ^ 1)
NORTH = lambda v: among(v, "head", 8, lambda i: (i + 2) % 8)
SOUTH = lambda v: among(v, "head", 8, lambda i: (i - 2) % 8)
OVER = lambda v: among(v, "head", 8, lambda i: i ^ 1)


def on_device(
    grid_state,
    encode_index,
    encode_weights,
    first_gain,
    project_in,
    project_out,
    second_gain,
    expand_weights,
    shrink_weights,
    decode_index,
    decode_weights,
    output_gain,
):
    band = lax.axis_index("seq")
    bands = lax.axis_size("seq")
    me = lax.axis_index("head")
    mesh_blocks = encode_weights.shape[0]
    mesh_rows = mesh_blocks * BLOCK
    grid_blocks = grid_state.shape[0] // BLOCK
    rim = mesh_blocks * BLOCK
    core, place = band % 2, (band // 2 + 2 * (band // 8)) % 4
    position = place * 2 + core
    packed = pack_weights(position, expand_weights, shrink_weights, project_out)
    last, first, packed = lax.optimization_barrier(
        (grid_state[-rim:], grid_state[:rim], packed)
    )
    low = shifted(last, 1)
    high = shifted(first, -1)
    swapped, north, south = OVER(packed), NORTH(packed), SOUTH(packed)
    swapped_north, swapped_south = NORTH(swapped), SOUTH(swapped)
    far, swapped_far = NORTH(north), SOUTH(swapped_south)
    inward = [project_in[:, j, :].reshape(8, BLOCK, BLOCK) for j in range(3)]
    low, high, *inward = lax.optimization_barrier((low, high, *inward))
    mesh_start = encode(
        encode_index - (band * grid_blocks - mesh_blocks), low, grid_state, high, encode_weights
    )
    half = mesh_rows // 2
    mine = jnp.stack(
        [
            jnp.stack(pair)
            for pair in (
                (packed, swapped),
                (north, swapped_north),
                (south, swapped_south),
                (far, swapped_far),
            )
        ]
    )
    x, mine = lax.optimization_barrier((mesh_start, mine))
    up, down = UP(mine), DOWN(mine)
    y, xa, xb, mine = lax.optimization_barrier((OVER(x), NORTH(x), SOUTH(x), mine))
    across = ACROSS(mine[:2])
    from_south = NORTH(jnp.concatenate([xa[:half], y]))
    from_north = SOUTH(jnp.concatenate([xb[half:], y]))
    xc = jnp.concatenate([from_south[:half], from_north[:half]])
    slots = (x, y, xa, from_south, xb, from_north, xc, OVER(xc))
    partner = me ^ 1
    order = jnp.stack(
        [me, partner] + [(v + by) % 8 for by in (6, 2, 4) for v in (me, partner)]
    ).astype(jnp.int32)
    queries, keys_values, share = project(order, slots, first_gain, inward)
    upper, lower, up, down, across = lax.optimization_barrier(
        (keys_values[mesh_rows - REACH :], keys_values[:REACH], up, down, across)
    )
    below, above, late = lax.optimization_barrier(
        (shifted(upper, 1), shifted(lower, -1), mine[2:])
    )
    edges = jnp.stack([band == 0, band == bands - 1]).astype(jnp.int32)
    context = attend(edges, queries, below, keys_values, above)
    context, *here = lax.optimization_barrier((context, mine, up, down, across, ACROSS(late)))
    parts = here + [TWIN(v) for v in here]
    context = lax.all_to_all(
        context.reshape(8, mesh_rows // 8, BLOCK), "head", 0, 0, tiled=True
    )
    places = [
        ((place + by) % 4) * 2 + side for side in (core, 1 - core) for by in (0, 3, 1, 2)
    ]
    table = jnp.concatenate([order, jnp.stack(places).astype(jnp.int32)])
    mesh_end = forward(table, parts, context, share, second_gain)
    mesh_end = lax.all_to_all(mesh_end, "head", 0, 0, tiled=True)
    mesh_end = mesh_end.reshape(mesh_blocks, BLOCK, BLOCK)
    edge = mesh_blocks // 2
    back, sums = decode(
        decode_index - (band * mesh_blocks - edge),
        shifted(mesh_end[-edge:], 1),
        mesh_end,
        shifted(mesh_end[:edge], -1),
        decode_weights,
    )
    sums = lax.all_to_all(
        jnp.broadcast_to(sums, (8, *sums.shape)), "head", 0, 0, tiled=True
    )
    return finish(sums, back, grid_state, output_gain)


def solution(mesh):
    in_specs = (
        P("seq", "head"),
        P("seq", None),
        P("seq", None, None, None),
        P(),
        P(None, None, "head"),
        P("head", None),
        P(),
        P(None, "head"),
        P("head", None),
        P("seq", None),
        P("seq", None, None, None),
        P("head"),
    )
    return jax.shard_map(
        on_device, mesh=mesh, in_specs=in_specs, out_specs=P("seq", "head"), check_vma=False
    )
```

```python
import jax
import jax.numpy as jnp
from jax import lax
from jax.experimental import pallas as pl
from jax.experimental.pallas import tpu as pltpu
from jax.sharding import PartitionSpec as P

D = 1024
HEAD_DIM = 64
WINDOW = 1120
REACH = 1152
BLOCK = 128
EPSILON = 1e-05
LOG2E = 1.4426950408889634
BF = jnp.bfloat16
F32 = jnp.float32
NT = (((1,), (1,)), ((), ()))
TN = (((0,), (0,)), ((), ()))
MIB = 1 << 20


def params(mib):
    return pltpu.CompilerParams(
        dimension_semantics=("arbitrary",), vmem_limit_bytes=mib * MIB
    )


def dot(a, b):
    return jnp.dot(a, b, preferred_element_type=F32)


def cost(flops, moved, powers=0):
    return pl.CostEstimate(flops=flops, bytes_accessed=moved, transcendentals=powers)


ANY = pl.BlockSpec(memory_space=pl.ANY)
FAR = pl.BlockSpec(memory_space=pltpu.HBM)


def whole(shape):
    return pl.BlockSpec(shape, lambda i, *_: (0,) * len(shape))


def pieces_of(ref, target, start, count, sems, first):
    length = ref.shape[0] // count
    return [
        pltpu.make_async_copy(
            ref.at[pl.ds(n * length, length)],
            target.at[pl.ds(start + n * length, length)],
            sems.at[first + n],
        )
        for n in range(count)
    ]


def encode_kernel(index, low, own, high, weights, out, source, held, made, sems):
    rim, slots = low.shape[0], weights.shape[1]
    ahead = pieces_of(low, source, 0, 2, sems, 0)
    ahead += pieces_of(own, source, rim, 4, sems, 2)
    ahead += pieces_of(high, source, rim + own.shape[0], 2, sems, 6)
    count = weights.shape[0]
    blocks = pieces_of(weights, held, 0, count, sems, 8)
    back = pieces_of(made, out, 0, 4, sems, 8 + count)
    for c in ahead + blocks:
        c.start()
    for c in ahead:
        c.wait()
    for b in range(count):
        if b % 4 == 0:
            for c in blocks[b : b + 4]:
                c.wait()
        left = jnp.concatenate([held[b, k] for k in range(slots)], axis=1)
        right = jnp.concatenate([source[index[b, k]] for k in range(slots)], axis=0)
        made[b * BLOCK : (b + 1) * BLOCK] = dot(left, right).astype(BF)
        if (b + 1) % (count // 4) == 0:
            back[b // (count // 4)].start()
    for c in back:
        c.wait()


def encode(index, low, own, high, weights):
    count, slots = weights.shape[:2]
    blocks = own.shape[0] // BLOCK
    rim = low.shape[0] // BLOCK
    shaped = [v.reshape(-1, BLOCK, BLOCK) for v in (low, own, high)]
    return pl.pallas_call(
        encode_kernel,
        out_shape=jax.ShapeDtypeStruct((count * BLOCK, BLOCK), BF),
        grid_spec=pltpu.PrefetchScalarGridSpec(
            num_scalar_prefetch=1,
            grid=(1,),
            in_specs=[ANY, FAR, ANY, FAR],
            out_specs=ANY,
            scratch_shapes=[
                pltpu.VMEM((blocks + 2 * rim, BLOCK, BLOCK), BF),
                pltpu.VMEM((count, slots, BLOCK, BLOCK), BF),
                pltpu.VMEM((count * BLOCK, BLOCK), BF),
                pltpu.SemaphoreType.DMA((12 + count,)),
            ],
        ),
        compiler_params=params(56),
        cost_estimate=cost(540_000_000, 8_000_000),
        name="encode",
    )(index, *shaped, weights)


def project_kernel(
    order, s0, s1, s2, s3, s4, s5, s6, s7, gain, wq, wk, wv,
    queries, keys_values, share, ordered, normed,
):
    step = pl.program_id(0)

    @pl.when(step == 0)
    def _():
        for p in range(8):
            ordered[p * BLOCK : (p + 1) * BLOCK] = jnp.concatenate(
                [w[order[p]] for w in (wq, wk, wv)], axis=1
            )

    slots = (s0, s1, s2, s3, s4, s5, s6, s7)
    rows = s0.shape[0]
    tile = share.shape[1]
    for n in range(rows // tile):

        @pl.when(order[0] == step * (rows // tile) + n)
        def _():
            for p in range(8):
                share[order[p]] = slots[p][n * tile : (n + 1) * tile]

    gains = [gain[order[p]] for p in range(8)]
    few = 32
    for n in range(rows // few):
        at = slice(n * few, (n + 1) * few)
        pieces = [s[at].astype(F32) for s in slots]
        total = pieces[0]
        for x in pieces[1:]:
            total = total + x
        average = jnp.sum(total, axis=1, keepdims=True) * (1.0 / D)
        pieces = [x - average for x in pieces]
        total = pieces[0] * pieces[0]
        for x in pieces[1:]:
            total = total + x * x
        spread = lax.rsqrt(jnp.sum(total, axis=1, keepdims=True) * (1.0 / D) + EPSILON)
        for p, x in enumerate(pieces):
            normed[at, p * BLOCK : (p + 1) * BLOCK] = (x * spread * gains[p]).astype(BF)
    made = dot(normed[...], ordered[...])
    queries[...] = (made[:, :BLOCK] * (HEAD_DIM**-0.5 * LOG2E)).astype(BF)
    keys_values[...] = made[:, BLOCK:].astype(BF)


def project(order, slots, gain, weights):
    rows = slots[0].shape[0]
    tile, steps = rows // 8, 4
    each = rows // steps
    full = pl.BlockSpec((each, BLOCK), lambda i, _: (i, 0))
    second = pl.BlockSpec((each, BLOCK), lambda i, _: (i + steps // 2, 0))
    return pl.pallas_call(
        project_kernel,
        out_shape=(
            jax.ShapeDtypeStruct((rows, BLOCK), BF),
            jax.ShapeDtypeStruct((rows, 2 * BLOCK), BF),
            jax.ShapeDtypeStruct((8, tile, BLOCK), BF),
        ),
        grid_spec=pltpu.PrefetchScalarGridSpec(
            num_scalar_prefetch=1,
            grid=(steps,),
            in_specs=[full, full, full, second, full, second, full, full]
            + [whole((8, 1, BLOCK))]
            + [whole((8, BLOCK, BLOCK))] * 3,
            out_specs=(
                full,
                pl.BlockSpec((each, 2 * BLOCK), lambda i, _: (i, 0)),
                whole((8, tile, BLOCK)),
            ),
            scratch_shapes=[pltpu.VMEM((D, 3 * BLOCK), BF), pltpu.VMEM((each, D), BF)],
        ),
        compiler_params=params(56),
        name="project",
    )(order, *slots, gain.reshape(8, 1, BLOCK), *weights)


TILE = 256
SPAN = TILE + 2 * REACH
CHUNKS = SPAN // TILE


def attend_kernel(edges, queries, low, own, high, out, keys, values, scores, powers, sems):
    step = pl.program_id(0)
    rows = own.shape[0]

    @pl.when(step == 0)
    def _():
        copies = []
        for n, (part, start) in enumerate(
            ((low, 0), (own, REACH), (high, REACH + rows))
        ):
            for m, target in enumerate((keys, values)):
                copies.append(
                    pltpu.make_async_copy(
                        part.at[:, pl.ds(m * BLOCK, BLOCK)],
                        target.at[pl.ds(start, part.shape[0]), pl.ds(0, BLOCK)],
                        sems.at[2 * n + m],
                    )
                )
        for c in copies:
            c.start()
        first = lax.broadcasted_iota(jnp.int32, (keys.shape[0], BLOCK), 1) == 0
        row = lax.broadcasted_iota(jnp.int32, (keys.shape[0], BLOCK), 0)
        absent = ((row < REACH) & (edges[0] == 1)) | (
            (row >= REACH + rows) & (edges[1] == 1)
        )
        keys[:, BLOCK:] = jnp.where(first & absent, -1e30, 0.0).astype(BF)
        for c in copies:
            c.wait()
        both = values[:, :BLOCK]
        left = lax.broadcasted_iota(jnp.int32, both.shape, 1) < HEAD_DIM
        ones = jnp.ones_like(both)
        values[:, :BLOCK] = jnp.where(left, both, ones)
        values[:, BLOCK:] = jnp.where(left, ones, both)

    lane = lax.broadcasted_iota(jnp.int32, (TILE, BLOCK), 1)
    q = queries[...]
    zero = jnp.zeros_like(q)
    both = jnp.concatenate(
        [jnp.where(lane < HEAD_DIM, q, zero), jnp.where(lane < HEAD_DIM, zero, q)], axis=0
    )
    mark = jnp.where(
        lax.broadcasted_iota(jnp.int32, (2 * TILE, BLOCK), 1) == 0, 1.0, 0.0
    ).astype(BF)
    stacked = jnp.concatenate([both, mark], axis=1)
    row = lax.broadcasted_iota(jnp.int32, (2 * TILE, TILE), 0) & (TILE - 1)
    column = lax.broadcasted_iota(jnp.int32, (2 * TILE, TILE), 1)
    highest = jnp.full((2 * TILE, BLOCK), -1e30, F32)
    for c in range(CHUNKS):
        part = keys[pl.ds(pl.multiple_of((step + c) * TILE, TILE), TILE)]
        s = lax.dot_general(stacked, part, NT, preferred_element_type=F32)
        least = c * TILE - REACH
        gap = column - row + least
        if least - TILE < -WINDOW:
            s = jnp.where(gap >= -WINDOW, s, -1e30)
        if least + TILE > WINDOW:
            s = jnp.where(gap <= WINDOW, s, -1e30)
        scores[:, c * TILE : (c + 1) * TILE] = s
        highest = jnp.maximum(highest, jnp.maximum(s[:, :BLOCK], s[:, BLOCK:]))
    peak = jnp.max(highest, axis=1, keepdims=True)
    span = pl.ds(pl.multiple_of(step * TILE, TILE), SPAN)
    totals = []
    for h in range(2):
        rows_of = slice(h * TILE, (h + 1) * TILE)
        for c in range(CHUNKS):
            at = slice(c * TILE, (c + 1) * TILE)
            powers[rows_of, at] = jnp.exp2(scores[rows_of, at] - peak[rows_of]).astype(BF)
        totals.append(dot(powers[rows_of], values[span, h * BLOCK : (h + 1) * BLOCK]))
    made = jnp.where(lane < HEAD_DIM, totals[0], totals[1])
    sums = jnp.where(lane < HEAD_DIM, totals[1], totals[0])
    out[...] = (made / pltpu.roll(sums, HEAD_DIM, 1)).astype(BF)


def attend(edges, queries, low, own, high):
    rows = own.shape[0]
    return pl.pallas_call(
        attend_kernel,
        out_shape=jax.ShapeDtypeStruct((rows, BLOCK), BF),
        grid_spec=pltpu.PrefetchScalarGridSpec(
            num_scalar_prefetch=1,
            grid=(rows // TILE,),
            in_specs=[pl.BlockSpec((TILE, BLOCK), lambda i, _: (i, 0)), ANY, ANY, ANY],
            out_specs=pl.BlockSpec((TILE, BLOCK), lambda i, _: (i, 0)),
            scratch_shapes=[
                pltpu.VMEM((rows + 2 * REACH, 2 * BLOCK), BF),
                pltpu.VMEM((rows + 2 * REACH, 2 * BLOCK), BF),
                pltpu.VMEM((2 * TILE, SPAN), F32),
                pltpu.VMEM((2 * TILE, SPAN), BF),
                pltpu.SemaphoreType.DMA((6,)),
            ],
        ),
        compiler_params=params(56),
        name="attend",
    )(edges, queries, low, own, high)


ROWS_E = 64
ROWS_S = 64
ROWS_P = 16
PACK = ROWS_E + ROWS_S + ROWS_P


def pack_weights(position, expand, shrink, project_out):
    part = lax.dynamic_slice_in_dim(expand, position * 2 * ROWS_E, 2 * ROWS_E, 0)
    return jnp.concatenate(
        [
            jnp.concatenate([part[:ROWS_E], part[ROWS_E:]], axis=1),
            lax.dynamic_slice_in_dim(shrink, position * ROWS_S, ROWS_S, 0),
            lax.dynamic_slice_in_dim(project_out, position * ROWS_P, ROWS_P, 0),
        ],
        axis=0,
    )


def gelu(v):
    return 0.5 * v * (1.0 + jnp.tanh(0.7978845608028654 * (v + 0.044715 * v * v * v)))


def forward_kernel(table, *refs):
    parts = refs[:8]
    context, share, gain, out, expand, shrink, outward, sems = refs[8:]
    groups = ([], [], [])
    width = expand.shape[3]
    for n, part in enumerate(parts):
        where = table[8 + n]
        for side in range(2):
            slot = 1 - side if n % 4 == 3 else side

            def copy(group, source, target):
                groups[group].append(
                    pltpu.make_async_copy(source, target, sems.at[group, len(groups[group])])
                )

            copy(
                0,
                part.at[:, side, pl.ds(ROWS_E + ROWS_S, ROWS_P), :],
                outward.at[
                    :, slot, pl.ds(pl.multiple_of(where * ROWS_P, ROWS_P), ROWS_P), :
                ],
            )
            for piece in range(2):
                copy(
                    1,
                    part.at[:, side, pl.ds(0, ROWS_E), pl.ds(piece * width, width)],
                    expand.at[
                        :,
                        slot,
                        pl.ds(
                            pl.multiple_of(where * 2 * ROWS_E + piece * ROWS_E, ROWS_E), ROWS_E
                        ),
                        :,
                    ],
                )
            copy(
                2,
                part.at[:, side, pl.ds(ROWS_E, ROWS_S), :],
                shrink.at[:, slot, pl.ds(pl.multiple_of(where * ROWS_S, ROWS_S), ROWS_S), :],
            )
    for group in groups:
        for c in group:
            c.start()
    for c in groups[0]:
        c.wait()
    total = dot(context[table[0]], outward[0, 0])
    for p in range(1, 8):
        total = total + dot(context[table[p]], outward[p // 2, p % 2])
    start = jnp.concatenate([share[h] for h in range(8)], axis=1).astype(F32)
    middle = (start + total).astype(BF).astype(F32)
    average = jnp.mean(middle, axis=1, keepdims=True)
    centred = middle - average
    spread = jnp.mean(centred * centred, axis=1, keepdims=True)
    normed = (centred * lax.rsqrt(spread + EPSILON) * gain[...]).astype(BF)
    for c in groups[1]:
        c.wait()
    hidden = [gelu(dot(normed, expand[p // 2, p % 2])).astype(BF) for p in range(8)]
    for c in groups[2]:
        c.wait()
    total = middle
    for p in range(8):
        total = total + dot(hidden[p], shrink[p // 2, p % 2])
    done = total.astype(BF)
    for h in range(8):
        out[h] = done[:, h * BLOCK : (h + 1) * BLOCK]


def forward(table, parts, context, share, gain):
    rows = share.shape[1]
    width = D // 2
    return pl.pallas_call(
        forward_kernel,
        out_shape=jax.ShapeDtypeStruct((8, rows, BLOCK), BF),
        grid_spec=pltpu.PrefetchScalarGridSpec(
            num_scalar_prefetch=1,
            grid=(1,),
            in_specs=[ANY] * 8
            + [whole((8, rows, BLOCK)), whole((8, rows, BLOCK)), whole((1, D))],
            out_specs=whole((8, rows, BLOCK)),
            scratch_shapes=[
                pltpu.VMEM((4, 2, D, width), BF),
                pltpu.VMEM((4, 2, width, D), BF),
                pltpu.VMEM((4, 2, BLOCK, D), BF),
                pltpu.SemaphoreType.DMA((3, 32)),
            ],
        ),
        compiler_params=params(56),
        cost_estimate=cost(4_800_000_000, 20_000_000, 1_100_000),
        name="forward",
    )(table, *parts, context, share, gain.reshape(1, D))


EACH = 8


def decode_kernel(index, low, own, high, weights, back, sums, source, held, kept, sems):
    rim, slots = low.shape[0], weights.shape[1]
    steps = weights.shape[0] // EACH
    ahead = pieces_of(low, source, 0, 1, sems, 0)
    ahead += pieces_of(own, source, rim, 2, sems, 1)
    ahead += pieces_of(high, source, rim + own.shape[0], 1, sems, 3)
    blocks = pieces_of(weights, held, 0, 2 * steps, sems, 4)
    done = pieces_of(kept, back, 0, steps, sems, 4 + 2 * steps)
    for c in ahead + blocks:
        c.start()
    for c in ahead:
        c.wait()
    row = lax.broadcasted_iota(jnp.int32, (BLOCK, BLOCK), 0)
    column = lax.broadcasted_iota(jnp.int32, (BLOCK, BLOCK), 1)
    for step in range(steps):
        blocks[2 * step].wait()
        blocks[2 * step + 1].wait()
        kinds = []
        for b in range(step * EACH, (step + 1) * EACH):
            left = jnp.concatenate([held[b, k] for k in range(slots)], axis=1)
            right = jnp.concatenate([source[index[b, k]] for k in range(slots)], axis=0)
            made = dot(left, right)
            kept[b * BLOCK : (b + 1) * BLOCK] = made.astype(BF)
            kinds.append((made, made * made))
        done[step].start()
        held_sums = [
            jnp.sum(
                jnp.where(row == column, jnp.sum(kinds[b][n], axis=1, keepdims=True), 0.0),
                axis=0,
                keepdims=True,
            )
            for n in range(2)
            for b in range(EACH)
        ]
        sums[step] = jnp.concatenate(held_sums, axis=0).astype(BF)
    for c in done:
        c.wait()


def decode(index, low, own, high, weights):
    count, slots = weights.shape[:2]
    blocks = own.shape[0]
    rim = low.shape[0]
    steps = count // EACH
    return pl.pallas_call(
        decode_kernel,
        out_shape=(
            jax.ShapeDtypeStruct((count * BLOCK, BLOCK), BF),
            jax.ShapeDtypeStruct((steps, 2 * EACH, BLOCK), BF),
        ),
        grid_spec=pltpu.PrefetchScalarGridSpec(
            num_scalar_prefetch=1,
            grid=(1,),
            in_specs=[ANY, ANY, ANY, FAR],
            out_specs=(ANY, whole((steps, 2 * EACH, BLOCK))),
            scratch_shapes=[
                pltpu.VMEM((blocks + 2 * rim, BLOCK, BLOCK), BF),
                pltpu.VMEM((count, slots, BLOCK, BLOCK), BF),
                pltpu.VMEM((count * BLOCK, BLOCK), BF),
                pltpu.SemaphoreType.DMA((4 + 3 * steps,)),
            ],
        ),
        compiler_params=params(56),
        cost_estimate=cost(540_000_000, 10_000_000),
        name="decode",
    )(index, low, own, high, weights)


def finish_kernel(sums, back, state, gain, out, stats, kept, base, made, sems):
    steps = sums.shape[1]
    count = sums.shape[0]
    first = pieces_of(sums, stats, 0, count, sems, 0)
    backs = pieces_of(back, kept, 0, steps, sems, count)
    states = pieces_of(state, base, 0, steps, sems, count + steps)
    outs = pieces_of(made, out, 0, steps, sems, count + 2 * steps)
    for c in first:
        c.start()
    for a, b in zip(backs, states):
        a.start()
        b.start()
    depth = count * 2 * EACH
    row = lax.broadcasted_iota(jnp.int32, (depth, 2 * EACH * BLOCK), 0)
    column = lax.broadcasted_iota(jnp.int32, (depth, 2 * EACH * BLOCK), 1)
    pick = jnp.where((row % (2 * EACH)) == (column // BLOCK), 1.0 / D, 0.0).astype(BF)
    for c in first:
        c.wait()
    for step in range(steps):
        parts = jnp.concatenate([stats[h, step] for h in range(count)], axis=0)
        spread = lax.dot_general(parts, pick, TN, preferred_element_type=F32)
        backs[step].wait()
        states[step].wait()
        for b in range(EACH):
            at = (step * EACH + b) * BLOCK
            average = spread[:, b * BLOCK : (b + 1) * BLOCK]
            squares = spread[:, (EACH + b) * BLOCK : (EACH + b + 1) * BLOCK]
            scale = lax.rsqrt(squares - average * average + EPSILON) * gain[...]
            made[at : at + BLOCK] = (
                base[at : at + BLOCK].astype(F32)
                + (kept[at : at + BLOCK].astype(F32) - average) * scale
            ).astype(BF)
        outs[step].start()
    for c in outs:
        c.wait()


def finish(sums, back, state, gain):
    rows = state.shape[0]
    count, steps = sums.shape[:2]
    return pl.pallas_call(
        finish_kernel,
        out_shape=jax.ShapeDtypeStruct((rows, BLOCK), BF),
        grid_spec=pl.GridSpec(
            grid=(1,),
            in_specs=[ANY, ANY, FAR, whole((1, BLOCK))],
            out_specs=ANY,
            scratch_shapes=[
                pltpu.VMEM(sums.shape, BF),
                pltpu.VMEM((rows, BLOCK), BF),
                pltpu.VMEM((rows, BLOCK), BF),
                pltpu.VMEM((rows, BLOCK), BF),
                pltpu.SemaphoreType.DMA((count + 3 * steps,)),
            ],
        ),
        compiler_params=params(56),
        cost_estimate=cost(540_000_000, 8_000_000),
        name="finish",
    )(sums, back, state, gain.reshape(1, BLOCK))


def shifted(value, by):
    return lax.ppermute(value, "seq", [(i, i + by) for i in range(16) if 0 <= i + by < 16])


def among(value, axis, count, to):
    return lax.ppermute(value, axis, [(i, to(i)) for i in range(count)])


def along_z(i, by):
    return (i // 8) * 8 + ((i // 2 + by) % 4) * 2 + i % 2


UP = lambda v: among(v, "seq", 16, lambda i: along_z(i, 1))
DOWN = lambda v: among(v, "seq", 16, lambda i: along_z(i, -1))
ACROSS = lambda v: among(v, ("seq", "head"), 128, lambda i: i ^ 65)
TWIN = lambda v: among(v, "seq", 16, lambda i: i ^ 1)
NORTH = lambda v: among(v, "head", 8, lambda i: (i + 2) % 8)
SOUTH = lambda v: among(v, "head", 8, lambda i: (i - 2) % 8)
OVER = lambda v: among(v, "head", 8, lambda i: i ^ 1)


def on_device(
    grid_state,
    encode_index,
    encode_weights,
    first_gain,
    project_in,
    project_out,
    second_gain,
    expand_weights,
    shrink_weights,
    decode_index,
    decode_weights,
    output_gain,
):
    band = lax.axis_index("seq")
    bands = lax.axis_size("seq")
    me = lax.axis_index("head")
    mesh_blocks = encode_weights.shape[0]
    mesh_rows = mesh_blocks * BLOCK
    grid_blocks = grid_state.shape[0] // BLOCK
    rim = mesh_blocks * BLOCK
    core, place = band % 2, (band // 2 + 2 * (band // 8)) % 4
    position = place * 2 + core
    packed = pack_weights(position, expand_weights, shrink_weights, project_out)
    last, first, packed = lax.optimization_barrier(
        (grid_state[-rim:], grid_state[:rim], packed)
    )
    low = shifted(last, 1)
    high = shifted(first, -1)
    swapped, north, south = OVER(packed), NORTH(packed), SOUTH(packed)
    swapped_north, swapped_south = NORTH(swapped), SOUTH(swapped)
    far, swapped_far = NORTH(north), SOUTH(swapped_south)
    inward = [project_in[:, j, :].reshape(8, BLOCK, BLOCK) for j in range(3)]
    low, high, *inward = lax.optimization_barrier((low, high, *inward))
    mesh_start = encode(
        encode_index - (band * grid_blocks - mesh_blocks), low, grid_state, high, encode_weights
    )
    half = mesh_rows // 2
    mine = jnp.stack(
        [
            jnp.stack(pair)
            for pair in (
                (packed, swapped),
                (north, swapped_north),
                (south, swapped_south),
                (far, swapped_far),
            )
        ]
    )
    x, mine = lax.optimization_barrier((mesh_start, mine))
    up, down = UP(mine), DOWN(mine)
    y, xa, xb, mine = lax.optimization_barrier((OVER(x), NORTH(x), SOUTH(x), mine))
    across = ACROSS(mine)
    from_south = NORTH(jnp.concatenate([xa[:half], y]))
    from_north = SOUTH(jnp.concatenate([xb[half:], y]))
    xc = jnp.concatenate([from_south[:half], from_north[:half]])
    slots = (x, y, xa, from_south, xb, from_north, xc, OVER(xc))
    partner = me ^ 1
    order = jnp.stack(
        [me, partner] + [(v + by) % 8 for by in (6, 2, 4) for v in (me, partner)]
    ).astype(jnp.int32)
    queries, keys_values, share = project(order, slots, first_gain, inward)
    upper, lower, up, down = lax.optimization_barrier(
        (keys_values[mesh_rows - REACH :], keys_values[:REACH], up, down)
    )
    below = shifted(upper, 1)
    above = shifted(lower, -1)
    edges = jnp.stack([band == 0, band == bands - 1]).astype(jnp.int32)
    context = attend(edges, queries, below, keys_values, above)
    context, *here = lax.optimization_barrier((context, mine, up, down, across))
    parts = here + [TWIN(v) for v in here]
    context = lax.all_to_all(
        context.reshape(8, mesh_rows // 8, BLOCK), "head", 0, 0, tiled=True
    )
    places = [
        ((place + by) % 4) * 2 + side for side in (core, 1 - core) for by in (0, 3, 1, 2)
    ]
    table = jnp.concatenate([order, jnp.stack(places).astype(jnp.int32)])
    mesh_end = forward(table, parts, context, share, second_gain)
    mesh_end = lax.all_to_all(mesh_end, "head", 0, 0, tiled=True)
    mesh_end = mesh_end.reshape(mesh_blocks, BLOCK, BLOCK)
    edge = mesh_blocks // 2
    back, sums = decode(
        decode_index - (band * mesh_blocks - edge),
        shifted(mesh_end[-edge:], 1),
        mesh_end,
        shifted(mesh_end[:edge], -1),
        decode_weights,
    )
    sums = lax.all_to_all(
        jnp.broadcast_to(sums, (8, *sums.shape)), "head", 0, 0, tiled=True
    )
    return finish(sums, back, grid_state, output_gain)


def solution(mesh):
    in_specs = (
        P("seq", "head"),
        P("seq", None),
        P("seq", None, None, None),
        P(),
        P(None, None, "head"),
        P("head", None),
        P(),
        P(None, "head"),
        P("head", None),
        P("seq", None),
        P("seq", None, None, None),
        P("head"),
    )
    return jax.shard_map(
        on_device, mesh=mesh, in_specs=in_specs, out_specs=P("seq", "head"), check_vma=False
    )
```

```python
import jax
import jax.numpy as jnp
from jax import lax
from jax.experimental import pallas as pl
from jax.experimental.pallas import tpu as pltpu
from jax.sharding import PartitionSpec as P

D = 1024
HEAD_DIM = 64
WINDOW = 1120
REACH = 1152
BLOCK = 128
EPSILON = 1e-05
LOG2E = 1.4426950408889634
BF = jnp.bfloat16
F32 = jnp.float32
NT = (((1,), (1,)), ((), ()))
TN = (((0,), (0,)), ((), ()))
MIB = 1 << 20


def params(mib):
    return pltpu.CompilerParams(
        dimension_semantics=("arbitrary",), vmem_limit_bytes=mib * MIB
    )


def dot(a, b):
    return jnp.dot(a, b, preferred_element_type=F32)


def cost(flops, moved, powers=0):
    return pl.CostEstimate(flops=flops, bytes_accessed=moved, transcendentals=powers)


ANY = pl.BlockSpec(memory_space=pl.ANY)
FAR = pl.BlockSpec(memory_space=pltpu.HBM)


def whole(shape):
    return pl.BlockSpec(shape, lambda i, *_: (0,) * len(shape))


def pieces_of(ref, target, start, count, sems, first):
    length = ref.shape[0] // count
    return [
        pltpu.make_async_copy(
            ref.at[pl.ds(n * length, length)],
            target.at[pl.ds(start + n * length, length)],
            sems.at[first + n],
        )
        for n in range(count)
    ]


def encode_kernel(index, low, own, high, weights, out, source, held, made, sems):
    rim, slots = low.shape[0], weights.shape[1]
    ahead = pieces_of(low, source, 0, 2, sems, 0)
    ahead += pieces_of(own, source, rim, 4, sems, 2)
    ahead += pieces_of(high, source, rim + own.shape[0], 2, sems, 6)
    count = weights.shape[0]
    blocks = pieces_of(weights, held, 0, count, sems, 8)
    back = pieces_of(made, out, 0, 4, sems, 8 + count)
    for c in ahead + blocks:
        c.start()
    for c in ahead:
        c.wait()
    for b in range(count):
        if b % 4 == 0:
            for c in blocks[b : b + 4]:
                c.wait()
        left = jnp.concatenate([held[b, k] for k in range(slots)], axis=1)
        right = jnp.concatenate([source[index[b, k]] for k in range(slots)], axis=0)
        made[b * BLOCK : (b + 1) * BLOCK] = dot(left, right).astype(BF)
        if (b + 1) % (count // 4) == 0:
            back[b // (count // 4)].start()
    for c in back:
        c.wait()


def encode(index, low, own, high, weights):
    count, slots = weights.shape[:2]
    blocks = own.shape[0] // BLOCK
    rim = low.shape[0] // BLOCK
    shaped = [v.reshape(-1, BLOCK, BLOCK) for v in (low, own, high)]
    return pl.pallas_call(
        encode_kernel,
        out_shape=jax.ShapeDtypeStruct((count * BLOCK, BLOCK), BF),
        grid_spec=pltpu.PrefetchScalarGridSpec(
            num_scalar_prefetch=1,
            grid=(1,),
            in_specs=[ANY, FAR, ANY, FAR],
            out_specs=ANY,
            scratch_shapes=[
                pltpu.VMEM((blocks + 2 * rim, BLOCK, BLOCK), BF),
                pltpu.VMEM((count, slots, BLOCK, BLOCK), BF),
                pltpu.VMEM((count * BLOCK, BLOCK), BF),
                pltpu.SemaphoreType.DMA((12 + count,)),
            ],
        ),
        compiler_params=params(56),
        cost_estimate=cost(540_000_000, 8_000_000),
        name="encode",
    )(index, *shaped, weights)


def project_kernel(
    order, s0, s1, s2, s3, s4, s5, s6, s7, gain, wq, wk, wv,
    queries, keys_values, share, ordered, normed,
):
    step = pl.program_id(0)

    @pl.when(step == 0)
    def _():
        for p in range(8):
            ordered[p * BLOCK : (p + 1) * BLOCK] = jnp.concatenate(
                [w[order[p]] for w in (wq, wk, wv)], axis=1
            )

    slots = (s0, s1, s2, s3, s4, s5, s6, s7)
    rows = s0.shape[0]
    tile = share.shape[1]
    for n in range(rows // tile):

        @pl.when(order[0] == step * (rows // tile) + n)
        def _():
            for p in range(8):
                share[order[p]] = slots[p][n * tile : (n + 1) * tile]

    gains = [gain[order[p]] for p in range(8)]
    few = 32
    for n in range(rows // few):
        at = slice(n * few, (n + 1) * few)
        pieces = [s[at].astype(F32) for s in slots]
        total = pieces[0]
        for x in pieces[1:]:
            total = total + x
        average = jnp.sum(total, axis=1, keepdims=True) * (1.0 / D)
        pieces = [x - average for x in pieces]
        total = pieces[0] * pieces[0]
        for x in pieces[1:]:
            total = total + x * x
        spread = lax.rsqrt(jnp.sum(total, axis=1, keepdims=True) * (1.0 / D) + EPSILON)
        for p, x in enumerate(pieces):
            normed[at, p * BLOCK : (p + 1) * BLOCK] = (x * spread * gains[p]).astype(BF)
    made = dot(normed[...], ordered[...])
    queries[...] = (made[:, :BLOCK] * (HEAD_DIM**-0.5 * LOG2E)).astype(BF)
    keys_values[...] = made[:, BLOCK:].astype(BF)


def project(order, slots, gain, weights):
    rows = slots[0].shape[0]
    tile, steps = rows // 8, 4
    each = rows // steps
    full = pl.BlockSpec((each, BLOCK), lambda i, _: (i, 0))
    second = pl.BlockSpec((each, BLOCK), lambda i, _: (i + steps // 2, 0))
    return pl.pallas_call(
        project_kernel,
        out_shape=(
            jax.ShapeDtypeStruct((rows, BLOCK), BF),
            jax.ShapeDtypeStruct((rows, 2 * BLOCK), BF),
            jax.ShapeDtypeStruct((8, tile, BLOCK), BF),
        ),
        grid_spec=pltpu.PrefetchScalarGridSpec(
            num_scalar_prefetch=1,
            grid=(steps,),
            in_specs=[full, full, full, second, full, second, full, full]
            + [whole((8, 1, BLOCK))]
            + [whole((8, BLOCK, BLOCK))] * 3,
            out_specs=(
                full,
                pl.BlockSpec((each, 2 * BLOCK), lambda i, _: (i, 0)),
                whole((8, tile, BLOCK)),
            ),
            scratch_shapes=[pltpu.VMEM((D, 3 * BLOCK), BF), pltpu.VMEM((each, D), BF)],
        ),
        compiler_params=params(56),
        name="project",
    )(order, *slots, gain.reshape(8, 1, BLOCK), *weights)


TILE = 256
SPAN = TILE + 2 * REACH
CHUNKS = SPAN // TILE


def attend_kernel(edges, queries, low, own, high, out, keys, values, scores, powers, sems):
    step = pl.program_id(0)
    rows = own.shape[0]

    @pl.when(step == 0)
    def _():
        copies = []
        for n, (part, start) in enumerate(
            ((low, 0), (own, REACH), (high, REACH + rows))
        ):
            for m, target in enumerate((keys, values)):
                copies.append(
                    pltpu.make_async_copy(
                        part.at[:, pl.ds(m * BLOCK, BLOCK)],
                        target.at[pl.ds(start, part.shape[0]), pl.ds(0, BLOCK)],
                        sems.at[2 * n + m],
                    )
                )
        for c in copies:
            c.start()
        first = lax.broadcasted_iota(jnp.int32, (keys.shape[0], BLOCK), 1) == 0
        row = lax.broadcasted_iota(jnp.int32, (keys.shape[0], BLOCK), 0)
        absent = ((row < REACH) & (edges[0] == 1)) | (
            (row >= REACH + rows) & (edges[1] == 1)
        )
        keys[:, BLOCK:] = jnp.where(first & absent, -1e30, 0.0).astype(BF)
        for c in copies:
            c.wait()
        both = values[:, :BLOCK]
        left = lax.broadcasted_iota(jnp.int32, both.shape, 1) < HEAD_DIM
        ones = jnp.ones_like(both)
        values[:, :BLOCK] = jnp.where(left, both, ones)
        values[:, BLOCK:] = jnp.where(left, ones, both)

    lane = lax.broadcasted_iota(jnp.int32, (TILE, BLOCK), 1)
    q = queries[...]
    zero = jnp.zeros_like(q)
    both = jnp.concatenate(
        [jnp.where(lane < HEAD_DIM, q, zero), jnp.where(lane < HEAD_DIM, zero, q)], axis=0
    )
    mark = jnp.where(
        lax.broadcasted_iota(jnp.int32, (2 * TILE, BLOCK), 1) == 0, 1.0, 0.0
    ).astype(BF)
    stacked = jnp.concatenate([both, mark], axis=1)
    row = lax.broadcasted_iota(jnp.int32, (2 * TILE, TILE), 0) & (TILE - 1)
    column = lax.broadcasted_iota(jnp.int32, (2 * TILE, TILE), 1)
    highest = jnp.full((2 * TILE, BLOCK), -1e30, F32)
    for c in range(CHUNKS):
        part = keys[pl.ds(pl.multiple_of((step + c) * TILE, TILE), TILE)]
        s = lax.dot_general(stacked, part, NT, preferred_element_type=F32)
        least = c * TILE - REACH
        gap = column - row + least
        if least - TILE < -WINDOW:
            s = jnp.where(gap >= -WINDOW, s, -1e30)
        if least + TILE > WINDOW:
            s = jnp.where(gap <= WINDOW, s, -1e30)
        scores[:, c * TILE : (c + 1) * TILE] = s
        highest = jnp.maximum(highest, jnp.maximum(s[:, :BLOCK], s[:, BLOCK:]))
    peak = jnp.max(highest, axis=1, keepdims=True)
    span = pl.ds(pl.multiple_of(step * TILE, TILE), SPAN)
    totals = []
    for h in range(2):
        rows_of = slice(h * TILE, (h + 1) * TILE)
        for c in range(CHUNKS):
            at = slice(c * TILE, (c + 1) * TILE)
            powers[rows_of, at] = jnp.exp2(scores[rows_of, at] - peak[rows_of]).astype(BF)
        totals.append(dot(powers[rows_of], values[span, h * BLOCK : (h + 1) * BLOCK]))
    made = jnp.where(lane < HEAD_DIM, totals[0], totals[1])
    sums = jnp.where(lane < HEAD_DIM, totals[1], totals[0])
    out[...] = (made / pltpu.roll(sums, HEAD_DIM, 1)).astype(BF)


def attend(edges, queries, low, own, high):
    rows = own.shape[0]
    return pl.pallas_call(
        attend_kernel,
        out_shape=jax.ShapeDtypeStruct((rows, BLOCK), BF),
        grid_spec=pltpu.PrefetchScalarGridSpec(
            num_scalar_prefetch=1,
            grid=(rows // TILE,),
            in_specs=[pl.BlockSpec((TILE, BLOCK), lambda i, _: (i, 0)), ANY, ANY, ANY],
            out_specs=pl.BlockSpec((TILE, BLOCK), lambda i, _: (i, 0)),
            scratch_shapes=[
                pltpu.VMEM((rows + 2 * REACH, 2 * BLOCK), BF),
                pltpu.VMEM((rows + 2 * REACH, 2 * BLOCK), BF),
                pltpu.VMEM((2 * TILE, SPAN), F32),
                pltpu.VMEM((2 * TILE, SPAN), BF),
                pltpu.SemaphoreType.DMA((6,)),
            ],
        ),
        compiler_params=params(56),
        name="attend",
    )(edges, queries, low, own, high)


ROWS_E = 64
ROWS_S = 64
ROWS_P = 16
PACK = ROWS_E + ROWS_S + ROWS_P


def pack_weights(position, expand, shrink, project_out):
    part = lax.dynamic_slice_in_dim(expand, position * 2 * ROWS_E, 2 * ROWS_E, 0)
    return jnp.concatenate(
        [
            jnp.concatenate([part[:ROWS_E], part[ROWS_E:]], axis=1),
            lax.dynamic_slice_in_dim(shrink, position * ROWS_S, ROWS_S, 0),
            lax.dynamic_slice_in_dim(project_out, position * ROWS_P, ROWS_P, 0),
        ],
        axis=0,
    )


def gelu(v):
    return 0.5 * v * (1.0 + jnp.tanh(0.7978845608028654 * (v + 0.044715 * v * v * v)))


def forward_kernel(table, *refs):
    parts = refs[:8]
    context, share, gain, out, expand, shrink, outward, sems = refs[8:]
    groups = ([], [], [])
    width = expand.shape[3]
    for n, part in enumerate(parts):
        where = table[8 + n]
        for side in range(2):
            slot = 1 - side if n % 4 == 3 else side

            def copy(group, source, target):
                groups[group].append(
                    pltpu.make_async_copy(source, target, sems.at[group, len(groups[group])])
                )

            copy(
                0,
                part.at[:, side, pl.ds(ROWS_E + ROWS_S, ROWS_P), :],
                outward.at[
                    :, slot, pl.ds(pl.multiple_of(where * ROWS_P, ROWS_P), ROWS_P), :
                ],
            )
            for piece in range(2):
                copy(
                    1,
                    part.at[:, side, pl.ds(0, ROWS_E), pl.ds(piece * width, width)],
                    expand.at[
                        :,
                        slot,
                        pl.ds(
                            pl.multiple_of(where * 2 * ROWS_E + piece * ROWS_E, ROWS_E), ROWS_E
                        ),
                        :,
                    ],
                )
            copy(
                2,
                part.at[:, side, pl.ds(ROWS_E, ROWS_S), :],
                shrink.at[:, slot, pl.ds(pl.multiple_of(where * ROWS_S, ROWS_S), ROWS_S), :],
            )
    for group in groups:
        for c in group:
            c.start()
    for c in groups[0]:
        c.wait()
    total = dot(context[table[0]], outward[0, 0])
    for p in range(1, 8):
        total = total + dot(context[table[p]], outward[p // 2, p % 2])
    start = jnp.concatenate([share[h] for h in range(8)], axis=1).astype(F32)
    middle = (start + total).astype(BF).astype(F32)
    average = jnp.mean(middle, axis=1, keepdims=True)
    centred = middle - average
    spread = jnp.mean(centred * centred, axis=1, keepdims=True)
    normed = (centred * lax.rsqrt(spread + EPSILON) * gain[...]).astype(BF)
    for c in groups[1]:
        c.wait()
    hidden = [gelu(dot(normed, expand[p // 2, p % 2])).astype(BF) for p in range(8)]
    for c in groups[2]:
        c.wait()
    total = middle
    for p in range(8):
        total = total + dot(hidden[p], shrink[p // 2, p % 2])
    done = total.astype(BF)
    for h in range(8):
        out[h] = done[:, h * BLOCK : (h + 1) * BLOCK]


def forward(table, parts, context, share, gain):
    rows = share.shape[1]
    width = D // 2
    return pl.pallas_call(
        forward_kernel,
        out_shape=jax.ShapeDtypeStruct((8, rows, BLOCK), BF),
        grid_spec=pltpu.PrefetchScalarGridSpec(
            num_scalar_prefetch=1,
            grid=(1,),
            in_specs=[ANY] * 8
            + [whole((8, rows, BLOCK)), whole((8, rows, BLOCK)), whole((1, D))],
            out_specs=whole((8, rows, BLOCK)),
            scratch_shapes=[
                pltpu.VMEM((4, 2, D, width), BF),
                pltpu.VMEM((4, 2, width, D), BF),
                pltpu.VMEM((4, 2, BLOCK, D), BF),
                pltpu.SemaphoreType.DMA((3, 32)),
            ],
        ),
        compiler_params=params(56),
        cost_estimate=cost(4_800_000_000, 20_000_000, 1_100_000),
        name="forward",
    )(table, *parts, context, share, gain.reshape(1, D))


EACH = 8


def decode_kernel(index, low, own, high, weights, back, sums, source, held, kept, sems):
    rim, slots = low.shape[0], weights.shape[1]
    steps = weights.shape[0] // EACH
    ahead = pieces_of(low, source, 0, 1, sems, 0)
    ahead += pieces_of(own, source, rim, 2, sems, 1)
    ahead += pieces_of(high, source, rim + own.shape[0], 1, sems, 3)
    blocks = pieces_of(weights, held, 0, 2 * steps, sems, 4)
    done = pieces_of(kept, back, 0, steps, sems, 4 + 2 * steps)
    for c in ahead + blocks:
        c.start()
    for c in ahead:
        c.wait()
    row = lax.broadcasted_iota(jnp.int32, (BLOCK, BLOCK), 0)
    column = lax.broadcasted_iota(jnp.int32, (BLOCK, BLOCK), 1)
    for step in range(steps):
        blocks[2 * step].wait()
        blocks[2 * step + 1].wait()
        kinds = []
        for b in range(step * EACH, (step + 1) * EACH):
            left = jnp.concatenate([held[b, k] for k in range(slots)], axis=1)
            right = jnp.concatenate([source[index[b, k]] for k in range(slots)], axis=0)
            made = dot(left, right)
            kept[b * BLOCK : (b + 1) * BLOCK] = made.astype(BF)
            kinds.append((made, made * made))
        done[step].start()
        held_sums = [
            jnp.sum(
                jnp.where(row == column, jnp.sum(kinds[b][n], axis=1, keepdims=True), 0.0),
                axis=0,
                keepdims=True,
            )
            for n in range(2)
            for b in range(EACH)
        ]
        sums[step] = jnp.concatenate(held_sums, axis=0).astype(BF)
    for c in done:
        c.wait()


def decode(index, low, own, high, weights):
    count, slots = weights.shape[:2]
    blocks = own.shape[0]
    rim = low.shape[0]
    steps = count // EACH
    return pl.pallas_call(
        decode_kernel,
        out_shape=(
            jax.ShapeDtypeStruct((count * BLOCK, BLOCK), BF),
            jax.ShapeDtypeStruct((steps, 2 * EACH, BLOCK), BF),
        ),
        grid_spec=pltpu.PrefetchScalarGridSpec(
            num_scalar_prefetch=1,
            grid=(1,),
            in_specs=[ANY, ANY, ANY, FAR],
            out_specs=(ANY, whole((steps, 2 * EACH, BLOCK))),
            scratch_shapes=[
                pltpu.VMEM((blocks + 2 * rim, BLOCK, BLOCK), BF),
                pltpu.VMEM((count, slots, BLOCK, BLOCK), BF),
                pltpu.VMEM((count * BLOCK, BLOCK), BF),
                pltpu.SemaphoreType.DMA((4 + 3 * steps,)),
            ],
        ),
        compiler_params=params(56),
        cost_estimate=cost(540_000_000, 10_000_000),
        name="decode",
    )(index, low, own, high, weights)


def finish_kernel(sums, back, state, gain, out, stats, kept, base, made, sems):
    steps = sums.shape[1]
    count = sums.shape[0]
    first = pieces_of(sums, stats, 0, count, sems, 0)
    backs = pieces_of(back, kept, 0, steps, sems, count)
    states = pieces_of(state, base, 0, steps, sems, count + steps)
    outs = pieces_of(made, out, 0, steps, sems, count + 2 * steps)
    for c in first:
        c.start()
    for a, b in zip(backs, states):
        a.start()
        b.start()
    depth = count * 2 * EACH
    row = lax.broadcasted_iota(jnp.int32, (depth, 2 * EACH * BLOCK), 0)
    column = lax.broadcasted_iota(jnp.int32, (depth, 2 * EACH * BLOCK), 1)
    pick = jnp.where((row % (2 * EACH)) == (column // BLOCK), 1.0 / D, 0.0).astype(BF)
    for c in first:
        c.wait()
    for step in range(steps):
        parts = jnp.concatenate([stats[h, step] for h in range(count)], axis=0)
        spread = lax.dot_general(parts, pick, TN, preferred_element_type=F32)
        backs[step].wait()
        states[step].wait()
        for b in range(EACH):
            at = (step * EACH + b) * BLOCK
            average = spread[:, b * BLOCK : (b + 1) * BLOCK]
            squares = spread[:, (EACH + b) * BLOCK : (EACH + b + 1) * BLOCK]
            scale = lax.rsqrt(squares - average * average + EPSILON) * gain[...]
            made[at : at + BLOCK] = (
                base[at : at + BLOCK].astype(F32)
                + (kept[at : at + BLOCK].astype(F32) - average) * scale
            ).astype(BF)
        outs[step].start()
    for c in outs:
        c.wait()


def finish(sums, back, state, gain):
    rows = state.shape[0]
    count, steps = sums.shape[:2]
    return pl.pallas_call(
        finish_kernel,
        out_shape=jax.ShapeDtypeStruct((rows, BLOCK), BF),
        grid_spec=pl.GridSpec(
            grid=(1,),
            in_specs=[ANY, ANY, FAR, whole((1, BLOCK))],
            out_specs=ANY,
            scratch_shapes=[
                pltpu.VMEM(sums.shape, BF),
                pltpu.VMEM((rows, BLOCK), BF),
                pltpu.VMEM((rows, BLOCK), BF),
                pltpu.VMEM((rows, BLOCK), BF),
                pltpu.SemaphoreType.DMA((count + 3 * steps,)),
            ],
        ),
        compiler_params=params(56),
        cost_estimate=cost(540_000_000, 8_000_000),
        name="finish",
    )(sums, back, state, gain.reshape(1, BLOCK))


def shifted(value, by):
    return lax.ppermute(value, "seq", [(i, i + by) for i in range(16) if 0 <= i + by < 16])


def among(value, axis, count, to):
    return lax.ppermute(value, axis, [(i, to(i)) for i in range(count)])


def along_z(i, by):
    return (i // 8) * 8 + ((i // 2 + by) % 4) * 2 + i % 2


UP = lambda v: among(v, "seq", 16, lambda i: along_z(i, 1))
DOWN = lambda v: among(v, "seq", 16, lambda i: along_z(i, -1))
ACROSS = lambda v: among(v, ("seq", "head"), 128, lambda i: i ^ 65)
TWIN = lambda v: among(v, "seq", 16, lambda i: i ^ 1)
NORTH = lambda v: among(v, "head", 8, lambda i: (i + 2) % 8)
SOUTH = lambda v: among(v, "head", 8, lambda i: (i - 2) % 8)
OVER = lambda v: among(v, "head", 8, lambda i: i ^ 1)


def on_device(
    grid_state,
    encode_index,
    encode_weights,
    first_gain,
    project_in,
    project_out,
    second_gain,
    expand_weights,
    shrink_weights,
    decode_index,
    decode_weights,
    output_gain,
):
    band = lax.axis_index("seq")
    bands = lax.axis_size("seq")
    me = lax.axis_index("head")
    mesh_blocks = encode_weights.shape[0]
    mesh_rows = mesh_blocks * BLOCK
    grid_blocks = grid_state.shape[0] // BLOCK
    rim = mesh_blocks * BLOCK
    core, place = band % 2, (band // 2 + 2 * (band // 8)) % 4
    position = place * 2 + core
    packed = pack_weights(position, expand_weights, shrink_weights, project_out)
    last, first, packed = lax.optimization_barrier(
        (grid_state[-rim:], grid_state[:rim], packed)
    )
    low = shifted(last, 1)
    high = shifted(first, -1)
    swapped, north, south = OVER(packed), NORTH(packed), SOUTH(packed)
    swapped_north, swapped_south = NORTH(swapped), SOUTH(swapped)
    far, swapped_far = NORTH(north), SOUTH(swapped_south)
    inward = [project_in[:, j, :].reshape(8, BLOCK, BLOCK) for j in range(3)]
    low, high, *inward = lax.optimization_barrier((low, high, *inward))
    mesh_start = encode(
        encode_index - (band * grid_blocks - mesh_blocks), low, grid_state, high, encode_weights
    )
    half = mesh_rows // 2
    mine = jnp.stack(
        [
            jnp.stack(pair)
            for pair in (
                (packed, swapped),
                (north, swapped_north),
                (south, swapped_south),
                (far, swapped_far),
            )
        ]
    )
    x, _, _ = lax.optimization_barrier((mesh_start, swapped_north, swapped_south))
    up, down = UP(mine), DOWN(mine)
    y, xa, xb, mine = lax.optimization_barrier((OVER(x), NORTH(x), SOUTH(x), mine))
    across = ACROSS(mine)
    from_south = NORTH(jnp.concatenate([xa[:half], y]))
    from_north = SOUTH(jnp.concatenate([xb[half:], y]))
    xc = jnp.concatenate([from_south[:half], from_north[:half]])
    slots = (x, y, xa, from_south, xb, from_north, xc, OVER(xc))
    partner = me ^ 1
    order = jnp.stack(
        [me, partner] + [(v + by) % 8 for by in (6, 2, 4) for v in (me, partner)]
    ).astype(jnp.int32)
    queries, keys_values, share = project(order, slots, first_gain, inward)
    upper, lower, up, down = lax.optimization_barrier(
        (keys_values[mesh_rows - REACH :], keys_values[:REACH], up, down)
    )
    below = shifted(upper, 1)
    above = shifted(lower, -1)
    edges = jnp.stack([band == 0, band == bands - 1]).astype(jnp.int32)
    context = attend(edges, queries, below, keys_values, above)
    context, *here = lax.optimization_barrier((context, mine, up, down, across))
    parts = here + [TWIN(v) for v in here]
    context = lax.all_to_all(
        context.reshape(8, mesh_rows // 8, BLOCK), "head", 0, 0, tiled=True
    )
    places = [
        ((place + by) % 4) * 2 + side for side in (core, 1 - core) for by in (0, 3, 1, 2)
    ]
    table = jnp.concatenate([order, jnp.stack(places).astype(jnp.int32)])
    mesh_end = forward(table, parts, context, share, second_gain)
    mesh_end = lax.all_to_all(mesh_end, "head", 0, 0, tiled=True)
    mesh_end = mesh_end.reshape(mesh_blocks, BLOCK, BLOCK)
    edge = mesh_blocks // 2
    back, sums = decode(
        decode_index - (band * mesh_blocks - edge),
        shifted(mesh_end[-edge:], 1),
        mesh_end,
        shifted(mesh_end[:edge], -1),
        decode_weights,
    )
    sums = lax.all_to_all(
        jnp.broadcast_to(sums, (8, *sums.shape)), "head", 0, 0, tiled=True
    )
    return finish(sums, back, grid_state, output_gain)


def solution(mesh):
    in_specs = (
        P("seq", "head"),
        P("seq", None),
        P("seq", None, None, None),
        P(),
        P(None, None, "head"),
        P("head", None),
        P(),
        P(None, "head"),
        P("head", None),
        P("seq", None),
        P("seq", None, None, None),
        P("head"),
    )
    return jax.shard_map(
        on_device, mesh=mesh, in_specs=in_specs, out_specs=P("seq", "head"), check_vma=False
    )
```

```python
import jax
import jax.numpy as jnp
from jax import lax
from jax.experimental import pallas as pl
from jax.experimental.pallas import tpu as pltpu
from jax.sharding import PartitionSpec as P

D = 1024
HEAD_DIM = 64
WINDOW = 1120
REACH = 1152
BLOCK = 128
EPSILON = 1e-05
LOG2E = 1.4426950408889634
BF = jnp.bfloat16
F32 = jnp.float32
NT = (((1,), (1,)), ((), ()))
TN = (((0,), (0,)), ((), ()))
MIB = 1 << 20


def params(mib):
    return pltpu.CompilerParams(
        dimension_semantics=("arbitrary",), vmem_limit_bytes=mib * MIB
    )


def dot(a, b):
    return jnp.dot(a, b, preferred_element_type=F32)


def cost(flops, moved, powers=0):
    return pl.CostEstimate(flops=flops, bytes_accessed=moved, transcendentals=powers)


ANY = pl.BlockSpec(memory_space=pl.ANY)
FAR = pl.BlockSpec(memory_space=pltpu.HBM)


def whole(shape):
    return pl.BlockSpec(shape, lambda i, *_: (0,) * len(shape))


def pieces_of(ref, target, start, count, sems, first):
    length = ref.shape[0] // count
    return [
        pltpu.make_async_copy(
            ref.at[pl.ds(n * length, length)],
            target.at[pl.ds(start + n * length, length)],
            sems.at[first + n],
        )
        for n in range(count)
    ]


def encode_kernel(index, low, own, high, weights, out, source, held, made, sems):
    rim, slots = low.shape[0], weights.shape[1]
    ahead = pieces_of(low, source, 0, 2, sems, 0)
    ahead += pieces_of(own, source, rim, 4, sems, 2)
    ahead += pieces_of(high, source, rim + own.shape[0], 2, sems, 6)
    count = weights.shape[0]
    blocks = pieces_of(weights, held, 0, count, sems, 8)
    back = pieces_of(made, out, 0, 4, sems, 8 + count)
    for c in ahead + blocks:
        c.start()
    for c in ahead:
        c.wait()
    for b in range(count):
        if b % 4 == 0:
            for c in blocks[b : b + 4]:
                c.wait()
        left = jnp.concatenate([held[b, k] for k in range(slots)], axis=1)
        right = jnp.concatenate([source[index[b, k]] for k in range(slots)], axis=0)
        made[b * BLOCK : (b + 1) * BLOCK] = dot(left, right).astype(BF)
        if (b + 1) % (count // 4) == 0:
            back[b // (count // 4)].start()
    for c in back:
        c.wait()


def encode(index, low, own, high, weights):
    count, slots = weights.shape[:2]
    blocks = own.shape[0] // BLOCK
    rim = low.shape[0] // BLOCK
    shaped = [v.reshape(-1, BLOCK, BLOCK) for v in (low, own, high)]
    return pl.pallas_call(
        encode_kernel,
        out_shape=jax.ShapeDtypeStruct((count * BLOCK, BLOCK), BF),
        grid_spec=pltpu.PrefetchScalarGridSpec(
            num_scalar_prefetch=1,
            grid=(1,),
            in_specs=[ANY, FAR, ANY, FAR],
            out_specs=ANY,
            scratch_shapes=[
                pltpu.VMEM((blocks + 2 * rim, BLOCK, BLOCK), BF),
                pltpu.VMEM((count, slots, BLOCK, BLOCK), BF),
                pltpu.VMEM((count * BLOCK, BLOCK), BF),
                pltpu.SemaphoreType.DMA((12 + count,)),
            ],
        ),
        compiler_params=params(56),
        cost_estimate=cost(540_000_000, 8_000_000),
        name="encode",
    )(index, *shaped, weights)


def project_kernel(
    order, s0, s1, s2, s3, s4, s5, s6, s7, gain, wq, wk, wv,
    queries, keys_values, share, lower, upper, ordered, normed,
):
    step = pl.program_id(0)

    @pl.when(step == 0)
    def _():
        for p in range(8):
            ordered[p * BLOCK : (p + 1) * BLOCK] = jnp.concatenate(
                [w[order[p]] for w in (wq, wk, wv)], axis=1
            )

    slots = (s0, s1, s2, s3, s4, s5, s6, s7)
    rows = s0.shape[0]
    tile = share.shape[1]
    for n in range(rows // tile):

        @pl.when(order[0] == step * (rows // tile) + n)
        def _():
            for p in range(8):
                share[order[p]] = slots[p][n * tile : (n + 1) * tile]

    gains = [gain[order[p]] for p in range(8)]
    few = 32
    for n in range(rows // few):
        at = slice(n * few, (n + 1) * few)
        pieces = [s[at].astype(F32) for s in slots]
        total = pieces[0]
        for x in pieces[1:]:
            total = total + x
        average = jnp.sum(total, axis=1, keepdims=True) * (1.0 / D)
        pieces = [x - average for x in pieces]
        total = pieces[0] * pieces[0]
        for x in pieces[1:]:
            total = total + x * x
        spread = lax.rsqrt(jnp.sum(total, axis=1, keepdims=True) * (1.0 / D) + EPSILON)
        for p, x in enumerate(pieces):
            normed[at, p * BLOCK : (p + 1) * BLOCK] = (x * spread * gains[p]).astype(BF)
    made = dot(normed[...], ordered[...])
    queries[...] = (made[:, :BLOCK] * (HEAD_DIM**-0.5 * LOG2E)).astype(BF)
    both = made[:, BLOCK:].astype(BF)
    keys_values[...] = both
    for n in range(4):
        start, stop = n * rows, (n + 1) * rows
        skip = 4 * rows - REACH

        @pl.when(step == n)
        def _():
            if start < REACH:
                lower[start : min(stop, REACH)] = both[: min(stop, REACH) - start]
            if stop > skip:
                upper[max(start, skip) - skip : stop - skip] = both[max(start, skip) - start :]


def project(order, slots, gain, weights):
    rows = slots[0].shape[0]
    tile, steps = rows // 8, 4
    each = rows // steps
    full = pl.BlockSpec((each, BLOCK), lambda i, _: (i, 0))
    second = pl.BlockSpec((each, BLOCK), lambda i, _: (i + steps // 2, 0))
    return pl.pallas_call(
        project_kernel,
        out_shape=(
            jax.ShapeDtypeStruct((rows, BLOCK), BF),
            jax.ShapeDtypeStruct((rows, 2 * BLOCK), BF),
            jax.ShapeDtypeStruct((8, tile, BLOCK), BF),
            jax.ShapeDtypeStruct((REACH, 2 * BLOCK), BF),
            jax.ShapeDtypeStruct((REACH, 2 * BLOCK), BF),
        ),
        grid_spec=pltpu.PrefetchScalarGridSpec(
            num_scalar_prefetch=1,
            grid=(steps,),
            in_specs=[full, full, full, second, full, second, full, full]
            + [whole((8, 1, BLOCK))]
            + [whole((8, BLOCK, BLOCK))] * 3,
            out_specs=(
                full,
                pl.BlockSpec((each, 2 * BLOCK), lambda i, _: (i, 0)),
                whole((8, tile, BLOCK)),
                whole((REACH, 2 * BLOCK)),
                whole((REACH, 2 * BLOCK)),
            ),
            scratch_shapes=[pltpu.VMEM((D, 3 * BLOCK), BF), pltpu.VMEM((each, D), BF)],
        ),
        compiler_params=params(56),
        name="project",
    )(order, *slots, gain.reshape(8, 1, BLOCK), *weights)


TILE = 256
SPAN = TILE + 2 * REACH
CHUNKS = SPAN // TILE


def attend_kernel(edges, queries, low, own, high, out, keys, values, scores, powers, sems):
    step = pl.program_id(0)
    rows = own.shape[0]

    @pl.when(step == 0)
    def _():
        copies = []
        for n, (part, start) in enumerate(
            ((low, 0), (own, REACH), (high, REACH + rows))
        ):
            for m, target in enumerate((keys, values)):
                copies.append(
                    pltpu.make_async_copy(
                        part.at[:, pl.ds(m * BLOCK, BLOCK)],
                        target.at[pl.ds(start, part.shape[0]), pl.ds(0, BLOCK)],
                        sems.at[2 * n + m],
                    )
                )
        for c in copies:
            c.start()
        first = lax.broadcasted_iota(jnp.int32, (keys.shape[0], BLOCK), 1) == 0
        row = lax.broadcasted_iota(jnp.int32, (keys.shape[0], BLOCK), 0)
        absent = ((row < REACH) & (edges[0] == 1)) | (
            (row >= REACH + rows) & (edges[1] == 1)
        )
        keys[:, BLOCK:] = jnp.where(first & absent, -1e30, 0.0).astype(BF)
        for c in copies:
            c.wait()
        both = values[:, :BLOCK]
        left = lax.broadcasted_iota(jnp.int32, both.shape, 1) < HEAD_DIM
        ones = jnp.ones_like(both)
        values[:, :BLOCK] = jnp.where(left, both, ones)
        values[:, BLOCK:] = jnp.where(left, ones, both)

    lane = lax.broadcasted_iota(jnp.int32, (TILE, BLOCK), 1)
    q = queries[...]
    zero = jnp.zeros_like(q)
    both = jnp.concatenate(
        [jnp.where(lane < HEAD_DIM, q, zero), jnp.where(lane < HEAD_DIM, zero, q)], axis=0
    )
    mark = jnp.where(
        lax.broadcasted_iota(jnp.int32, (2 * TILE, BLOCK), 1) == 0, 1.0, 0.0
    ).astype(BF)
    stacked = jnp.concatenate([both, mark], axis=1)
    row = lax.broadcasted_iota(jnp.int32, (2 * TILE, TILE), 0) & (TILE - 1)
    column = lax.broadcasted_iota(jnp.int32, (2 * TILE, TILE), 1)
    highest = jnp.full((2 * TILE, BLOCK), -1e30, F32)
    for c in range(CHUNKS):
        part = keys[pl.ds(pl.multiple_of((step + c) * TILE, TILE), TILE)]
        s = lax.dot_general(stacked, part, NT, preferred_element_type=F32)
        least = c * TILE - REACH
        gap = column - row + least
        if least - TILE < -WINDOW:
            s = jnp.where(gap >= -WINDOW, s, -1e30)
        if least + TILE > WINDOW:
            s = jnp.where(gap <= WINDOW, s, -1e30)
        scores[:, c * TILE : (c + 1) * TILE] = s
        highest = jnp.maximum(highest, jnp.maximum(s[:, :BLOCK], s[:, BLOCK:]))
    peak = jnp.max(highest, axis=1, keepdims=True)
    span = pl.ds(pl.multiple_of(step * TILE, TILE), SPAN)
    totals = []
    for h in range(2):
        rows_of = slice(h * TILE, (h + 1) * TILE)
        for c in range(CHUNKS):
            at = slice(c * TILE, (c + 1) * TILE)
            powers[rows_of, at] = jnp.exp2(scores[rows_of, at] - peak[rows_of]).astype(BF)
        totals.append(dot(powers[rows_of], values[span, h * BLOCK : (h + 1) * BLOCK]))
    made = jnp.where(lane < HEAD_DIM, totals[0], totals[1])
    sums = jnp.where(lane < HEAD_DIM, totals[1], totals[0])
    out[...] = (made / pltpu.roll(sums, HEAD_DIM, 1)).astype(BF)


def attend(edges, queries, low, own, high):
    rows = own.shape[0]
    return pl.pallas_call(
        attend_kernel,
        out_shape=jax.ShapeDtypeStruct((rows, BLOCK), BF),
        grid_spec=pltpu.PrefetchScalarGridSpec(
            num_scalar_prefetch=1,
            grid=(rows // TILE,),
            in_specs=[pl.BlockSpec((TILE, BLOCK), lambda i, _: (i, 0)), ANY, ANY, ANY],
            out_specs=pl.BlockSpec((TILE, BLOCK), lambda i, _: (i, 0)),
            scratch_shapes=[
                pltpu.VMEM((rows + 2 * REACH, 2 * BLOCK), BF),
                pltpu.VMEM((rows + 2 * REACH, 2 * BLOCK), BF),
                pltpu.VMEM((2 * TILE, SPAN), F32),
                pltpu.VMEM((2 * TILE, SPAN), BF),
                pltpu.SemaphoreType.DMA((6,)),
            ],
        ),
        compiler_params=params(56),
        name="attend",
    )(edges, queries, low, own, high)


ROWS_E = 64
ROWS_S = 64
ROWS_P = 16
PACK = ROWS_E + ROWS_S + ROWS_P


def pack_weights(position, expand, shrink, project_out):
    part = lax.dynamic_slice_in_dim(expand, position * 2 * ROWS_E, 2 * ROWS_E, 0)
    return jnp.concatenate(
        [
            jnp.concatenate([part[:ROWS_E], part[ROWS_E:]], axis=1),
            lax.dynamic_slice_in_dim(shrink, position * ROWS_S, ROWS_S, 0),
            lax.dynamic_slice_in_dim(project_out, position * ROWS_P, ROWS_P, 0),
        ],
        axis=0,
    )


def gelu(v):
    return 0.5 * v * (1.0 + jnp.tanh(0.7978845608028654 * (v + 0.044715 * v * v * v)))


def forward_kernel(table, *refs):
    parts = refs[:8]
    context, share, gain, out, expand, shrink, outward, sems = refs[8:]
    groups = ([], [], [])
    width = expand.shape[3]
    for n, part in enumerate(parts):
        where = table[8 + n]
        for side in range(2):
            slot = 1 - side if n % 4 == 3 else side

            def copy(group, source, target):
                groups[group].append(
                    pltpu.make_async_copy(source, target, sems.at[group, len(groups[group])])
                )

            copy(
                0,
                part.at[:, side, pl.ds(ROWS_E + ROWS_S, ROWS_P), :],
                outward.at[
                    :, slot, pl.ds(pl.multiple_of(where * ROWS_P, ROWS_P), ROWS_P), :
                ],
            )
            for piece in range(2):
                copy(
                    1,
                    part.at[:, side, pl.ds(0, ROWS_E), pl.ds(piece * width, width)],
                    expand.at[
                        :,
                        slot,
                        pl.ds(
                            pl.multiple_of(where * 2 * ROWS_E + piece * ROWS_E, ROWS_E), ROWS_E
                        ),
                        :,
                    ],
                )
            copy(
                2,
                part.at[:, side, pl.ds(ROWS_E, ROWS_S), :],
                shrink.at[:, slot, pl.ds(pl.multiple_of(where * ROWS_S, ROWS_S), ROWS_S), :],
            )
    for group in groups:
        for c in group:
            c.start()
    for c in groups[0]:
        c.wait()
    total = dot(context[table[0]], outward[0, 0])
    for p in range(1, 8):
        total = total + dot(context[table[p]], outward[p // 2, p % 2])
    start = jnp.concatenate([share[h] for h in range(8)], axis=1).astype(F32)
    middle = (start + total).astype(BF).astype(F32)
    average = jnp.mean(middle, axis=1, keepdims=True)
    centred = middle - average
    spread = jnp.mean(centred * centred, axis=1, keepdims=True)
    normed = (centred * lax.rsqrt(spread + EPSILON) * gain[...]).astype(BF)
    for c in groups[1]:
        c.wait()
    hidden = [gelu(dot(normed, expand[p // 2, p % 2])).astype(BF) for p in range(8)]
    for c in groups[2]:
        c.wait()
    total = middle
    for p in range(8):
        total = total + dot(hidden[p], shrink[p // 2, p % 2])
    done = total.astype(BF)
    for h in range(8):
        out[h] = done[:, h * BLOCK : (h + 1) * BLOCK]


def forward(table, parts, context, share, gain):
    rows = share.shape[1]
    width = D // 2
    return pl.pallas_call(
        forward_kernel,
        out_shape=jax.ShapeDtypeStruct((8, rows, BLOCK), BF),
        grid_spec=pltpu.PrefetchScalarGridSpec(
            num_scalar_prefetch=1,
            grid=(1,),
            in_specs=[ANY] * 8
            + [whole((8, rows, BLOCK)), whole((8, rows, BLOCK)), whole((1, D))],
            out_specs=whole((8, rows, BLOCK)),
            scratch_shapes=[
                pltpu.VMEM((4, 2, D, width), BF),
                pltpu.VMEM((4, 2, width, D), BF),
                pltpu.VMEM((4, 2, BLOCK, D), BF),
                pltpu.SemaphoreType.DMA((3, 32)),
            ],
        ),
        compiler_params=params(56),
        cost_estimate=cost(4_800_000_000, 20_000_000, 1_100_000),
        name="forward",
    )(table, *parts, context, share, gain.reshape(1, D))


EACH = 8


def decode_kernel(index, low, own, high, weights, back, sums, source, held, kept, sems):
    rim, slots = low.shape[0], weights.shape[1]
    steps = weights.shape[0] // EACH
    ahead = pieces_of(low, source, 0, 1, sems, 0)
    ahead += pieces_of(own, source, rim, 2, sems, 1)
    ahead += pieces_of(high, source, rim + own.shape[0], 1, sems, 3)
    blocks = pieces_of(weights, held, 0, 2 * steps, sems, 4)
    done = pieces_of(kept, back, 0, steps, sems, 4 + 2 * steps)
    for c in ahead + blocks:
        c.start()
    for c in ahead:
        c.wait()
    row = lax.broadcasted_iota(jnp.int32, (BLOCK, BLOCK), 0)
    column = lax.broadcasted_iota(jnp.int32, (BLOCK, BLOCK), 1)
    for step in range(steps):
        blocks[2 * step].wait()
        blocks[2 * step + 1].wait()
        kinds = []
        for b in range(step * EACH, (step + 1) * EACH):
            left = jnp.concatenate([held[b, k] for k in range(slots)], axis=1)
            right = jnp.concatenate([source[index[b, k]] for k in range(slots)], axis=0)
            made = dot(left, right)
            kept[b * BLOCK : (b + 1) * BLOCK] = made.astype(BF)
            kinds.append((made, made * made))
        done[step].start()
        held_sums = [
            jnp.sum(
                jnp.where(row == column, jnp.sum(kinds[b][n], axis=1, keepdims=True), 0.0),
                axis=0,
                keepdims=True,
            )
            for n in range(2)
            for b in range(EACH)
        ]
        sums[step] = jnp.concatenate(held_sums, axis=0).astype(BF)
    for c in done:
        c.wait()


def decode(index, low, own, high, weights):
    count, slots = weights.shape[:2]
    blocks = own.shape[0]
    rim = low.shape[0]
    steps = count // EACH
    return pl.pallas_call(
        decode_kernel,
        out_shape=(
            jax.ShapeDtypeStruct((count * BLOCK, BLOCK), BF),
            jax.ShapeDtypeStruct((steps, 2 * EACH, BLOCK), BF),
        ),
        grid_spec=pltpu.PrefetchScalarGridSpec(
            num_scalar_prefetch=1,
            grid=(1,),
            in_specs=[ANY, ANY, ANY, FAR],
            out_specs=(ANY, whole((steps, 2 * EACH, BLOCK))),
            scratch_shapes=[
                pltpu.VMEM((blocks + 2 * rim, BLOCK, BLOCK), BF),
                pltpu.VMEM((count, slots, BLOCK, BLOCK), BF),
                pltpu.VMEM((count * BLOCK, BLOCK), BF),
                pltpu.SemaphoreType.DMA((4 + 3 * steps,)),
            ],
        ),
        compiler_params=params(56),
        cost_estimate=cost(540_000_000, 10_000_000),
        name="decode",
    )(index, low, own, high, weights)


def finish_kernel(sums, back, state, gain, out, stats, kept, base, made, sems):
    steps = sums.shape[1]
    count = sums.shape[0]
    first = pieces_of(sums, stats, 0, count, sems, 0)
    backs = pieces_of(back, kept, 0, steps, sems, count)
    states = pieces_of(state, base, 0, steps, sems, count + steps)
    outs = pieces_of(made, out, 0, steps, sems, count + 2 * steps)
    for c in first:
        c.start()
    for a, b in zip(backs, states):
        a.start()
        b.start()
    depth = count * 2 * EACH
    row = lax.broadcasted_iota(jnp.int32, (depth, 2 * EACH * BLOCK), 0)
    column = lax.broadcasted_iota(jnp.int32, (depth, 2 * EACH * BLOCK), 1)
    pick = jnp.where((row % (2 * EACH)) == (column // BLOCK), 1.0 / D, 0.0).astype(BF)
    for c in first:
        c.wait()
    for step in range(steps):
        parts = jnp.concatenate([stats[h, step] for h in range(count)], axis=0)
        spread = lax.dot_general(parts, pick, TN, preferred_element_type=F32)
        backs[step].wait()
        states[step].wait()
        for b in range(EACH):
            at = (step * EACH + b) * BLOCK
            average = spread[:, b * BLOCK : (b + 1) * BLOCK]
            squares = spread[:, (EACH + b) * BLOCK : (EACH + b + 1) * BLOCK]
            scale = lax.rsqrt(squares - average * average + EPSILON) * gain[...]
            made[at : at + BLOCK] = (
                base[at : at + BLOCK].astype(F32)
                + (kept[at : at + BLOCK].astype(F32) - average) * scale
            ).astype(BF)
        outs[step].start()
    for c in outs:
        c.wait()


def finish(sums, back, state, gain):
    rows = state.shape[0]
    count, steps = sums.shape[:2]
    return pl.pallas_call(
        finish_kernel,
        out_shape=jax.ShapeDtypeStruct((rows, BLOCK), BF),
        grid_spec=pl.GridSpec(
            grid=(1,),
            in_specs=[ANY, ANY, FAR, whole((1, BLOCK))],
            out_specs=ANY,
            scratch_shapes=[
                pltpu.VMEM(sums.shape, BF),
                pltpu.VMEM((rows, BLOCK), BF),
                pltpu.VMEM((rows, BLOCK), BF),
                pltpu.VMEM((rows, BLOCK), BF),
                pltpu.SemaphoreType.DMA((count + 3 * steps,)),
            ],
        ),
        compiler_params=params(56),
        cost_estimate=cost(540_000_000, 8_000_000),
        name="finish",
    )(sums, back, state, gain.reshape(1, BLOCK))


def shifted(value, by):
    return lax.ppermute(value, "seq", [(i, i + by) for i in range(16) if 0 <= i + by < 16])


def among(value, axis, count, to):
    return lax.ppermute(value, axis, [(i, to(i)) for i in range(count)])


def along_z(i, by):
    return (i // 8) * 8 + ((i // 2 + by) % 4) * 2 + i % 2


UP = lambda v: among(v, "seq", 16, lambda i: along_z(i, 1))
DOWN = lambda v: among(v, "seq", 16, lambda i: along_z(i, -1))
ACROSS = lambda v: among(v, ("seq", "head"), 128, lambda i: i ^ 65)
TWIN = lambda v: among(v, "seq", 16, lambda i: i ^ 1)
NORTH = lambda v: among(v, "head", 8, lambda i: (i + 2) % 8)
SOUTH = lambda v: among(v, "head", 8, lambda i: (i - 2) % 8)
OVER = lambda v: among(v, "head", 8, lambda i: i ^ 1)


def on_device(
    grid_state,
    encode_index,
    encode_weights,
    first_gain,
    project_in,
    project_out,
    second_gain,
    expand_weights,
    shrink_weights,
    decode_index,
    decode_weights,
    output_gain,
):
    band = lax.axis_index("seq")
    bands = lax.axis_size("seq")
    me = lax.axis_index("head")
    mesh_blocks = encode_weights.shape[0]
    mesh_rows = mesh_blocks * BLOCK
    grid_blocks = grid_state.shape[0] // BLOCK
    rim = mesh_blocks * BLOCK
    core, place = band % 2, (band // 2 + 2 * (band // 8)) % 4
    position = place * 2 + core
    packed = pack_weights(position, expand_weights, shrink_weights, project_out)
    last, first, packed = lax.optimization_barrier(
        (grid_state[-rim:], grid_state[:rim], packed)
    )
    low = shifted(last, 1)
    high = shifted(first, -1)
    swapped, north, south = OVER(packed), NORTH(packed), SOUTH(packed)
    swapped_north, swapped_south = NORTH(swapped), SOUTH(swapped)
    far, swapped_far = NORTH(north), SOUTH(swapped_south)
    inward = [project_in[:, j, :].reshape(8, BLOCK, BLOCK) for j in range(3)]
    low, high, *inward = lax.optimization_barrier((low, high, *inward))
    mesh_start = encode(
        encode_index - (band * grid_blocks - mesh_blocks), low, grid_state, high, encode_weights
    )
    half = mesh_rows // 2
    mine = jnp.stack(
        [
            jnp.stack(pair)
            for pair in (
                (packed, swapped),
                (north, swapped_north),
                (south, swapped_south),
                (far, swapped_far),
            )
        ]
    )
    x, _, _ = lax.optimization_barrier((mesh_start, swapped_north, swapped_south))
    up, down = UP(mine), DOWN(mine)
    y, xa, xb, mine = lax.optimization_barrier((OVER(x), NORTH(x), SOUTH(x), mine))
    across = ACROSS(mine)
    from_south = NORTH(jnp.concatenate([xa[:half], y]))
    from_north = SOUTH(jnp.concatenate([xb[half:], y]))
    xc = jnp.concatenate([from_south[:half], from_north[:half]])
    slots = (x, y, xa, from_south, xb, from_north, xc, OVER(xc))
    partner = me ^ 1
    order = jnp.stack(
        [me, partner] + [(v + by) % 8 for by in (6, 2, 4) for v in (me, partner)]
    ).astype(jnp.int32)
    queries, keys_values, share, lower, upper = project(order, slots, first_gain, inward)
    upper, lower, up, down = lax.optimization_barrier(
        (upper, lower, up, down)
    )
    below = shifted(upper, 1)
    above = shifted(lower, -1)
    edges = jnp.stack([band == 0, band == bands - 1]).astype(jnp.int32)
    context = attend(edges, queries, below, keys_values, above)
    context, *here = lax.optimization_barrier((context, mine, up, down, across))
    parts = here + [TWIN(v) for v in here]
    context = lax.all_to_all(
        context.reshape(8, mesh_rows // 8, BLOCK), "head", 0, 0, tiled=True
    )
    places = [
        ((place + by) % 4) * 2 + side for side in (core, 1 - core) for by in (0, 3, 1, 2)
    ]
    table = jnp.concatenate([order, jnp.stack(places).astype(jnp.int32)])
    mesh_end = forward(table, parts, context, share, second_gain)
    mesh_end = lax.all_to_all(mesh_end, "head", 0, 0, tiled=True)
    mesh_end = mesh_end.reshape(mesh_blocks, BLOCK, BLOCK)
    edge = mesh_blocks // 2
    back, sums = decode(
        decode_index - (band * mesh_blocks - edge),
        shifted(mesh_end[-edge:], 1),
        mesh_end,
        shifted(mesh_end[:edge], -1),
        decode_weights,
    )
    sums = lax.all_to_all(
        jnp.broadcast_to(sums, (8, *sums.shape)), "head", 0, 0, tiled=True
    )
    return finish(sums, back, grid_state, output_gain)


def solution(mesh):
    in_specs = (
        P("seq", "head"),
        P("seq", None),
        P("seq", None, None, None),
        P(),
        P(None, None, "head"),
        P("head", None),
        P(),
        P(None, "head"),
        P("head", None),
        P("seq", None),
        P("seq", None, None, None),
        P("head"),
    )
    return jax.shard_map(
        on_device, mesh=mesh, in_specs=in_specs, out_specs=P("seq", "head"), check_vma=False
    )
```

```python
import jax
import jax.numpy as jnp
from jax import lax
from jax.experimental import pallas as pl
from jax.experimental.pallas import tpu as pltpu
from jax.sharding import PartitionSpec as P

D = 1024
HEAD_DIM = 64
WINDOW = 1120
REACH = 1152
BLOCK = 128
EPSILON = 1e-05
LOG2E = 1.4426950408889634
BF = jnp.bfloat16
F32 = jnp.float32
NT = (((1,), (1,)), ((), ()))
TN = (((0,), (0,)), ((), ()))
MIB = 1 << 20


def params(mib):
    return pltpu.CompilerParams(
        dimension_semantics=("arbitrary",), vmem_limit_bytes=mib * MIB
    )


def dot(a, b):
    return jnp.dot(a, b, preferred_element_type=F32)


def cost(flops, moved, powers=0):
    return pl.CostEstimate(flops=flops, bytes_accessed=moved, transcendentals=powers)


ANY = pl.BlockSpec(memory_space=pl.ANY)
FAR = pl.BlockSpec(memory_space=pltpu.HBM)


def whole(shape):
    return pl.BlockSpec(shape, lambda i, *_: (0,) * len(shape))


def pieces_of(ref, target, start, count, sems, first):
    length = ref.shape[0] // count
    return [
        pltpu.make_async_copy(
            ref.at[pl.ds(n * length, length)],
            target.at[pl.ds(start + n * length, length)],
            sems.at[first + n],
        )
        for n in range(count)
    ]


def encode_kernel(index, low, own, high, weights, out, source, held, made, sems):
    rim, slots = low.shape[0], weights.shape[1]
    ahead = pieces_of(low, source, 0, 2, sems, 0)
    ahead += pieces_of(own, source, rim, 4, sems, 2)
    ahead += pieces_of(high, source, rim + own.shape[0], 2, sems, 6)
    count = weights.shape[0]
    blocks = pieces_of(weights, held, 0, count, sems, 8)
    back = pieces_of(made, out, 0, 4, sems, 8 + count)
    for c in ahead + blocks:
        c.start()
    for c in ahead:
        c.wait()
    for b in range(count):
        if b % 4 == 0:
            for c in blocks[b : b + 4]:
                c.wait()
        left = jnp.concatenate([held[b, k] for k in range(slots)], axis=1)
        right = jnp.concatenate([source[index[b, k]] for k in range(slots)], axis=0)
        made[b * BLOCK : (b + 1) * BLOCK] = dot(left, right).astype(BF)
        if (b + 1) % (count // 4) == 0:
            back[b // (count // 4)].start()
    for c in back:
        c.wait()


def encode(index, low, own, high, weights):
    count, slots = weights.shape[:2]
    blocks = own.shape[0] // BLOCK
    rim = low.shape[0] // BLOCK
    shaped = [v.reshape(-1, BLOCK, BLOCK) for v in (low, own, high)]
    return pl.pallas_call(
        encode_kernel,
        out_shape=jax.ShapeDtypeStruct((count * BLOCK, BLOCK), BF),
        grid_spec=pltpu.PrefetchScalarGridSpec(
            num_scalar_prefetch=1,
            grid=(1,),
            in_specs=[ANY, FAR, ANY, FAR],
            out_specs=ANY,
            scratch_shapes=[
                pltpu.VMEM((blocks + 2 * rim, BLOCK, BLOCK), BF),
                pltpu.VMEM((count, slots, BLOCK, BLOCK), BF),
                pltpu.VMEM((count * BLOCK, BLOCK), BF),
                pltpu.SemaphoreType.DMA((12 + count,)),
            ],
        ),
        compiler_params=params(56),
        cost_estimate=cost(540_000_000, 8_000_000),
        name="encode",
    )(index, *shaped, weights)


def project_kernel(
    order, s0, s1, s2, s3, s4, s5, s6, s7, gain, wq, wk, wv,
    queries, keys_values, share, lower, upper, ordered, normed,
):
    step = pl.program_id(0)

    @pl.when(step == 0)
    def _():
        for p in range(8):
            ordered[p * BLOCK : (p + 1) * BLOCK] = jnp.concatenate(
                [w[order[p]] for w in (wq, wk, wv)], axis=1
            )

    slots = (s0, s1, s2, s3, s4, s5, s6, s7)
    rows = s0.shape[0]
    tile = share.shape[1]
    for n in range(rows // tile):

        @pl.when(order[0] == step * (rows // tile) + n)
        def _():
            for p in range(8):
                share[order[p]] = slots[p][n * tile : (n + 1) * tile]

    gains = [gain[order[p]] for p in range(8)]
    few = 32
    for n in range(rows // few):
        at = slice(n * few, (n + 1) * few)
        pieces = [s[at].astype(F32) for s in slots]
        total = pieces[0]
        for x in pieces[1:]:
            total = total + x
        average = jnp.sum(total, axis=1, keepdims=True) * (1.0 / D)
        pieces = [x - average for x in pieces]
        total = pieces[0] * pieces[0]
        for x in pieces[1:]:
            total = total + x * x
        spread = lax.rsqrt(jnp.sum(total, axis=1, keepdims=True) * (1.0 / D) + EPSILON)
        for p, x in enumerate(pieces):
            normed[at, p * BLOCK : (p + 1) * BLOCK] = (x * spread * gains[p]).astype(BF)
    made = dot(normed[...], ordered[...])
    queries[...] = (made[:, :BLOCK] * (HEAD_DIM**-0.5 * LOG2E)).astype(BF)
    both = made[:, BLOCK:].astype(BF)
    keys_values[...] = both
    for n in range(4):
        start, stop = n * rows, (n + 1) * rows
        skip = 4 * rows - REACH

        @pl.when(step == n)
        def _():
            if start < REACH:
                lower[start : min(stop, REACH)] = both[: min(stop, REACH) - start]
            if stop > skip:
                upper[max(start, skip) - skip : stop - skip] = both[max(start, skip) - start :]


def project(order, slots, gain, weights):
    rows = slots[0].shape[0]
    tile, steps = rows // 8, 4
    each = rows // steps
    full = pl.BlockSpec((each, BLOCK), lambda i, _: (i, 0))
    second = pl.BlockSpec((each, BLOCK), lambda i, _: (i + steps // 2, 0))
    return pl.pallas_call(
        project_kernel,
        out_shape=(
            jax.ShapeDtypeStruct((rows, BLOCK), BF),
            jax.ShapeDtypeStruct((rows, 2 * BLOCK), BF),
            jax.ShapeDtypeStruct((8, tile, BLOCK), BF),
            jax.ShapeDtypeStruct((REACH, 2 * BLOCK), BF),
            jax.ShapeDtypeStruct((REACH, 2 * BLOCK), BF),
        ),
        grid_spec=pltpu.PrefetchScalarGridSpec(
            num_scalar_prefetch=1,
            grid=(steps,),
            in_specs=[full, full, full, second, full, second, full, full]
            + [whole((8, 1, BLOCK))]
            + [whole((8, BLOCK, BLOCK))] * 3,
            out_specs=(
                full,
                pl.BlockSpec((each, 2 * BLOCK), lambda i, _: (i, 0)),
                whole((8, tile, BLOCK)),
                whole((REACH, 2 * BLOCK)),
                whole((REACH, 2 * BLOCK)),
            ),
            scratch_shapes=[pltpu.VMEM((D, 3 * BLOCK), BF), pltpu.VMEM((each, D), BF)],
        ),
        compiler_params=params(56),
        name="project",
    )(order, *slots, gain.reshape(8, 1, BLOCK), *weights)


TILE = 256
SPAN = TILE + 2 * REACH
CHUNKS = SPAN // TILE


def attend_kernel(edges, queries, low, own, high, out, keys, values, scores, powers, sems):
    step = pl.program_id(0)
    rows = own.shape[0]

    @pl.when(step == 0)
    def _():
        copies = []
        for n, (part, start) in enumerate(
            ((low, 0), (own, REACH), (high, REACH + rows))
        ):
            for m, target in enumerate((keys, values)):
                copies.append(
                    pltpu.make_async_copy(
                        part.at[:, pl.ds(m * BLOCK, BLOCK)],
                        target.at[pl.ds(start, part.shape[0]), pl.ds(0, BLOCK)],
                        sems.at[2 * n + m],
                    )
                )
        for c in copies:
            c.start()
        first = lax.broadcasted_iota(jnp.int32, (keys.shape[0], BLOCK), 1) == 0
        row = lax.broadcasted_iota(jnp.int32, (keys.shape[0], BLOCK), 0)
        absent = ((row < REACH) & (edges[0] == 1)) | (
            (row >= REACH + rows) & (edges[1] == 1)
        )
        keys[:, BLOCK:] = jnp.where(first & absent, -1e30, 0.0).astype(BF)
        for c in copies:
            c.wait()
        both = values[:, :BLOCK]
        left = lax.broadcasted_iota(jnp.int32, both.shape, 1) < HEAD_DIM
        ones = jnp.ones_like(both)
        values[:, :BLOCK] = jnp.where(left, both, ones)
        values[:, BLOCK:] = jnp.where(left, ones, both)

    lane = lax.broadcasted_iota(jnp.int32, (TILE, BLOCK), 1)
    q = queries[...]
    zero = jnp.zeros_like(q)
    both = jnp.concatenate(
        [jnp.where(lane < HEAD_DIM, q, zero), jnp.where(lane < HEAD_DIM, zero, q)], axis=0
    )
    mark = jnp.where(
        lax.broadcasted_iota(jnp.int32, (2 * TILE, BLOCK), 1) == 0, 1.0, 0.0
    ).astype(BF)
    stacked = jnp.concatenate([both, mark], axis=1)
    row = lax.broadcasted_iota(jnp.int32, (2 * TILE, TILE), 0) & (TILE - 1)
    column = lax.broadcasted_iota(jnp.int32, (2 * TILE, TILE), 1)
    highest = jnp.full((2 * TILE, BLOCK), -1e30, F32)
    for c in range(CHUNKS):
        part = keys[pl.ds(pl.multiple_of((step + c) * TILE, TILE), TILE)]
        s = lax.dot_general(stacked, part, NT, preferred_element_type=F32)
        least = c * TILE - REACH
        gap = column - row + least
        if least - TILE < -WINDOW:
            s = jnp.where(gap >= -WINDOW, s, -1e30)
        if least + TILE > WINDOW:
            s = jnp.where(gap <= WINDOW, s, -1e30)
        scores[:, c * TILE : (c + 1) * TILE] = s
        highest = jnp.maximum(highest, jnp.maximum(s[:, :BLOCK], s[:, BLOCK:]))
    peak = jnp.max(highest, axis=1, keepdims=True)
    span = pl.ds(pl.multiple_of(step * TILE, TILE), SPAN)
    totals = []
    for h in range(2):
        rows_of = slice(h * TILE, (h + 1) * TILE)
        for c in range(CHUNKS):
            at = slice(c * TILE, (c + 1) * TILE)
            powers[rows_of, at] = jnp.exp2(scores[rows_of, at] - peak[rows_of]).astype(BF)
        totals.append(dot(powers[rows_of], values[span, h * BLOCK : (h + 1) * BLOCK]))
    made = jnp.where(lane < HEAD_DIM, totals[0], totals[1])
    sums = jnp.where(lane < HEAD_DIM, totals[1], totals[0])
    out[...] = (made / pltpu.roll(sums, HEAD_DIM, 1)).astype(BF)


def attend(edges, queries, low, own, high):
    rows = own.shape[0]
    return pl.pallas_call(
        attend_kernel,
        out_shape=jax.ShapeDtypeStruct((rows, BLOCK), BF),
        grid_spec=pltpu.PrefetchScalarGridSpec(
            num_scalar_prefetch=1,
            grid=(rows // TILE,),
            in_specs=[pl.BlockSpec((TILE, BLOCK), lambda i, _: (i, 0)), ANY, ANY, ANY],
            out_specs=pl.BlockSpec((TILE, BLOCK), lambda i, _: (i, 0)),
            scratch_shapes=[
                pltpu.VMEM((rows + 2 * REACH, 2 * BLOCK), BF),
                pltpu.VMEM((rows + 2 * REACH, 2 * BLOCK), BF),
                pltpu.VMEM((2 * TILE, SPAN), F32),
                pltpu.VMEM((2 * TILE, SPAN), BF),
                pltpu.SemaphoreType.DMA((6,)),
            ],
        ),
        compiler_params=params(56),
        name="attend",
    )(edges, queries, low, own, high)


ROWS_E = 64
ROWS_S = 64
ROWS_P = 16
PACK = ROWS_E + ROWS_S + ROWS_P


def pack_weights(position, expand, shrink, project_out):
    part = lax.dynamic_slice_in_dim(expand, position * 2 * ROWS_E, 2 * ROWS_E, 0)
    return jnp.concatenate(
        [
            jnp.concatenate([part[:ROWS_E], part[ROWS_E:]], axis=1),
            lax.dynamic_slice_in_dim(shrink, position * ROWS_S, ROWS_S, 0),
            lax.dynamic_slice_in_dim(project_out, position * ROWS_P, ROWS_P, 0),
        ],
        axis=0,
    )


def gelu(v):
    return 0.5 * v * (1.0 + jnp.tanh(0.7978845608028654 * (v + 0.044715 * v * v * v)))


def forward_kernel(table, *refs):
    parts = refs[:8]
    context, share, gain, out, expand, shrink, outward, sems = refs[8:]
    groups = ([], [], [])
    width = expand.shape[3]
    for n, part in enumerate(parts):
        where = table[8 + n]
        for side in range(2):
            slot = 1 - side if n % 4 == 3 else side

            def copy(group, source, target):
                groups[group].append(
                    pltpu.make_async_copy(source, target, sems.at[group, len(groups[group])])
                )

            copy(
                0,
                part.at[:, side, pl.ds(ROWS_E + ROWS_S, ROWS_P), :],
                outward.at[
                    :, slot, pl.ds(pl.multiple_of(where * ROWS_P, ROWS_P), ROWS_P), :
                ],
            )
            for piece in range(2):
                copy(
                    1,
                    part.at[:, side, pl.ds(0, ROWS_E), pl.ds(piece * width, width)],
                    expand.at[
                        :,
                        slot,
                        pl.ds(
                            pl.multiple_of(where * 2 * ROWS_E + piece * ROWS_E, ROWS_E), ROWS_E
                        ),
                        :,
                    ],
                )
            copy(
                2,
                part.at[:, side, pl.ds(ROWS_E, ROWS_S), :],
                shrink.at[:, slot, pl.ds(pl.multiple_of(where * ROWS_S, ROWS_S), ROWS_S), :],
            )
    for group in groups:
        for c in group:
            c.start()
    for c in groups[0]:
        c.wait()
    total = dot(context[table[0]], outward[0, 0])
    for p in range(1, 8):
        total = total + dot(context[table[p]], outward[p // 2, p % 2])
    start = jnp.concatenate([share[h] for h in range(8)], axis=1).astype(F32)
    middle = (start + total).astype(BF).astype(F32)
    average = jnp.mean(middle, axis=1, keepdims=True)
    centred = middle - average
    spread = jnp.mean(centred * centred, axis=1, keepdims=True)
    normed = (centred * lax.rsqrt(spread + EPSILON) * gain[...]).astype(BF)
    for c in groups[1]:
        c.wait()
    hidden = [gelu(dot(normed, expand[p // 2, p % 2])).astype(BF) for p in range(8)]
    for c in groups[2]:
        c.wait()
    total = middle
    for p in range(8):
        total = total + dot(hidden[p], shrink[p // 2, p % 2])
    done = total.astype(BF)
    for h in range(8):
        out[h] = done[:, h * BLOCK : (h + 1) * BLOCK]


def forward(table, parts, context, share, gain):
    rows = share.shape[1]
    width = D // 2
    return pl.pallas_call(
        forward_kernel,
        out_shape=jax.ShapeDtypeStruct((8, rows, BLOCK), BF),
        grid_spec=pltpu.PrefetchScalarGridSpec(
            num_scalar_prefetch=1,
            grid=(1,),
            in_specs=[ANY] * 8
            + [whole((8, rows, BLOCK)), whole((8, rows, BLOCK)), whole((1, D))],
            out_specs=whole((8, rows, BLOCK)),
            scratch_shapes=[
                pltpu.VMEM((4, 2, D, width), BF),
                pltpu.VMEM((4, 2, width, D), BF),
                pltpu.VMEM((4, 2, BLOCK, D), BF),
                pltpu.SemaphoreType.DMA((3, 32)),
            ],
        ),
        compiler_params=params(56),
        cost_estimate=cost(4_800_000_000, 20_000_000, 1_100_000),
        name="forward",
    )(table, *parts, context, share, gain.reshape(1, D))


EACH = 8


def decode_kernel(index, low, own, high, weights, back, sums, source, held, kept, sems):
    rim, slots = low.shape[0], weights.shape[1]
    steps = weights.shape[0] // EACH
    ahead = pieces_of(low, source, 0, 1, sems, 0)
    ahead += pieces_of(own, source, rim, 2, sems, 1)
    ahead += pieces_of(high, source, rim + own.shape[0], 1, sems, 3)
    blocks = pieces_of(weights, held, 0, 2 * steps, sems, 4)
    done = pieces_of(kept, back, 0, steps, sems, 4 + 2 * steps)
    for c in ahead + blocks:
        c.start()
    for c in ahead:
        c.wait()
    row = lax.broadcasted_iota(jnp.int32, (BLOCK, BLOCK), 0)
    column = lax.broadcasted_iota(jnp.int32, (BLOCK, BLOCK), 1)
    for step in range(steps):
        if step % 2 == 0:
            for c in blocks[2 * step : 2 * step + 4]:
                c.wait()
        kinds = []
        for b in range(step * EACH, (step + 1) * EACH):
            left = jnp.concatenate([held[b, k] for k in range(slots)], axis=1)
            right = jnp.concatenate([source[index[b, k]] for k in range(slots)], axis=0)
            made = dot(left, right)
            kept[b * BLOCK : (b + 1) * BLOCK] = made.astype(BF)
            kinds.append((made, made * made))
        done[step].start()
        held_sums = [
            jnp.sum(
                jnp.where(row == column, jnp.sum(kinds[b][n], axis=1, keepdims=True), 0.0),
                axis=0,
                keepdims=True,
            )
            for n in range(2)
            for b in range(EACH)
        ]
        sums[step] = jnp.concatenate(held_sums, axis=0).astype(BF)
    for c in done:
        c.wait()


def decode(index, low, own, high, weights):
    count, slots = weights.shape[:2]
    blocks = own.shape[0]
    rim = low.shape[0]
    steps = count // EACH
    return pl.pallas_call(
        decode_kernel,
        out_shape=(
            jax.ShapeDtypeStruct((count * BLOCK, BLOCK), BF),
            jax.ShapeDtypeStruct((steps, 2 * EACH, BLOCK), BF),
        ),
        grid_spec=pltpu.PrefetchScalarGridSpec(
            num_scalar_prefetch=1,
            grid=(1,),
            in_specs=[ANY, ANY, ANY, FAR],
            out_specs=(ANY, whole((steps, 2 * EACH, BLOCK))),
            scratch_shapes=[
                pltpu.VMEM((blocks + 2 * rim, BLOCK, BLOCK), BF),
                pltpu.VMEM((count, slots, BLOCK, BLOCK), BF),
                pltpu.VMEM((count * BLOCK, BLOCK), BF),
                pltpu.SemaphoreType.DMA((4 + 3 * steps,)),
            ],
        ),
        compiler_params=params(56),
        cost_estimate=cost(540_000_000, 10_000_000),
        name="decode",
    )(index, low, own, high, weights)


def finish_kernel(sums, back, state, gain, out, stats, kept, base, made, sems):
    steps = sums.shape[1]
    count = sums.shape[0]
    first = pieces_of(sums, stats, 0, count, sems, 0)
    backs = pieces_of(back, kept, 0, steps, sems, count)
    states = pieces_of(state, base, 0, steps, sems, count + steps)
    outs = pieces_of(made, out, 0, steps, sems, count + 2 * steps)
    for c in first:
        c.start()
    for a, b in zip(backs, states):
        a.start()
        b.start()
    depth = count * 2 * EACH
    row = lax.broadcasted_iota(jnp.int32, (depth, 2 * EACH * BLOCK), 0)
    column = lax.broadcasted_iota(jnp.int32, (depth, 2 * EACH * BLOCK), 1)
    pick = jnp.where((row % (2 * EACH)) == (column // BLOCK), 1.0 / D, 0.0).astype(BF)
    for c in first:
        c.wait()
    for step in range(steps):
        parts = jnp.concatenate([stats[h, step] for h in range(count)], axis=0)
        spread = lax.dot_general(parts, pick, TN, preferred_element_type=F32)
        if step % 2 == 0:
            for c in backs[step : step + 2] + states[step : step + 2]:
                c.wait()
        for b in range(EACH):
            at = (step * EACH + b) * BLOCK
            average = spread[:, b * BLOCK : (b + 1) * BLOCK]
            squares = spread[:, (EACH + b) * BLOCK : (EACH + b + 1) * BLOCK]
            scale = lax.rsqrt(squares - average * average + EPSILON) * gain[...]
            made[at : at + BLOCK] = (
                base[at : at + BLOCK].astype(F32)
                + (kept[at : at + BLOCK].astype(F32) - average) * scale
            ).astype(BF)
        outs[step].start()
    for c in outs:
        c.wait()


def finish(sums, back, state, gain):
    rows = state.shape[0]
    count, steps = sums.shape[:2]
    return pl.pallas_call(
        finish_kernel,
        out_shape=jax.ShapeDtypeStruct((rows, BLOCK), BF),
        grid_spec=pl.GridSpec(
            grid=(1,),
            in_specs=[ANY, ANY, FAR, whole((1, BLOCK))],
            out_specs=ANY,
            scratch_shapes=[
                pltpu.VMEM(sums.shape, BF),
                pltpu.VMEM((rows, BLOCK), BF),
                pltpu.VMEM((rows, BLOCK), BF),
                pltpu.VMEM((rows, BLOCK), BF),
                pltpu.SemaphoreType.DMA((count + 3 * steps,)),
            ],
        ),
        compiler_params=params(56),
        cost_estimate=cost(540_000_000, 8_000_000),
        name="finish",
    )(sums, back, state, gain.reshape(1, BLOCK))


def shifted(value, by):
    return lax.ppermute(value, "seq", [(i, i + by) for i in range(16) if 0 <= i + by < 16])


def among(value, axis, count, to):
    return lax.ppermute(value, axis, [(i, to(i)) for i in range(count)])


def along_z(i, by):
    return (i // 8) * 8 + ((i // 2 + by) % 4) * 2 + i % 2


UP = lambda v: among(v, "seq", 16, lambda i: along_z(i, 1))
DOWN = lambda v: among(v, "seq", 16, lambda i: along_z(i, -1))
ACROSS = lambda v: among(v, ("seq", "head"), 128, lambda i: i ^ 65)
TWIN = lambda v: among(v, "seq", 16, lambda i: i ^ 1)
NORTH = lambda v: among(v, "head", 8, lambda i: (i + 2) % 8)
SOUTH = lambda v: among(v, "head", 8, lambda i: (i - 2) % 8)
OVER = lambda v: among(v, "head", 8, lambda i: i ^ 1)


def on_device(
    grid_state,
    encode_index,
    encode_weights,
    first_gain,
    project_in,
    project_out,
    second_gain,
    expand_weights,
    shrink_weights,
    decode_index,
    decode_weights,
    output_gain,
):
    band = lax.axis_index("seq")
    bands = lax.axis_size("seq")
    me = lax.axis_index("head")
    mesh_blocks = encode_weights.shape[0]
    mesh_rows = mesh_blocks * BLOCK
    grid_blocks = grid_state.shape[0] // BLOCK
    rim = mesh_blocks * BLOCK
    core, place = band % 2, (band // 2 + 2 * (band // 8)) % 4
    position = place * 2 + core
    packed = pack_weights(position, expand_weights, shrink_weights, project_out)
    last, first, packed = lax.optimization_barrier(
        (grid_state[-rim:], grid_state[:rim], packed)
    )
    low = shifted(last, 1)
    high = shifted(first, -1)
    swapped, north, south = OVER(packed), NORTH(packed), SOUTH(packed)
    swapped_north, swapped_south = NORTH(swapped), SOUTH(swapped)
    far, swapped_far = NORTH(north), SOUTH(swapped_south)
    inward = [project_in[:, j, :].reshape(8, BLOCK, BLOCK) for j in range(3)]
    low, high, *inward = lax.optimization_barrier((low, high, *inward))
    mesh_start = encode(
        encode_index - (band * grid_blocks - mesh_blocks), low, grid_state, high, encode_weights
    )
    half = mesh_rows // 2
    mine = jnp.stack(
        [
            jnp.stack(pair)
            for pair in (
                (packed, swapped),
                (north, swapped_north),
                (south, swapped_south),
                (far, swapped_far),
            )
        ]
    )
    x, _, _ = lax.optimization_barrier((mesh_start, swapped_north, swapped_south))
    up, down = UP(mine), DOWN(mine)
    y, xa, xb, mine = lax.optimization_barrier((OVER(x), NORTH(x), SOUTH(x), mine))
    across = ACROSS(mine)
    from_south = NORTH(jnp.concatenate([xa[:half], y]))
    from_north = SOUTH(jnp.concatenate([xb[half:], y]))
    xc = jnp.concatenate([from_south[:half], from_north[:half]])
    slots = (x, y, xa, from_south, xb, from_north, xc, OVER(xc))
    partner = me ^ 1
    order = jnp.stack(
        [me, partner] + [(v + by) % 8 for by in (6, 2, 4) for v in (me, partner)]
    ).astype(jnp.int32)
    queries, keys_values, share, lower, upper = project(order, slots, first_gain, inward)
    upper, lower, up, down = lax.optimization_barrier(
        (upper, lower, up, down)
    )
    below = shifted(upper, 1)
    above = shifted(lower, -1)
    edges = jnp.stack([band == 0, band == bands - 1]).astype(jnp.int32)
    context = attend(edges, queries, below, keys_values, above)
    context, *here = lax.optimization_barrier((context, mine, up, down, across))
    parts = here + [TWIN(v) for v in here]
    context = lax.all_to_all(
        context.reshape(8, mesh_rows // 8, BLOCK), "head", 0, 0, tiled=True
    )
    places = [
        ((place + by) % 4) * 2 + side for side in (core, 1 - core) for by in (0, 3, 1, 2)
    ]
    table = jnp.concatenate([order, jnp.stack(places).astype(jnp.int32)])
    mesh_end = forward(table, parts, context, share, second_gain)
    mesh_end = lax.all_to_all(mesh_end, "head", 0, 0, tiled=True)
    mesh_end = mesh_end.reshape(mesh_blocks, BLOCK, BLOCK)
    edge = mesh_blocks // 2
    back, sums = decode(
        decode_index - (band * mesh_blocks - edge),
        shifted(mesh_end[-edge:], 1),
        mesh_end,
        shifted(mesh_end[:edge], -1),
        decode_weights,
    )
    sums = lax.all_to_all(
        jnp.broadcast_to(sums, (8, *sums.shape)), "head", 0, 0, tiled=True
    )
    return finish(sums, back, grid_state, output_gain)


def solution(mesh):
    in_specs = (
        P("seq", "head"),
        P("seq", None),
        P("seq", None, None, None),
        P(),
        P(None, None, "head"),
        P("head", None),
        P(),
        P(None, "head"),
        P("head", None),
        P("seq", None),
        P("seq", None, None, None),
        P("head"),
    )
    return jax.shard_map(
        on_device, mesh=mesh, in_specs=in_specs, out_specs=P("seq", "head"), check_vma=False
    )
```
